32 devices in a mesh: dp: 8 (over y, x, core), tensor: 4 (over z).
Axes of the slice: x: 2, y: 2, z: 4, core: 2. Of those that a mesh axis runs over, the one named last changes fastest.
Arguments:
- inputs: bfloat16 [4096, 1024], P(('dp', 'tensor')), may hold values from -6 to 6
- cotangent: bfloat16 [4096, 1024], P(('dp', 'tensor')), may hold values from -6 to 6
- norm_attend: bfloat16 [1024], replicated, may hold values from 0.5 to 1.5
- norm_memory: bfloat16 [1024], replicated, may hold values from 0.5 to 1.5
- project_in: bfloat16 [1024, 3, 1024], P('dp', None, 'tensor'), may hold values from -0.1875 to 0.1875
- project_out: bfloat16 [1024, 1024], P('tensor', 'dp'), may hold values from -2 to 2
- query_weight: bfloat16 [1024, 2048], P('dp', 'tensor'), may hold values from -0.1875 to 0.1875
- gate_weight: bfloat16 [1024, 1024], P('dp', 'tensor'), may hold values from -0.1875 to 0.1875
- memory_out: bfloat16 [1024, 1024], P('tensor', 'dp'), may hold values from -0.5 to 0.5
- half_keys: bfloat16 [4, 2, 256, 256], P('tensor'), may hold values from -6 to 6
- value_table: bfloat16 [65536, 1024], P('dp', 'tensor'), may hold values from -6 to 6
- key_picks: int32 [4, 2, 32, 4096], P(None, None, None, 'dp'), may hold values from 0 to 255
- segment_ids: int32 [4096], P('dp'), may hold values from 0 to 2, as said below
- adapter_ids: int32 [8, 3], P('dp'), may hold values from 0 to 7
- down_input: bfloat16 [1024, 384], P('dp'), may hold values from -0.1875 to 0.1875
- up_input: bfloat16 [128, 3, 1024], P('dp', None, 'tensor'), may hold values from -1.5 to 1.5
- down_attend: bfloat16 [1024, 128], P('tensor', 'dp'), may hold values from -2 to 2
- up_attend: bfloat16 [128, 1024], P('dp'), may hold values from -1.5 to 1.5
- down_memory: bfloat16 [1024, 256], P('dp'), may hold values from -0.1875 to 0.1875
- up_query: bfloat16 [128, 2048], P('dp', 'tensor'), may hold values from -1.5 to 1.5
- up_gate: bfloat16 [128, 1024], P('dp', 'tensor'), may hold values from -1.5 to 1.5
- down_mixed: bfloat16 [1024, 128], P('tensor', 'dp'), may hold values from -0.5 to 0.5
- up_mixed: bfloat16 [128, 1024], P('dp'), may hold values from -1.5 to 1.5
Outputs:
- outputs: bfloat16 [4096, 1024], P(('dp', 'tensor'))
- input_grad: float32 [4096, 1024], P(('dp', 'tensor'))
- grad_down_input: float32 [1024, 384], P('dp', 'tensor')
- grad_up_input: float32 [128, 3, 1024], P('dp', None, 'tensor')
- grad_down_attend: float32 [1024, 128], P('tensor', 'dp')
- grad_up_attend: float32 [128, 1024], P('dp', 'tensor')
- grad_down_memory: float32 [1024, 256], P('dp', 'tensor')
- grad_up_query: float32 [128, 2048], P('dp', 'tensor')
- grad_up_gate: float32 [128, 1024], P('dp', 'tensor')
- grad_down_mixed: float32 [1024, 128], P('tensor', 'dp')
- grad_up_mixed: float32 [128, 1024], P('dp', 'tensor')
The draws below stay inside these ranges and needn't reach their ends.
Inputs may be any that keep to these rules, and one draw needn't show every extreme that they name: `segment_ids`: in each group the prompt (0) comes first with 256 to 384 tokens, then continuation 1, then continuation 2, each continuation holding a quarter or more of the rest.
All inputs are finite; a program needn't handle non-finite values.
Results may differ from the reference program's by a relative error of at most 0.03.
Values may be sent and summed in bfloat16 or wider, within the bound.
A program may use at most 192 MiB of HBM per device.

```python
import jax
import jax.numpy as jnp
from jax import lax

D = 1024
HEADS = 16
HD = 64
MHEADS = 4
MQ = 512
HALF = 256
NKEYS = 256
ROWS = 65536
PICKS = 32
RANK = 16
NAD = 8
SEQS = 3
GTOK = 512
GROUPS = 8
TOKENS = 4096


def draw_segment_ids(key, part):
    groups = TOKENS // GTOK
    prompt_key = jax.random.fold_in(key, 11)
    split_key = jax.random.fold_in(key, 12)
    prompt = jax.random.randint(prompt_key, (groups, 1), GTOK // 2, 3 * GTOK // 4 + 1)
    remain = GTOK - prompt
    first = remain // 4 + jax.random.randint(split_key, (groups, 1), 0, remain // 2 + 1)
    places = jnp.arange(GTOK)[None, :]
    labels = (places >= prompt).astype(jnp.int32) + (places >= prompt + first).astype(jnp.int32)
    return labels.reshape(TOKENS)


def with_ends(array, stream_key, smallest, top_value):
    index_at = [jax.random.randint(jax.random.fold_in(stream_key, axis), (), 0, length) for axis, length in enumerate(array.shape)]
    widest = array.shape.index(max(array.shape))
    neighbour = index_at[:widest] + [(index_at[widest] + 1) % array.shape[widest]] + index_at[widest + 1:]
    return array.at[tuple(index_at)].set(smallest).at[tuple(neighbour)].set(top_value)


def levels(own_key, extent, shards, low, top_value):
    loudness, own = 1.0, jax.random.fold_in(own_key, 6)
    for axis_at, shards_of in shards:
        steps = jnp.exp(jax.random.uniform(jax.random.fold_in(own, axis_at), (shards_of,), jnp.float32, low / len(shards), top_value / len(shards)))
        loudness = loudness * jnp.repeat(steps, extent[axis_at] // shards_of).reshape([-1 if axis == axis_at else 1 for axis in range(len(extent))])
    return loudness


def centred(own_key, extent, spread, reach, shards=(), dtype=jnp.bfloat16):
    entries = spread * jax.random.normal(own_key, extent, jnp.float32)
    if shards:
        entries = entries * levels(own_key, extent, shards, -0.22, 0.18)
    return jnp.clip(entries, -reach, reach).astype(dtype)


def setup_inputs(seed: int = 0) -> dict:
    arg_keys = jax.random.split(jax.random.key(seed), 24)
    inputs = centred(arg_keys[0], (TOKENS, D), 1.0, 6.0, ((0, 32),))
    cotangent = centred(arg_keys[1], (TOKENS, D), 1.0, 6.0, ((0, 32),))
    norm_attend = jnp.clip(1.0 + 0.1 * jax.random.normal(arg_keys[2], (D,), jnp.float32), 0.5, 1.5).astype(jnp.bfloat16)
    norm_memory = jnp.clip(1.0 + 0.1 * jax.random.normal(arg_keys[3], (D,), jnp.float32), 0.5, 1.5).astype(jnp.bfloat16)
    project_in = centred(arg_keys[4], (D, 3, D), D ** -0.5, 0.1875, ((0, 8), (2, 4)))
    project_out = centred(arg_keys[5], (D, D), (max(D // 128, 4)) ** -0.5, 2.0, ((0, 4), (1, 8)))
    query_weight = centred(arg_keys[6], (D, MHEADS * MQ), D ** -0.5, 0.1875, ((0, 8), (1, 4)))
    gate_weight = centred(arg_keys[7], (D, D), D ** -0.5, 0.1875, ((0, 8), (1, 4)))
    memory_out = centred(arg_keys[8], (D, D), (max(D // 8, 4)) ** -0.5, 0.5, ((0, 4), (1, 8)))
    half_keys = centred(arg_keys[9], (MHEADS, 2, NKEYS, HALF), 1.0, 6.0, ((0, 4),))
    value_table = centred(arg_keys[10], (ROWS, D), 1.0, 6.0, ((0, 8), (1, 4)))
    key_picks = with_ends(jax.random.randint(arg_keys[11], (MHEADS, 2, PICKS, TOKENS), 0, NKEYS), jax.random.fold_in(arg_keys[11], 1), 0, NKEYS - 1).astype(jnp.int32)
    segment_ids = draw_segment_ids(jax.random.fold_in(arg_keys[23], 71), 0)
    adapter_ids = with_ends(jax.random.randint(arg_keys[13], (GROUPS, SEQS), 0, NAD), jax.random.fold_in(arg_keys[13], 1), 0, NAD - 1).astype(jnp.int32)
    down_input = centred(arg_keys[14], (D, NAD * 3 * RANK), D ** -0.5, 0.1875, ((0, 8),))
    up_input = centred(arg_keys[15], (NAD * RANK, 3, D), RANK ** -0.5, 1.5, ((0, 8), (2, 4)))
    down_attend = centred(arg_keys[16], (D, NAD * RANK), (max(D // 128, 4)) ** -0.5, 2.0, ((0, 4), (1, 8)))
    up_attend = centred(arg_keys[17], (NAD * RANK, D), RANK ** -0.5, 1.5, ((0, 8),))
    down_memory = centred(arg_keys[18], (D, NAD * 2 * RANK), D ** -0.5, 0.1875, ((0, 8),))
    up_query = centred(arg_keys[19], (NAD * RANK, MHEADS * MQ), RANK ** -0.5, 1.5, ((0, 8), (1, 4)))
    up_gate = centred(arg_keys[20], (NAD * RANK, D), RANK ** -0.5, 1.5, ((0, 8), (1, 4)))
    down_mixed = centred(arg_keys[21], (D, NAD * RANK), (max(D // 8, 4)) ** -0.5, 0.5, ((0, 4), (1, 8)))
    up_mixed = centred(arg_keys[22], (NAD * RANK, D), RANK ** -0.5, 1.5, ((0, 8),))
    return dict(inputs=inputs, cotangent=cotangent, norm_attend=norm_attend, norm_memory=norm_memory, project_in=project_in, project_out=project_out, query_weight=query_weight, gate_weight=gate_weight, memory_out=memory_out, half_keys=half_keys, value_table=value_table, key_picks=key_picks, segment_ids=segment_ids, adapter_ids=adapter_ids, down_input=down_input, up_input=up_input, down_attend=down_attend, up_attend=up_attend, down_memory=down_memory, up_query=up_query, up_gate=up_gate, down_mixed=down_mixed, up_mixed=up_mixed)


HIGHEST = lax.Precision.HIGHEST
EPS = 1e-06

@jax.custom_vjp
def low(v):
    return lax.optimization_barrier(v.astype(jnp.bfloat16)).astype(jnp.float32)

@jax.custom_vjp
def low_back(v):
    return v

def low_keep(v):
    return (low(v), None)

def low_pass(kept, grad):
    return (grad,)

def back_keep(v):
    return (v, None)

def back_low(kept, grad):
    return (low(grad),)
low.defvjp(low_keep, low_pass)
low_back.defvjp(back_keep, back_low)

def matmul(left, right):
    return jnp.dot(left, right, precision=HIGHEST)

def rms_norm(values, gain):
    return values * lax.rsqrt(lax.optimization_barrier(jnp.mean(values * values, axis=-1, keepdims=True)) + EPS) * gain

def adapter_in(hidden, chosen, member):
    ranks = jnp.einsum('nd,dsk->nsk', hidden, chosen, precision=HIGHEST) * member[:, :, None]
    return low(low_back(ranks))

def layer(inputs, adapters, frozen, segments, chosen_ids, picks):
    down_input, up_input, down_attend, up_attend, down_memory, up_query, up_gate, down_mixed, up_mixed = adapters
    norm_attend, norm_memory, project_in, project_out, query_weight, gate_weight, memory_out, half_keys, value_table = frozen
    count = inputs.shape[0]
    member = (segments[:, None] == jnp.arange(SEQS)[None, :]).astype(jnp.float32)
    normed_one = low(rms_norm(inputs, norm_attend))
    low_one = adapter_in(normed_one, down_input.reshape(D, NAD, 3 * RANK)[:, chosen_ids], member)
    up_one = up_input.reshape(NAD, RANK, 3, D)[chosen_ids]
    projected = jnp.einsum('nd,dpe->npe', normed_one, project_in, precision=HIGHEST)
    projected = projected + jnp.einsum('nspr,srpe->npe', low_one.reshape(count, SEQS, 3, RANK), up_one, precision=HIGHEST)
    projected = low(low_back(projected))
    heads = projected.reshape(count, 3, HEADS, HD).transpose(2, 1, 0, 3)
    places = jnp.arange(count)
    visible = (places[None, :] <= places[:, None]) & ((segments[None, :] == 0) | (segments[None, :] == segments[:, None]))

    def one_head(block):
        scores = low_back(matmul(block[0], block[1].T) * HD ** (-0.5))
        scores = jnp.where(visible, scores, -1e+30)
        probs = jax.nn.softmax(scores, axis=-1)
        return matmul(low(probs), block[2])
    attended = lax.map(jax.checkpoint(one_head), heads)
    attended = low(low_back(attended.transpose(1, 0, 2).reshape(count, D)))
    low_two = adapter_in(attended, down_attend.reshape(D, NAD, RANK)[:, chosen_ids], member)
    branch = matmul(attended, project_out) + jnp.einsum('nsr,sre->ne', low_two, up_attend.reshape(NAD, RANK, D)[chosen_ids], precision=HIGHEST)
    middle = inputs + low_back(branch)
    normed_two = low(rms_norm(middle, norm_memory))
    low_three = adapter_in(normed_two, down_memory.reshape(D, NAD, 2 * RANK)[:, chosen_ids], member).reshape(count, SEQS, 2, RANK)
    memory_query = matmul(normed_two, query_weight) + jnp.einsum('nsr,sre->ne', low_three[:, :, 0], up_query.reshape(NAD, RANK, MHEADS * MQ)[chosen_ids], precision=HIGHEST)
    memory_query = low_back(memory_query)
    gate_pre = matmul(normed_two, gate_weight) + jnp.einsum('nsr,sre->ne', low_three[:, :, 1], up_gate.reshape(NAD, RANK, D)[chosen_ids], precision=HIGHEST)
    gate_pre = low_back(gate_pre)
    split_query = memory_query.reshape(count, MHEADS, 2, MQ // 2).transpose(1, 2, 0, 3)

    def one_memory(block):
        query_half, keys_half, picked = block
        first = jnp.take_along_axis(matmul(query_half[0], keys_half[0].T), picked[0].T, axis=1)
        second = jnp.take_along_axis(matmul(query_half[1], keys_half[1].T), picked[1].T, axis=1)
        weights = jax.nn.softmax((first + second) * MQ ** (-0.5), axis=-1)
        rows = picked[0].T * NKEYS + picked[1].T
        return jnp.einsum('nj,njc->nc', low(weights), value_table[rows], precision=HIGHEST)
    recalled = low_back(lax.optimization_barrier(jnp.sum(lax.map(jax.checkpoint(one_memory), (split_query, half_keys, picks)), axis=0)))
    mixed = low(jax.nn.silu(gate_pre) * recalled)
    low_four = adapter_in(mixed, down_mixed.reshape(D, NAD, RANK)[:, chosen_ids], member)
    memory_branch = matmul(mixed, memory_out) + jnp.einsum('nsr,sre->ne', low_four, up_mixed.reshape(NAD, RANK, D)[chosen_ids], precision=HIGHEST)
    return middle + low_back(memory_branch)

def reference(inputs, cotangent, norm_attend, norm_memory, project_in, project_out, query_weight, gate_weight, memory_out, half_keys, value_table, key_picks, segment_ids, adapter_ids, down_input, up_input, down_attend, up_attend, down_memory, up_query, up_gate, down_mixed, up_mixed):
    frozen = tuple((item.astype(jnp.float32) for item in (norm_attend, norm_memory, project_in, project_out, query_weight, gate_weight, memory_out, half_keys, value_table)))
    adapters = tuple((item.astype(jnp.float32) for item in (down_input, up_input, down_attend, up_attend, down_memory, up_query, up_gate, down_mixed, up_mixed)))
    groups = TOKENS // GTOK
    group_inputs = inputs.astype(jnp.float32).reshape(groups, GTOK, D)
    group_cot = cotangent.astype(jnp.float32).reshape(groups, GTOK, D)
    group_segments = segment_ids.reshape(groups, GTOK)
    group_picks = key_picks.reshape(MHEADS, 2, PICKS, groups, GTOK).transpose(3, 0, 1, 2, 4)

    def step(totals, items):
        block_inputs, block_cot, block_segments, block_ids, block_picks = items

        def run(values, *weights):
            return layer(values, weights, frozen, block_segments, block_ids, block_picks)
        result, pull = jax.vjp(run, block_inputs, *adapters)
        grads = pull(block_cot)
        totals = tuple((total + grad for total, grad in zip(totals, grads[1:])))
        return (totals, (result.astype(jnp.bfloat16), grads[0]))
    zeros = tuple((jnp.zeros_like(item) for item in adapters))
    totals, (results, input_grads) = lax.scan(step, zeros, (group_inputs, group_cot, group_segments, adapter_ids, group_picks))
    return (results.reshape(TOKENS, D), input_grads.reshape(TOKENS, D), totals[0], totals[1], totals[2], totals[3], totals[4], totals[5], totals[6], totals[7], totals[8])
```

```python
import functools

import jax
import jax.numpy as jnp
from jax import lax
from jax.experimental import pallas as pl
from jax.experimental.pallas import tpu as pltpu
from jax.sharding import PartitionSpec as P

DP, TP = "dp", "tensor"
HD = 64
NKEYS = 256
RANK = 16
NAD = 8
EPS = 1e-06
NEGATIVE = -1e30
F32, BF16, I32 = jnp.float32, jnp.bfloat16, jnp.int32
MESH = pl.DeviceIdType.MESH
ANY = pl.BlockSpec(memory_space=pl.ANY)


def mm(a, b):
    return lax.dot_general(a, b, (((1,), (0,)), ((), ())), preferred_element_type=F32)


def mt(a, b):
    return lax.dot_general(a, b, (((1,), (1,)), ((), ())), preferred_element_type=F32)


def tm(a, b):
    return lax.dot_general(a, b, (((0,), (0,)), ((), ())), preferred_element_type=F32)


def two_parts(x):
    top = x.astype(BF16)
    return top, (x - top.astype(F32)).astype(BF16)


SHARE, PIECE, TREE = 0, 1, 2


def exchange(items, cid):
    arrays = [item[0] for item in items]
    kinds = [item[1] for item in items]
    axes = [item[2] for item in items]
    n = len(items)
    used = [axis for axis in (DP, TP) if axis in axes]
    sizes = {axis: lax.axis_size(axis) for axis in used}
    most = max(sizes.values())
    trees = [a for a in range(n) if kinds[a] == TREE]

    def body(*refs):
        ins, outs = refs[:n], refs[n : 2 * n]
        send, recv, pass_send, pass_recv, local = refs[2 * n :]
        me = {axis: lax.axis_index(axis) for axis in used}
        barrier = pltpu.get_barrier_semaphore()
        for axis in used:

            @pl.loop(1, sizes[axis])
            def _(d):
                pl.semaphore_signal(
                    barrier,
                    inc=1,
                    device_id={axis: lax.rem(me[axis] + d, sizes[axis])},
                    device_id_type=MESH,
                )

        def source(a, p):
            return ins[a].at[p] if kinds[a] == PIECE else ins[a]

        own = [
            pltpu.make_async_copy(source(a, me[axes[a]]), outs[a].at[me[axes[a]]], local.at[a])
            for a in range(n)
        ]
        for c in own:
            c.start()
        pl.semaphore_wait(barrier, sum(sizes.values()) - len(used))

        def copy(a, d):
            axis = axes[a]
            peer = lax.rem(me[axis] + d, sizes[axis])
            return pltpu.make_async_remote_copy(
                src_ref=source(a, peer),
                dst_ref=outs[a].at[me[axis]],
                send_sem=send.at[a, d],
                recv_sem=recv.at[a, d],
                device_id={axis: peer},
                device_id_type=MESH,
            )

        def tree_copy(a, d):
            peer = lax.rem(me[DP] + 2 * d, sizes[DP])
            return pltpu.make_async_remote_copy(
                src_ref=ins[a],
                dst_ref=outs[a].at[me[DP]],
                send_sem=send.at[a, d],
                recv_sem=recv.at[a, d],
                device_id={DP: peer},
                device_id_type=MESH,
            )

        def pass_on(a, d):
            holder = lax.rem(me[DP] - 2 * d + sizes[DP], sizes[DP])
            sibling = me[DP] + 1 - 2 * lax.rem(me[DP], 2)
            return pltpu.make_async_remote_copy(
                src_ref=ins[a] if isinstance(d, int) else outs[a].at[holder],
                dst_ref=outs[a].at[holder],
                send_sem=pass_send.at[a, d],
                recv_sem=pass_recv.at[a, d],
                device_id={DP: sibling},
                device_id_type=MESH,
            )

        if trees:

            @pl.loop(1, sizes[DP] // 2)
            def _(d):
                for a in trees:
                    tree_copy(a, d).start()

            for a in trees:
                pass_on(a, 0).start()
        for axis in used:
            mine = [a for a in range(n) if axes[a] == axis and kinds[a] != TREE]
            if mine:

                @pl.loop(1, sizes[axis])
                def _(d):
                    for a in mine:
                        copy(a, d).start()

        if trees:

            @pl.loop(1, sizes[DP] // 2)
            def _(d):
                for a in trees:
                    tree_copy(a, d).wait_recv()
                    pass_on(a, d).start()

            @pl.loop(1, sizes[DP] // 2)
            def _(d):
                for a in trees:
                    tree_copy(a, d).wait_send()
                    pass_on(a, d).wait()

            for a in trees:
                pass_on(a, 0).wait()
        for axis in used:
            mine = [a for a in range(n) if axes[a] == axis and kinds[a] != TREE]
            if mine:

                @pl.loop(1, sizes[axis])
                def _(d):
                    for a in mine:
                        copy(a, d).wait()

        for c in own:
            c.wait()

    shapes = [
        jax.ShapeDtypeStruct(
            (sizes[axes[a]],) + (x.shape[1:] if kinds[a] == PIECE else x.shape), x.dtype
        )
        for a, x in enumerate(arrays)
    ]
    sems = pltpu.SemaphoreType.DMA((n, most))
    return pl.pallas_call(
        body,
        out_shape=shapes,
        in_specs=[ANY] * n,
        out_specs=[ANY] * n,
        scratch_shapes=[sems, sems, sems, sems, pltpu.SemaphoreType.DMA((n,))],
        compiler_params=pltpu.CompilerParams(collective_id=cid, has_side_effects=True),
    )(*arrays)


def rms_forward(values, gain):
    factor = lax.rsqrt(jnp.mean(values * values, axis=-1, keepdims=True) + EPS)
    return values * factor * gain


def rms_backward(values, gain, upstream):
    factor = lax.rsqrt(jnp.mean(values * values, axis=-1, keepdims=True) + EPS)
    scaled = upstream * gain
    return factor * scaled - values * (factor * factor * factor) * jnp.mean(
        values * scaled, axis=-1, keepdims=True
    )


def block_probs(projected, key_segments, query_segments, h, r, block, width, scale):
    top = (r + 1) * block
    at = slice(r * block, top)
    lanes = slice(h * HD, (h + 1) * HD)
    queries = projected[at, lanes]
    keys = projected[:top, width + h * HD : width + (h + 1) * HD]
    values = projected[:top, 2 * width + h * HD : 2 * width + (h + 1) * HD]
    scores = mt(queries, keys) * scale
    place = lax.broadcasted_iota(I32, (block, top), 0) + r * block
    other = lax.broadcasted_iota(I32, (block, top), 1)
    ahead = key_segments[:, :top]
    seen = (other <= place) & ((ahead == 0) | (ahead == query_segments[at, :]))
    scores = jnp.where(seen, scores, NEGATIVE)
    raised = jnp.exp(scores - jnp.max(scores, axis=-1, keepdims=True))
    probs = raised / jnp.sum(raised, axis=-1, keepdims=True)
    return queries, keys, values, probs


def attention_forward(projected, segments, width, block=128):
    count = projected.shape[0]

    def body(projected_ref, across_ref, down_ref, out_ref):
        for h in range(width // HD):
            for r in range(count // block):
                _, _, values, probs = block_probs(
                    projected_ref, across_ref, down_ref, h, r, block, width, HD**-0.5
                )
                out_ref[r * block : (r + 1) * block, h * HD : (h + 1) * HD] = mm(
                    probs.astype(BF16), values
                ).astype(BF16)

    return pl.pallas_call(
        body,
        out_shape=jax.ShapeDtypeStruct((count, width), BF16),
        compiler_params=pltpu.CompilerParams(vmem_limit_bytes=32 << 20),
    )(projected, segments[None, :], segments[:, None])


def attention_backward(projected, segments, upstream, width, block=128):
    count = projected.shape[0]
    scale = HD**-0.5

    def body(projected_ref, across_ref, down_ref, upstream_ref, out_ref, key_sum, value_sum):
        for h in range(width // HD):
            key_sum[...] = jnp.zeros_like(key_sum)
            value_sum[...] = jnp.zeros_like(value_sum)
            lanes = slice(h * HD, (h + 1) * HD)
            for r in range(count // block):
                at, top = slice(r * block, (r + 1) * block), (r + 1) * block
                queries, keys, values, probs = block_probs(
                    projected_ref, across_ref, down_ref, h, r, block, width, scale
                )
                above = upstream_ref[at, lanes]
                grad_probs = mt(above, values)
                inner = jnp.sum(probs * grad_probs, axis=-1, keepdims=True)
                grad_scores = (probs * (grad_probs - inner)).astype(BF16)
                out_ref[at, lanes] = (mm(grad_scores, keys) * scale).astype(BF16)
                key_sum[:top, :] += tm(grad_scores, queries)
                value_sum[:top, :] += tm(probs.astype(BF16), above)
            out_ref[:, width + h * HD : width + (h + 1) * HD] = (key_sum[...] * scale).astype(BF16)
            out_ref[:, 2 * width + h * HD : 2 * width + (h + 1) * HD] = value_sum[...].astype(BF16)

    return pl.pallas_call(
        body,
        out_shape=jax.ShapeDtypeStruct((count, 3 * width), BF16),
        scratch_shapes=[pltpu.VMEM((count, HD), F32), pltpu.VMEM((count, HD), F32)],
        compiler_params=pltpu.CompilerParams(vmem_limit_bytes=32 << 20),
    )(projected, segments[None, :], segments[:, None], upstream)


def pick_weights(query, keys, picks):
    count, half = query.shape[0], keys.shape[2]
    number = picks.shape[1]
    chunk = 128
    scale = (2 * half) ** -0.5

    def body(query_ref, keys_ref, picks_ref, out_ref, every):
        for part in range(2):
            top, rest = two_parts(query_ref[:, part * half : (part + 1) * half])
            every[...] = mt(keys_ref[part], top) + mt(keys_ref[part], rest)
            slot = lax.broadcasted_iota(I32, (NKEYS, chunk), 0)
            for c in range(count // chunk):
                lanes = slice(c * chunk, (c + 1) * chunk)
                scores = every[:, lanes]
                rows = []
                for k in range(number):
                    hit = slot == picks_ref[part, k : k + 1, lanes]
                    rows.append(jnp.sum(jnp.where(hit, scores, 0.0), axis=0, keepdims=True))
                found = jnp.concatenate(rows, axis=0)
                if part == 0:
                    out_ref[:, lanes] = found
                else:
                    total = (out_ref[:, lanes] + found) * scale
                    raised = jnp.exp(total - jnp.max(total, axis=0, keepdims=True))
                    out_ref[:, lanes] = raised / jnp.sum(raised, axis=0, keepdims=True)

    return pl.pallas_call(
        body,
        out_shape=jax.ShapeDtypeStruct((number, count), F32),
        scratch_shapes=[pltpu.VMEM((NKEYS, count), F32)],
        compiler_params=pltpu.CompilerParams(vmem_limit_bytes=32 << 20),
    )(query, keys, picks)


def query_grads(weights, pieces, keys, picks):
    number, count = weights.shape
    half = keys.shape[2]
    chunk = 128
    scale = (2 * half) ** -0.5

    def body(weights_ref, pieces_ref, keys_ref, picks_ref, out_ref, dense):
        slot = lax.broadcasted_iota(I32, (NKEYS, chunk), 0)
        for part in range(2):
            for c in range(count // chunk):
                lanes = slice(c * chunk, (c + 1) * chunk)
                weight = weights_ref[:, lanes]
                grad = sum(pieces_ref[p, :, lanes].astype(F32) for p in range(pieces.shape[0]))
                grad = weight * (grad - jnp.sum(grad * weight, axis=0, keepdims=True)) * scale
                total = jnp.zeros((NKEYS, chunk), F32)
                for k in range(number):
                    hit = slot == picks_ref[part, k : k + 1, lanes]
                    total += jnp.where(hit, grad[k : k + 1, :], 0.0)
                dense[:, lanes] = total
            top, rest = two_parts(dense[...])
            out_ref[:, part * half : (part + 1) * half] = (
                tm(top, keys_ref[part]) + tm(rest, keys_ref[part])
            ).astype(BF16)

    return pl.pallas_call(
        body,
        out_shape=jax.ShapeDtypeStruct((count, 2 * half), BF16),
        scratch_shapes=[pltpu.VMEM((NKEYS, count), F32)],
        compiler_params=pltpu.CompilerParams(vmem_limit_bytes=32 << 20),
    )(weights, pieces, keys, picks)


def spread_picks(first, second, weights, sub=32, conv=32):
    tokens, picks = first.shape
    stride = sub + 1

    def body(first_ref, second_ref, weights_ref, out_ref, low, high):
        slot = lax.broadcasted_iota(I32, (NKEYS, picks), 0)
        for n in range(sub):
            b = jnp.where(slot == second_ref[n : n + 1, :], 1.0, 0.0).astype(BF16)
            a = jnp.where(slot == first_ref[n : n + 1, :], weights_ref[n : n + 1, :], 0.0)
            both = mt(a.astype(BF16), b)
            low[pl.ds(n, NKEYS, stride=stride), :] = both[:, :128]
            high[pl.ds(n, NKEYS, stride=stride), :] = both[:, 128:]

        @pl.loop(0, NKEYS // conv)
        def _(c):
            for q in range(conv):
                i = c * conv + q
                at = pl.multiple_of(i * NKEYS, NKEYS)
                rows = pl.ds(i * stride, sub)
                out_ref[:, pl.ds(at, 128)] = low[rows, :].astype(BF16)
                out_ref[:, pl.ds(at + 128, 128)] = high[rows, :].astype(BF16)

    line = pl.BlockSpec((sub, picks), lambda t: (t, 0))
    rows = NKEYS * NKEYS
    return pl.pallas_call(
        body,
        grid=(tokens // sub,),
        out_shape=jax.ShapeDtypeStruct((tokens, rows), BF16),
        in_specs=[line] * 3,
        out_specs=pl.BlockSpec((sub, rows), lambda t: (t, 0)),
        scratch_shapes=[pltpu.VMEM((NKEYS * stride, 128), F32)] * 2,
        compiler_params=pltpu.CompilerParams(vmem_limit_bytes=40 << 20),
    )(first, second, weights)


def recall(dense, table, block=4096):
    tokens, rows = dense.shape
    width = table.shape[1]

    def body(dense_ref, table_ref, out_ref):
        @pl.when(pl.program_id(0) == 0)
        def _():
            out_ref[...] = jnp.zeros_like(out_ref)

        out_ref[...] += mm(dense_ref[...], table_ref[...])

    return pl.pallas_call(
        body,
        grid=(rows // block,),
        out_shape=jax.ShapeDtypeStruct((tokens, width), F32),
        in_specs=[
            pl.BlockSpec((tokens, block), lambda s: (0, s)),
            pl.BlockSpec((block, width), lambda s: (s, 0)),
        ],
        out_specs=pl.BlockSpec((tokens, width), lambda s: (0, 0)),
        compiler_params=pltpu.CompilerParams(vmem_limit_bytes=40 << 20),
    )(dense, table)


def pick_grads(first, second, grads, scale, table, per_block=16):
    tokens, picks = first.shape
    width = grads.shape[1]
    rows = per_block * NKEYS
    blocks = table.shape[0] // rows

    def body(first_ref, second_ref, grads_ref, scale_ref, table_ref, out_ref, kept):
        step = pl.program_id(0)

        @pl.when(step == 0)
        def _():
            kept[...] = jnp.zeros_like(kept)

        own = first_ref[...]
        low = second_ref[...] & 127
        factor = jnp.broadcast_to(scale_ref[...], (tokens, 128))
        total = kept[...]
        for b in range(per_block):
            every = mt(grads_ref[...], table_ref[b * NKEYS : (b + 1) * NKEYS, :])
            packed = (every[:, 128:] * factor).astype(I32) * 65536 + (
                every[:, :128] * factor
            ).astype(I32)
            found = jnp.take_along_axis(packed, low, axis=1, mode="promise_in_bounds")
            total = jnp.where(own == step * per_block + b, found, total)
        kept[...] = total

        @pl.when(step == blocks - 1)
        def _():
            p = kept[...]
            right = lax.shift_right_arithmetic(lax.shift_left(p, 16), 16)
            left = lax.shift_right_arithmetic(p - right, 16)
            both = jnp.where(second_ref[...] >= 128, left, right).astype(F32) / factor
            out_ref[...] = both.T.astype(BF16)

    whole = lambda shape: pl.BlockSpec(shape, lambda s: (0, 0))
    return pl.pallas_call(
        body,
        grid=(blocks,),
        out_shape=jax.ShapeDtypeStruct((picks, tokens), BF16),
        in_specs=[
            whole((tokens, picks)),
            whole((tokens, picks)),
            whole((tokens, width)),
            whole((tokens, 1)),
            pl.BlockSpec((rows, width), lambda s: (s, 0)),
        ],
        out_specs=whole((picks, tokens)),
        scratch_shapes=[pltpu.VMEM((tokens, picks), I32)],
        compiler_params=pltpu.CompilerParams(vmem_limit_bytes=48 << 20),
    )(first, second, grads, scale, table)


def by_part(down, parts):
    shaped = down.reshape(down.shape[0], NAD, parts, RANK).transpose(0, 2, 1, 3)
    return shaped.reshape(down.shape)


def on_device(
    inputs,
    cotangent,
    norm_attend,
    norm_memory,
    project_in,
    project_out,
    query_weight,
    gate_weight,
    memory_out,
    half_keys,
    value_table,
    key_picks,
    segment_ids,
    adapter_ids,
    down_input,
    up_input,
    down_attend,
    up_attend,
    down_memory,
    up_query,
    up_gate,
    down_mixed,
    up_mixed,
):
    groups = lax.axis_size(DP)
    ranks = lax.axis_size(TP)
    rank = lax.axis_index(TP)
    local = inputs.shape[0]
    count = segment_ids.shape[0]
    width = project_in.shape[2]
    model = inputs.shape[1]
    space = NAD * RANK
    own_adapters = NAD // ranks

    table = lax.all_gather(value_table, DP, axis=0, tiled=True)
    small = jnp.concatenate(
        [
            up_input.reshape(up_input.shape[0], 3 * width),
            up_query,
            up_gate,
            up_attend,
            up_mixed,
            down_attend.T,
            down_mixed.T,
        ],
        axis=1,
    )
    flat_in = project_in.reshape(project_in.shape[0], 3 * width)
    shards = (flat_in, by_part(down_input, 3), small, project_out.T)
    late = (query_weight, gate_weight, by_part(down_memory, 2), memory_out.T)
    got = exchange([(inputs, SHARE, TP)] + [(x, TREE, DP) for x in shards + late], 1)
    input_rows = got[0].reshape(count, model)
    full_in, full_down_input, full_small, out_t, full_query, full_gate, full_down_memory, mixed_t = [
        x.reshape(-1, x.shape[2]) for x in got[1:]
    ]
    at, pieces = 0, []
    for size in (3 * width, up_query.shape[1], width, model, model, width, width):
        pieces.append(full_small[:, at : at + size])
        at += size
    full_up_input, full_up_query, full_up_gate, full_up_attend, full_up_mixed, attend_t, low_mixed_t = (
        pieces
    )

    owner = jnp.zeros((count,), I32)
    for s in range(adapter_ids.shape[1]):
        owner = jnp.where(segment_ids == s, adapter_ids[0, s], owner)
    column = jnp.arange(space)
    mask = (owner[:, None] == (column // RANK)[None, :]).astype(F32)
    mask_own = lax.dynamic_slice_in_dim(mask, rank * local, local, 0)
    mask_two = jnp.concatenate([mask, mask], axis=1)
    mask_three = jnp.concatenate([mask_two, mask], axis=1)

    first_picks = key_picks[:, 0].reshape(-1, count).T
    second_picks = key_picks[:, 1].reshape(-1, count).T
    own_picks = lax.dynamic_index_in_dim(key_picks, rank, 0, keepdims=False)

    gain_one = norm_attend.astype(F32)
    gain_two = norm_memory.astype(F32)
    normed_one = rms_forward(input_rows.astype(F32), gain_one).astype(BF16)
    low_one = (mm(normed_one, full_down_input) * mask_three).astype(BF16)
    projected = mm(normed_one, full_in) + jnp.concatenate(
        [
            mm(
                low_one[:, p * space : (p + 1) * space],
                full_up_input[:, p * width : (p + 1) * width],
            )
            for p in range(3)
        ],
        axis=1,
    )
    projected = projected.astype(BF16)
    attended = attention_forward(projected, segment_ids, width)
    partial_out = mt(attended, out_t).astype(BF16)
    partial_two = (mt(attended, attend_t) * mask).astype(BF16)
    out_pieces, two_pieces = exchange(
        [
            (partial_out.reshape(ranks, local, model), PIECE, TP),
            (partial_two.reshape(ranks, local, space), PIECE, TP),
        ],
        2,
    )
    low_two = two_pieces.astype(F32).sum(axis=0).astype(BF16)
    residual = inputs.astype(F32)
    middle = residual + out_pieces.astype(F32).sum(axis=0) + mm(low_two, full_up_attend)
    normed_two = rms_forward(middle, gain_two).astype(BF16)
    largest = jnp.max(jnp.sum(jnp.square(value_table.astype(F32)), axis=1))
    normed_rows, low_two_rows, cotangent_rows, norms = exchange(
        [
            (normed_two, SHARE, TP),
            (low_two, SHARE, TP),
            (cotangent, SHARE, TP),
            (jnp.broadcast_to(largest, (8, 128)), SHARE, DP),
        ],
        3,
    )
    normed_rows = normed_rows.reshape(count, model)
    low_two_rows = low_two_rows.reshape(count, space)
    cotangent_rows = cotangent_rows.reshape(count, model)

    low_three = (mm(normed_rows, full_down_memory) * mask_two).astype(BF16)
    memory_query = mm(normed_rows, full_query) + mm(low_three[:, :space], full_up_query)
    gate_pre = mm(normed_rows, full_gate) + mm(low_three[:, space:], full_up_gate)
    weights = pick_weights(memory_query, half_keys[0], own_picks)
    (all_weights,) = exchange([(weights.astype(BF16), SHARE, TP)], 4)
    by_token = all_weights.reshape(-1, count).astype(F32).T
    dense = spread_picks(first_picks, second_picks, by_token)

    grad_low_four = (mt(cotangent_rows, full_up_mixed) * mask).astype(BF16)
    grad_mixed = mm(cotangent_rows, mixed_t) + mm(grad_low_four, low_mixed_t)

    recalled = recall(dense, table)
    sigmoid = jax.nn.sigmoid(gate_pre)
    gate_act = gate_pre * sigmoid
    mixed = (gate_act * recalled).astype(BF16)
    grad_recalled = (grad_mixed * gate_act).astype(BF16)
    grad_gate = (grad_mixed * recalled * sigmoid * (1.0 + gate_pre * (1.0 - sigmoid))).astype(BF16)
    bound = jnp.max(norms) * jnp.sum(
        jnp.square(grad_recalled.astype(F32)), axis=1, keepdims=True
    )
    scale = 32000.0 * lax.rsqrt(jnp.maximum(bound, 1e-30))
    picked = pick_grads(first_picks, second_picks, grad_recalled, scale, table)
    (pick_pieces,) = exchange([(picked.reshape(ranks, -1, count), PIECE, TP)], 5)

    partial_mixed = mt(mixed, mixed_t).astype(BF16)
    partial_four = (mt(mixed, low_mixed_t) * mask).astype(BF16)
    grad_down_mixed = tm(grad_low_four, mixed)

    grad_query = query_grads(weights, pick_pieces, half_keys[0], own_picks)
    partial_normed = (mt(grad_query, full_query) + mt(grad_gate, full_gate)).astype(BF16)
    folds = [
        ((column[:, None] % RANK) == (column[None, :] - p * RANK)).astype(BF16) for p in range(3)
    ]
    three_query = (mt(grad_query, full_up_query) * mask).astype(BF16)
    three_gate = (mt(grad_gate, full_up_gate) * mask).astype(BF16)
    partial_three = (mm(three_query, folds[0]) + mm(three_gate, folds[1])).astype(BF16)
    grad_up_query = tm(low_three[:, :space], grad_query)
    grad_up_gate = tm(low_three[:, space:], grad_gate)
    normed_pieces, three_pieces, mixed_pieces, four_pieces = exchange(
        [
            (partial_normed.reshape(ranks, local, model), PIECE, TP),
            (partial_three.reshape(ranks, local, space), PIECE, TP),
            (partial_mixed.reshape(ranks, local, model), PIECE, TP),
            (partial_four.reshape(ranks, local, space), PIECE, TP),
        ],
        6,
    )
    low_four = four_pieces.astype(F32).sum(axis=0).astype(BF16)
    outputs = (
        middle + mixed_pieces.astype(F32).sum(axis=0) + mm(low_four, full_up_mixed)
    ).astype(BF16)
    grad_three = three_pieces.astype(F32).sum(axis=0).astype(BF16)
    grad_three_full = jnp.concatenate(
        [mt(grad_three, folds[p]) * mask_own for p in range(2)], axis=1
    ).astype(BF16)
    grad_normed_two = normed_pieces.astype(F32).sum(axis=0) + mt(grad_three_full, full_down_memory)
    grad_middle = cotangent.astype(F32) + rms_backward(middle, gain_two, grad_normed_two)
    grad_branch = grad_middle.astype(BF16)
    branch_rows, grad_three_rows, low_four_rows = exchange(
        [(grad_branch, SHARE, TP), (grad_three, SHARE, TP), (low_four, SHARE, TP)], 7
    )
    branch_rows = branch_rows.reshape(count, model)
    grad_three_rows = grad_three_rows.reshape(count, space)
    low_four_rows = low_four_rows.reshape(count, space)

    grad_low_two = (mt(branch_rows, full_up_attend) * mask).astype(BF16)
    grad_attended = (mm(branch_rows, out_t) + mm(grad_low_two, attend_t)).astype(BF16)
    grad_projected = attention_backward(projected, segment_ids, grad_attended, width)
    partial_input = mt(grad_projected, full_in).astype(BF16)
    partial_one = sum(
        mm(
            (
                mt(
                    grad_projected[:, p * width : (p + 1) * width],
                    full_up_input[:, p * width : (p + 1) * width],
                )
                * mask
            ).astype(BF16),
            folds[p],
        )
        for p in range(3)
    ).astype(BF16)
    input_pieces, one_partials = exchange(
        [(partial_input.reshape(ranks, local, model), PIECE, TP), (partial_one, SHARE, TP)], 8
    )
    grad_one_rows = one_partials.astype(F32).sum(axis=0).astype(BF16)
    grad_one = lax.dynamic_slice_in_dim(grad_one_rows, rank * local, local, 0)
    grad_one_full = jnp.concatenate(
        [mt(grad_one, folds[p]) * mask_own for p in range(3)], axis=1
    ).astype(BF16)
    grad_normed_one = input_pieces.astype(F32).sum(axis=0) + mt(grad_one_full, full_down_input)
    input_grad = grad_middle + rms_backward(residual, gain_one, grad_normed_one)

    def own_columns(compact, parts):
        columns = jnp.arange(own_adapters * parts * RANK)
        pattern = (column[:, None] == (columns % (parts * RANK))[None, :]).astype(BF16)
        mine = owner[:, None] == (rank * own_adapters + columns // (parts * RANK))[None, :]
        return jnp.where(mine, mm(compact, pattern), 0.0).astype(BF16)

    grad_down_input = tm(normed_one, own_columns(grad_one_rows, 3))
    grad_down_memory = tm(normed_rows, own_columns(grad_three_rows, 2))
    grad_up_input = jnp.concatenate(
        [
            tm(
                low_one[:, p * space : (p + 1) * space],
                grad_projected[:, p * width : (p + 1) * width],
            )
            for p in range(3)
        ],
        axis=1,
    )
    grad_down_attend = tm(grad_low_two, attended)
    own_branch = lax.dynamic_slice_in_dim(branch_rows, rank * width, width, 1)
    own_cotangent = lax.dynamic_slice_in_dim(cotangent_rows, rank * width, width, 1)
    grad_up_attend = tm(low_two_rows, own_branch)
    grad_up_mixed = tm(low_four_rows, own_cotangent)
    ups = jnp.concatenate(
        [
            grad_up_input,
            grad_up_query,
            grad_up_gate,
            grad_up_attend,
            grad_up_mixed,
            grad_down_attend,
            grad_down_mixed,
        ],
        axis=1,
    ).astype(BF16)
    downs = jnp.concatenate([grad_down_input, grad_down_memory], axis=1).astype(BF16)
    up_parts, down_parts = exchange(
        [
            (ups.reshape(groups, -1, ups.shape[1]), PIECE, DP),
            (downs.reshape(groups, -1, downs.shape[1]), PIECE, DP),
        ],
        9,
    )
    up_sums = up_parts.astype(F32).sum(axis=0)
    down_sums = down_parts.astype(F32).sum(axis=0)
    at, parts = 0, []
    for size in (3 * width, up_query.shape[1], width, width, width, width, width):
        parts.append(up_sums[:, at : at + size])
        at += size
    cut = own_adapters * 3 * RANK
    return (
        outputs,
        input_grad,
        down_sums[:, :cut],
        parts[0].reshape(up_input.shape),
        parts[5].T,
        parts[3],
        down_sums[:, cut:],
        parts[1],
        parts[2],
        parts[6].T,
        parts[4],
    )


def solution(mesh):
    rows = P((DP, TP), None)
    both = P(DP, TP)
    wide = P(DP, None)
    turned = P(TP, DP)
    split = P(DP, None, TP)
    return jax.shard_map(
        on_device,
        mesh=mesh,
        in_specs=(
            rows,
            rows,
            P(),
            P(),
            split,
            turned,
            both,
            both,
            turned,
            P(TP, None, None, None),
            both,
            P(None, None, None, DP),
            P(DP),
            wide,
            wide,
            split,
            turned,
            wide,
            wide,
            both,
            both,
            turned,
            wide,
        ),
        out_specs=(rows, rows, both, split, turned, both, both, both, both, turned, both),
        check_vma=False,
    )
```

```python
import functools

import jax
import jax.numpy as jnp
from jax import lax
from jax.experimental import pallas as pl
from jax.experimental.pallas import tpu as pltpu
from jax.sharding import PartitionSpec as P

DP, TP = "dp", "tensor"
HD = 64
PARTS = 1
NKEYS = 256
RANK = 16
NAD = 8
EPS = 1e-06
NEGATIVE = -1e30
F32, BF16, I32 = jnp.float32, jnp.bfloat16, jnp.int32
MESH = pl.DeviceIdType.MESH
ANY = pl.BlockSpec(memory_space=pl.ANY)


def mm(a, b):
    return lax.dot_general(a, b, (((1,), (0,)), ((), ())), preferred_element_type=F32)


def mt(a, b):
    return lax.dot_general(a, b, (((1,), (1,)), ((), ())), preferred_element_type=F32)


def tm(a, b):
    return lax.dot_general(a, b, (((0,), (0,)), ((), ())), preferred_element_type=F32)


def two_parts(x):
    top = x.astype(BF16)
    return top, (x - top.astype(F32)).astype(BF16)


SHARE, PIECE, SPLIT, SIDE, TREE, NEST = range(6)


def exchange(items, cid):
    arrays = [item[0] for item in items]
    kinds = [item[1] for item in items]
    axes = [item[2] for item in items]
    n = len(items)
    trees = [a for a in range(n) if kinds[a] in (TREE, NEST)]
    nests = [a for a in range(n) if kinds[a] == NEST]
    used = [axis for axis in (DP, TP) if axis in axes or (axis == TP and nests)]
    sizes = {axis: lax.axis_size(axis) for axis in used}
    half = sizes[DP] // 2 if trees else 0
    relayed = half == 4
    route, load = {}, [0, 0]
    for a in sorted(trees, key=lambda a: -arrays[a].size * (4 if a in nests else 1)):
        route[a] = 1 + (load[0] > load[1])
        load[route[a] - 1] += arrays[a].size * (4 if a in nests else 1)
    most = max(half if a in trees else sizes[axes[a]] for a in range(n))

    def columns(ref, a, p, kind):
        wide = arrays[a].shape[-1] // (sizes[axes[a]] if kind == SPLIT else 1)
        return ref.at[:, pl.ds(pl.multiple_of(p * wide, wide), wide)]

    def body(*refs):
        ins, outs = refs[:n], refs[n : 2 * n]
        stages = dict(zip(nests, refs[2 * n : 2 * n + len(nests)]))
        send, recv, pass_send, pass_recv, nest_send, nest_recv, local = refs[2 * n + len(nests) :]
        me = {axis: lax.axis_index(axis) for axis in used}
        barrier = pltpu.get_barrier_semaphore()
        for axis in used:

            @pl.loop(1, sizes[axis])
            def _(d):
                pl.semaphore_signal(
                    barrier,
                    inc=1,
                    device_id={axis: lax.rem(me[axis] + d, sizes[axis])},
                    device_id_type=MESH,
                )

        def source(a, p):
            if kinds[a] in (PIECE, SIDE):
                return ins[a].at[p]
            return columns(ins[a], a, p, SPLIT) if kinds[a] == SPLIT else ins[a]

        def place(a, p):
            return columns(outs[a], a, p, SIDE) if kinds[a] == SIDE else outs[a].at[p]

        own = []
        for a in range(n):
            if kinds[a] == NEST:
                home = columns(stages[a], a, me[TP], SIDE)
                own.append(pltpu.make_async_copy(ins[a], home, local.at[a]))
            else:
                here = me[axes[a]]
                own.append(pltpu.make_async_copy(source(a, here), place(a, here), local.at[a]))
        for c in own:
            c.start()
        pl.semaphore_wait(barrier, sum(sizes.values()) - len(used))

        def copy(a, d):
            axis = axes[a]
            peer = lax.rem(me[axis] + d, sizes[axis])
            return pltpu.make_async_remote_copy(
                src_ref=source(a, peer),
                dst_ref=place(a, me[axis]),
                send_sem=send.at[a, d],
                recv_sem=recv.at[a, d],
                device_id={axis: peer},
                device_id_type=MESH,
            )

        def nest_copy(a, d):
            return pltpu.make_async_remote_copy(
                src_ref=ins[a],
                dst_ref=columns(stages[a], a, me[TP], SIDE),
                send_sem=nest_send.at[nests.index(a), d],
                recv_sem=nest_recv.at[nests.index(a), d],
                device_id={TP: lax.rem(me[TP] + d, sizes[TP])},
                device_id_type=MESH,
            )

        def first(a):
            return stages[a] if a in stages else ins[a]

        def partner(d):
            if not relayed:
                return lax.rem(me[DP] + 2 * d, sizes[DP])
            across = 2 - 4 * lax.rem(lax.div(me[DP], 2), 2) if d & 1 else 0
            along = 4 - 8 * lax.div(me[DP], 4) if d & 2 else 0
            return me[DP] + across + along

        def holder(d):
            if relayed or (isinstance(d, int) and d == 0):
                return partner(d) if d else me[DP]
            return lax.rem(me[DP] - 2 * d + sizes[DP], sizes[DP])

        def tree_copy(a, d):
            relay = relayed and d == 3
            shard = outs[a].at[holder(route[a])] if relay else first(a)
            return pltpu.make_async_remote_copy(
                src_ref=shard,
                dst_ref=shard if relay else outs[a].at[me[DP]],
                send_sem=send.at[a, d],
                recv_sem=recv.at[a, d],
                device_id={DP: partner(3 - route[a] if relay else d)},
                device_id_type=MESH,
            )

        def pass_on(a, d):
            own = isinstance(d, int) and d == 0
            return pltpu.make_async_remote_copy(
                src_ref=first(a) if own else outs[a].at[holder(d)],
                dst_ref=outs[a].at[holder(d)],
                send_sem=pass_send.at[trees.index(a), d],
                recv_sem=pass_recv.at[trees.index(a), d],
                device_id={DP: me[DP] + 1 - 2 * lax.rem(me[DP], 2)},
                device_id_type=MESH,
            )

        def over(start, stop, chosen, step):
            if chosen:

                @pl.loop(start, stop)
                def _(d):
                    for a in chosen:
                        step(a, d)

        plain = [a for a in trees if a not in nests]
        over(1, sizes.get(TP, 1), nests, lambda a, d: nest_copy(a, d).start())

        def begin(chosen):
            if relayed:
                for a in chosen:
                    tree_copy(a, 1).start()
                    tree_copy(a, 2).start()
            else:
                over(1, half, chosen, lambda a, d: tree_copy(a, d).start())
            for a in chosen:
                pass_on(a, 0).start()

        begin(plain)
        flat = {axis: [a for a in range(n) if axes[a] == axis and a not in trees] for axis in used}
        for axis in used:
            over(1, sizes[axis], flat[axis], lambda a, d: copy(a, d).start())
        over(1, sizes.get(TP, 1), nests, lambda a, d: nest_copy(a, d).wait())
        homes = []
        for a in nests:
            own[a].wait()
            homes.append(pltpu.make_async_copy(stages[a], outs[a].at[me[DP]], local.at[a]))
            homes[-1].start()
        begin(nests)

        def forward(a, d):
            tree_copy(a, d).wait_recv()
            pass_on(a, d).start()

        def settle(a, d):
            tree_copy(a, d).wait_send()
            pass_on(a, d).wait()

        for chosen in (plain, nests):
            if relayed:
                for a in chosen:
                    forward(a, route[a])
                    tree_copy(a, 3).start()
                for a in chosen:
                    forward(a, 3 - route[a])
            else:
                over(1, half, chosen, forward)
        if relayed:
            for a in trees:
                forward(a, 3)
            for d in range(1, 4):
                for a in trees:
                    settle(a, d)
        else:
            over(1, half, trees, settle)
        for a in trees:
            pass_on(a, 0).wait()
        for axis in used:
            over(1, sizes[axis], flat[axis], lambda a, d: copy(a, d).wait())
        for c in homes + [own[a] for a in range(n) if a not in nests]:
            c.wait()

    shapes = []
    for a, x in enumerate(arrays):
        peers = sizes[axes[a]]
        shape = {
            PIECE: (peers,) + x.shape[1:],
            SPLIT: (peers, x.shape[0], x.shape[-1] // peers),
            SIDE: x.shape[1:-1] + (peers * x.shape[-1],),
            NEST: (peers, x.shape[0], sizes.get(TP, 1) * x.shape[-1]),
        }.get(kinds[a], (peers,) + x.shape)
        shapes.append(jax.ShapeDtypeStruct(shape, x.dtype))
    for a in nests:
        shapes.append(jax.ShapeDtypeStruct(shapes[a].shape[1:], arrays[a].dtype))
    flat_sems = pltpu.SemaphoreType.DMA((n, most))
    pass_sems = pltpu.SemaphoreType.DMA((max(len(trees), 1), max(half, 1)))
    nest_sems = pltpu.SemaphoreType.DMA((max(len(nests), 1), sizes.get(TP, 1)))
    return pl.pallas_call(
        body,
        out_shape=shapes,
        in_specs=[ANY] * n,
        out_specs=[ANY] * len(shapes),
        scratch_shapes=[flat_sems] * 2
        + [pass_sems] * 2
        + [nest_sems] * 2
        + [pltpu.SemaphoreType.DMA((n,))],
        compiler_params=pltpu.CompilerParams(collective_id=cid, has_side_effects=True),
    )(*arrays)[:n]


def whole(shape):
    return pl.BlockSpec(shape, lambda *_: (0,) * len(shape))


def stage(body, outs, ins, scratch=(), limit=56):
    return pl.pallas_call(
        body,
        grid=(1,),
        out_shape=[jax.ShapeDtypeStruct(shape, dtype) for shape, dtype in outs],
        in_specs=[whole(x.shape) for x in ins],
        out_specs=[whole(shape) for shape, _ in outs],
        scratch_shapes=list(scratch),
        compiler_params=pltpu.CompilerParams(vmem_limit_bytes=limit << 20),
    )(*ins)


def rms_forward(values, gain):
    factor = lax.rsqrt(jnp.mean(values * values, axis=-1, keepdims=True) + EPS)
    return values * factor * gain


def rms_backward(values, gain, upstream):
    factor = lax.rsqrt(jnp.mean(values * values, axis=-1, keepdims=True) + EPS)
    scaled = upstream * gain
    return factor * scaled - values * (factor * factor * factor) * jnp.mean(
        values * scaled, axis=-1, keepdims=True
    )


def masked(values, owner):
    columns = lax.broadcasted_iota(I32, values.shape, 1)
    adapter = lax.rem(lax.div(columns, RANK), NAD)
    return jnp.where(adapter == owner, values, 0.0).astype(BF16)


def folding(parts):
    shape = (parts * RANK, parts * NAD * RANK)
    short = lax.broadcasted_iota(I32, shape, 0)
    column = lax.broadcasted_iota(I32, shape, 1)
    same = (lax.div(short, RANK) == lax.div(column, NAD * RANK)) & (
        lax.rem(short, RANK) == lax.rem(column, RANK)
    )
    return jnp.where(same, 1.0, 0.0).astype(BF16)


def shorten(values):
    return mt(folding(values.shape[1] // (NAD * RANK)), values).astype(BF16)


def lengthen(short, owner):
    return masked(tm(short, folding(short.shape[0] // RANK)), owner)


def side_by_side(blocks):
    return jnp.concatenate([blocks[p] for p in range(blocks.shape[0])], axis=1)


def block_probs(queries, keys, across_ref, down_ref, r, block):
    top = (r + 1) * block
    at = slice(r * block, top)
    scores = mt(queries[at], keys[:top]) * HD**-0.5
    place = lax.broadcasted_iota(I32, (block, top), 0) + r * block
    other = lax.broadcasted_iota(I32, (block, top), 1)
    ahead = across_ref[:, :top]
    seen = (other <= place) & ((ahead == 0) | (ahead == down_ref[at, :]))
    scores = jnp.where(seen, scores, NEGATIVE)
    raised = jnp.exp(scores - jnp.max(scores, axis=-1, keepdims=True))
    return raised / jnp.sum(raised, axis=-1, keepdims=True)


def wide_lanes(pair, base=0):
    return pl.ds(pl.multiple_of(base + pair * 2 * HD, 2 * HD), 2 * HD)


def project_and_attend(rows, gain, down, ups, weight, across, below, owner, block=128):
    count, model = rows.shape
    width = weight.shape[1] // 3
    space = NAD * RANK

    def body(
        rows_ref, gain_ref, down_ref, ups_ref, weight_ref, across_ref, below_ref, owner_ref,
        normed_ref, low_ref, projected_ref, out_ref,
    ):
        @pl.loop(0, count // block)
        def _(c):
            at = pl.ds(pl.multiple_of(c * block, block), block)
            normed = rms_forward(rows_ref[at, :].astype(F32), gain_ref[...]).astype(BF16)
            normed_ref[at, :] = normed
            low = masked(mm(normed, down_ref[...]), owner_ref[at, :])
            low_ref[at, :] = low
            for p in range(3):
                lanes = slice(p * width, (p + 1) * width)
                projected_ref[at, lanes] = (
                    mm(normed, weight_ref[:, lanes])
                    + mm(low[:, p * space : (p + 1) * space], ups_ref[:, lanes])
                ).astype(BF16)

        @pl.loop(0, width // (2 * HD))
        def _(pair):
            queries, keys, values = [projected_ref[:, wide_lanes(pair, p * width)] for p in range(3)]
            for r in range(count // block):
                top = (r + 1) * block
                parts = []
                for lanes in (slice(0, HD), slice(HD, 2 * HD)):
                    probs = block_probs(
                        queries[:, lanes], keys[:, lanes], across_ref, below_ref, r, block
                    )
                    parts.append(mm(probs.astype(BF16), values[:top, lanes]))
                out_ref[r * block : top, wide_lanes(pair)] = jnp.concatenate(
                    parts, axis=1
                ).astype(BF16)

    return stage(
        body,
        [
            ((count, model), BF16),
            ((count, 3 * space), BF16),
            ((count, 3 * width), BF16),
            ((count, width), BF16),
        ],
        (rows, gain, down, ups, weight, across, below, owner),
    )


def after_attention(attended, attend_t, out_t, ups, spot, rows, gain, owner):
    local, model = rows.shape

    def body(
        attended_ref, attend_ref, out_ref, ups_ref, rows_ref, gain_ref, owner_ref,
        middle_ref, normed_ref, short_ref,
    ):
        low = masked(mt(attended_ref[...], attend_ref[...]), owner_ref[...])
        middle = (
            rows_ref[...].astype(F32)
            + mt(attended_ref[...], out_ref[...])
            + mm(low, ups_ref[:, spot])
        )
        middle_ref[...] = middle
        normed_ref[...] = rms_forward(middle, gain_ref[...]).astype(BF16)
        short_ref[...] = shorten(low)

    return stage(
        body,
        [((local, model), F32), ((local, model), BF16), ((RANK, local), BF16)],
        (attended, attend_t, out_t, ups, rows, gain, owner),
    )


def ask_memory(normed, down, query, gate, ups, query_spot, gate_spot, owner, keys, picks, block=128):
    count = normed.shape[0]
    half = keys.shape[2]
    number = picks.shape[2]
    width = gate.shape[1]
    space = NAD * RANK
    scale = (2 * half) ** -0.5

    def body(
        normed_ref, down_ref, query_ref, gate_ref, ups_ref, owner_ref, keys_ref, picks_ref,
        low_ref, gate_pre_ref, weights_ref, narrow_ref, asked, every,
    ):
        rank = lax.axis_index(TP)

        @pl.loop(0, count // block)
        def _(c):
            at = pl.ds(pl.multiple_of(c * block, block), block)
            rows = normed_ref[at, :]
            low = masked(mm(rows, down_ref[...]), owner_ref[at, :])
            low_ref[at, :] = low
            asked[at, :] = mm(rows, query_ref[...]) + mm(low[:, :space], ups_ref[:, query_spot])
            gate_pre_ref[at, :] = mm(rows, gate_ref[...]) + mm(
                low[:, space:], ups_ref[:, gate_spot]
            )

        slot = lax.broadcasted_iota(I32, (NKEYS, block), 0)
        for part in range(2):
            top, rest = two_parts(asked[:, part * half : (part + 1) * half])
            every[...] = mt(keys_ref[part], top) + mt(keys_ref[part], rest)

            @pl.loop(0, count // block)
            def _(c):
                lanes = pl.ds(pl.multiple_of(c * block, block), block)
                scores = every[:, lanes]
                rows = []
                for k in range(number):
                    hit = slot == picks_ref[rank, part, k : k + 1, lanes]
                    rows.append(jnp.sum(jnp.where(hit, scores, 0.0), axis=0, keepdims=True))
                found = jnp.concatenate(rows, axis=0)
                if part == 0:
                    weights_ref[:, lanes] = found
                else:
                    total = (weights_ref[:, lanes] + found) * scale
                    raised = jnp.exp(total - jnp.max(total, axis=0, keepdims=True))
                    weights = raised / jnp.sum(raised, axis=0, keepdims=True)
                    weights_ref[:, lanes] = weights
                    narrow_ref[:, lanes] = weights.astype(BF16)

    return stage(
        body,
        [
            ((count, 2 * space), BF16),
            ((count, width), F32),
            ((number, count), F32),
            ((number, count), BF16),
        ],
        (normed, down, query, gate, ups, owner, keys, picks),
        [pltpu.VMEM((count, 2 * half), F32), pltpu.VMEM((NKEYS, count), F32)],
    )


def mixed_upstream(rows, mixed_t, ups, up_spot, low_spot, owner, block=128):
    count = rows.shape[0]
    width = mixed_t.shape[1]

    def body(rows_ref, mixed_ref, ups_ref, owner_ref, low_ref, out_ref):
        @pl.loop(0, count // block)
        def _(c):
            at = pl.ds(pl.multiple_of(c * block, block), block)
            low = masked(mt(rows_ref[at, :], ups_ref[:, up_spot]), owner_ref[at, :])
            low_ref[at, :] = low
            out_ref[at, :] = mm(rows_ref[at, :], mixed_ref[...]) + mm(low, ups_ref[:, low_spot])

    return stage(
        body,
        [((count, NAD * RANK), BF16), ((count, width), F32)],
        (rows, mixed_t, ups, owner),
    )


def memory_back(
    weights, pieces, keys, picks, query, gate, grad_gate, mixed, ups, spots, owner, block=128
):
    query_spot, gate_spot, low_spot = spots
    number, count = weights.shape
    half = keys.shape[2]
    scale = (2 * half) ** -0.5
    model = query.shape[0]

    def body(
        weights_ref, pieces_ref, keys_ref, picks_ref, query_ref, gate_ref, grad_gate_ref,
        mixed_ref, ups_ref, owner_ref, grad_query_ref, partial_ref, three_ref, four_ref, dense,
    ):
        rank = lax.axis_index(TP)
        slot = lax.broadcasted_iota(I32, (NKEYS, block), 0)
        for part in range(2):

            @pl.loop(0, count // block)
            def _(c):
                lanes = pl.ds(pl.multiple_of(c * block, block), block)
                weight = weights_ref[:, lanes]
                grad = sum(pieces_ref[p, :, lanes].astype(F32) for p in range(pieces.shape[0]))
                grad = weight * (grad - jnp.sum(grad * weight, axis=0, keepdims=True)) * scale
                total = jnp.zeros((NKEYS, block), F32)
                for k in range(number):
                    hit = slot == picks_ref[rank, part, k : k + 1, lanes]
                    total += jnp.where(hit, grad[k : k + 1, :], 0.0)
                dense[:, lanes] = total

            top, rest = two_parts(dense[...])
            grad_query_ref[:, part * half : (part + 1) * half] = (
                tm(top, keys_ref[part]) + tm(rest, keys_ref[part])
            ).astype(BF16)

        @pl.loop(0, count // block)
        def _(c):
            at = pl.ds(pl.multiple_of(c * block, block), block)
            asked, gates, own = grad_query_ref[at, :], grad_gate_ref[at, :], owner_ref[at, :]
            partial_ref[at, :] = (mt(asked, query_ref[...]) + mt(gates, gate_ref[...])).astype(BF16)
            three = jnp.concatenate(
                [mt(asked, ups_ref[:, query_spot]), mt(gates, ups_ref[:, gate_spot])], axis=1
            )
            three_ref[:, at] = shorten(masked(three, own))
            four_ref[:, at] = shorten(masked(mt(mixed_ref[at, :], ups_ref[:, low_spot]), own))

    return stage(
        body,
        [
            ((count, 2 * half), BF16),
            ((count, model), BF16),
            ((2 * RANK, count), BF16),
            ((RANK, count), BF16),
        ],
        (weights, pieces, keys, picks, query, gate, grad_gate, mixed, ups, owner),
        [pltpu.VMEM((NKEYS, count), F32)],
    )


def residual_back(
    pieces, three, four, middle, cotangent, gain, down_memory, ups, spots, out_t, attend_t, owner,
    mixed_parts,
):
    attend_spot, mixed_spot = spots
    local, model = middle.shape
    count = three.shape[2]

    def body(
        pieces_ref, three_ref, four_ref, middle_ref, cotangent_ref, gain_ref, down_ref, ups_ref,
        out_ref, attend_ref, owner_ref, *refs
    ):
        mixed_refs = refs[: len(mixed_parts)]
        middle_grad_ref, branch_ref, attended_ref, short_ref, three_sum_ref, four_sum_ref, added_ref = (
            refs[len(mixed_parts) :]
        )
        own = pl.ds(pl.multiple_of(lax.axis_index(TP) * local, local), local)
        owner = owner_ref[...]

        def total(ref):
            return sum(ref[p].astype(F32) for p in range(ref.shape[0]))

        three_sum_ref[...] = total(three_ref).astype(BF16)
        four_sum_ref[...] = total(four_ref).astype(BF16)
        low_four = lengthen(four_sum_ref[:, own], owner)
        added_ref[...] = (
            middle_ref[...]
            + sum(ref[...].astype(F32) for ref in mixed_refs)
            + mm(low_four, ups_ref[:, mixed_spot])
        ).astype(BF16)
        grad_three = lengthen(three_sum_ref[:, own], owner)
        upstream = total(pieces_ref) + mt(grad_three, down_ref[...])
        grad = cotangent_ref[...].astype(F32) + rms_backward(
            middle_ref[...], gain_ref[...], upstream
        )
        middle_grad_ref[...] = grad
        branch = grad.astype(BF16)
        branch_ref[...] = branch
        low = masked(mt(branch, ups_ref[:, attend_spot]), owner)
        attended_ref[...] = (mm(branch, out_ref[...]) + mm(low, attend_ref[...])).astype(BF16)
        short_ref[...] = shorten(low)

    return stage(
        body,
        [
            ((local, model), F32),
            ((local, model), BF16),
            ((local, model), BF16),
            ((RANK, local), BF16),
            ((2 * RANK, count), BF16),
            ((RANK, count), BF16),
            ((local, model), BF16),
        ],
        (
            pieces, three, four, middle, cotangent, gain, down_memory, ups, out_t, attend_t, owner,
            *mixed_parts,
        ),
    )


def attend_back(projected, upstream, across, below, weight, ups, owner, block=128):
    count = projected.shape[0]
    width = weight.shape[1] // 3
    model = weight.shape[0]

    def body(
        projected_ref, upstream_ref, across_ref, below_ref, weight_ref, ups_ref, owner_ref,
        grads_ref, partial_ref, short_ref, key_sum, value_sum,
    ):
        @pl.loop(0, width // (2 * HD))
        def _(pair):
            queries, keys, values = [projected_ref[:, wide_lanes(pair, p * width)] for p in range(3)]
            above = upstream_ref[:, wide_lanes(pair)]
            key_sum[...] = jnp.zeros_like(key_sum)
            value_sum[...] = jnp.zeros_like(value_sum)
            for r in range(count // block):
                at, top = slice(r * block, (r + 1) * block), (r + 1) * block
                parts = []
                for h in range(2):
                    lanes = slice(h * HD, (h + 1) * HD)
                    probs = block_probs(
                        queries[:, lanes], keys[:, lanes], across_ref, below_ref, r, block
                    )
                    grad_probs = mt(above[at, lanes], values[:top, lanes])
                    inner = jnp.sum(probs * grad_probs, axis=-1, keepdims=True)
                    grad_scores = (probs * (grad_probs - inner)).astype(BF16)
                    parts.append(mm(grad_scores, keys[:top, lanes]))
                    key_sum[h, :top, :] += tm(grad_scores, queries[at, lanes])
                    value_sum[h, :top, :] += tm(probs.astype(BF16), above[at, lanes])
                grads_ref[at, wide_lanes(pair)] = (
                    jnp.concatenate(parts, axis=1) * HD**-0.5
                ).astype(BF16)
            grads_ref[:, wide_lanes(pair, width)] = (
                jnp.concatenate([key_sum[0], key_sum[1]], axis=1) * HD**-0.5
            ).astype(BF16)
            grads_ref[:, wide_lanes(pair, 2 * width)] = jnp.concatenate(
                [value_sum[0], value_sum[1]], axis=1
            ).astype(BF16)

        @pl.loop(0, count // block)
        def _(c):
            at = pl.ds(pl.multiple_of(c * block, block), block)
            partial_ref[at, :] = mt(grads_ref[at, :], weight_ref[...]).astype(BF16)
            one = jnp.concatenate(
                [
                    mt(
                        grads_ref[at, p * width : (p + 1) * width],
                        ups_ref[:, p * width : (p + 1) * width],
                    )
                    for p in range(3)
                ],
                axis=1,
            )
            short_ref[:, at] = shorten(masked(one, owner_ref[at, :]))

    return stage(
        body,
        [((count, 3 * width), BF16), ((count, model), BF16), ((3 * RANK, count), BF16)],
        (projected, upstream, across, below, weight, ups, owner),
        [pltpu.VMEM((2, count, HD), F32)] * 2,
    )


def input_back(pieces, one, grad_middle, rows, gain, down, owner):
    local, model = rows.shape
    count = one.shape[2]

    def body(
        pieces_ref, one_ref, middle_ref, rows_ref, gain_ref, down_ref, owner_ref, out_ref, sum_ref
    ):
        own = pl.ds(pl.multiple_of(lax.axis_index(TP) * local, local), local)

        def total(ref):
            return sum(ref[p].astype(F32) for p in range(ref.shape[0]))

        sum_ref[...] = total(one_ref).astype(BF16)
        low = lengthen(sum_ref[:, own], owner_ref[...])
        upstream = total(pieces_ref) + mt(low, down_ref[...])
        out_ref[...] = middle_ref[...] + rms_backward(
            rows_ref[...].astype(F32), gain_ref[...], upstream
        )

    return stage(
        body,
        [((local, model), F32), ((3 * RANK, count), BF16)],
        (pieces, one, grad_middle, rows, gain, down, owner),
    )


def own_columns(short, owner, first):
    high, count = short.shape
    adapters = NAD // lax.axis_size(TP)
    pattern = lax.broadcasted_iota(I32, (high, adapters * high), 0) == lax.rem(
        lax.broadcasted_iota(I32, (high, adapters * high), 1), high
    )
    spread = tm(short, jnp.where(pattern, 1.0, 0.0).astype(BF16))
    adapter = lax.div(lax.broadcasted_iota(I32, (count, adapters * high), 1), high) + first
    return jnp.where(adapter == owner, spread, 0.0).astype(BF16)


def adapter_grads(
    low_one, grad_projected, low_three, grad_query, grad_gate, two_short, branch, four_short,
    cotangent, two_back, attended, grad_low_four, mixed, normed_one, one_short, normed_two,
    three_short, owner,
):
    count, width = attended.shape
    model = normed_one.shape[1]
    space = NAD * RANK
    cut = NAD // lax.axis_size(TP) * RANK
    asked = grad_query.shape[1]

    def body(
        low_one_ref, projected_ref, low_three_ref, query_ref, gate_ref, two_ref, branch_ref,
        four_ref, cotangent_ref, back_ref, attended_ref, low_four_ref, mixed_ref, one_rows_ref,
        one_ref, two_rows_ref, three_ref, owner_ref, ups_ref, downs_ref,
    ):
        owner = owner_ref[...]
        rank = lax.axis_index(TP)
        at = 0

        def put(low, rows):
            nonlocal at
            ups_ref[:, at : at + rows.shape[1]] = tm(low, rows).astype(BF16)
            at += rows.shape[1]

        for p in range(3):
            put(
                low_one_ref[:, p * space : (p + 1) * space],
                projected_ref[:, p * width : (p + 1) * width],
            )
        put(low_three_ref[:, :space], query_ref[...])
        put(low_three_ref[:, space:], gate_ref[...])
        put(lengthen(side_by_side(two_ref), owner), branch_ref[...])
        own = pl.ds(pl.multiple_of(rank * width, width), width)
        put(lengthen(four_ref[...], owner), cotangent_ref[:, own])
        put(lengthen(side_by_side(back_ref), owner), attended_ref[...])
        put(low_four_ref[...], mixed_ref[...])
        first = rank * (NAD // lax.axis_size(TP))
        one = own_columns(one_ref[...], owner, first)
        three = own_columns(three_ref[...], owner, first)

        @pl.loop(0, model // width)
        def _(c):
            lanes = pl.ds(pl.multiple_of(c * width, width), width)
            downs_ref[lanes, : 3 * cut] = tm(one_rows_ref[:, lanes], one).astype(BF16)
            downs_ref[lanes, 3 * cut :] = tm(two_rows_ref[:, lanes], three).astype(BF16)

    return stage(
        body,
        [((space, 7 * width + 2 * width + asked - width), BF16), ((model, 5 * cut), BF16)],
        (
            low_one, grad_projected, low_three, grad_query, grad_gate, two_short, branch,
            four_short, cotangent, two_back, attended, grad_low_four, mixed, normed_one,
            one_short, normed_two, three_short, owner,
        ),
    )


def spread_picks(first, second, weights, sub=32, conv=32):
    tokens, picks = first.shape
    stride = sub + 1

    def body(first_ref, second_ref, weights_ref, out_ref, low, high):
        slot = lax.broadcasted_iota(I32, (NKEYS, picks), 0)
        for n in range(sub):
            b = jnp.where(slot == second_ref[n : n + 1, :], 1.0, 0.0).astype(BF16)
            a = jnp.where(slot == first_ref[n : n + 1, :], weights_ref[n : n + 1, :], 0.0)
            both = mt(a.astype(BF16), b)
            low[pl.ds(n, NKEYS, stride=stride), :] = both[:, :128]
            high[pl.ds(n, NKEYS, stride=stride), :] = both[:, 128:]

        @pl.loop(0, NKEYS // conv)
        def _(c):
            for q in range(conv):
                i = c * conv + q
                at = pl.multiple_of(i * NKEYS, NKEYS)
                rows = pl.ds(i * stride, sub)
                out_ref[:, pl.ds(at, 128)] = low[rows, :].astype(BF16)
                out_ref[:, pl.ds(at + 128, 128)] = high[rows, :].astype(BF16)

    line = pl.BlockSpec((sub, picks), lambda t: (t, 0))
    rows = NKEYS * NKEYS
    return pl.pallas_call(
        body,
        grid=(tokens // sub,),
        out_shape=jax.ShapeDtypeStruct((tokens, rows), BF16),
        in_specs=[line] * 3,
        out_specs=pl.BlockSpec((sub, rows), lambda t: (t, 0)),
        scratch_shapes=[pltpu.VMEM((NKEYS * stride, 128), F32)] * 2,
        compiler_params=pltpu.CompilerParams(vmem_limit_bytes=40 << 20),
    )(first, second, weights)


def recall(dense, table, part, parts, before, after):
    tokens, rows = dense.shape
    width = table.shape[2]
    groups, block = table.shape[0], table.shape[1]
    last = part == parts - 1

    def body(*refs):
        dense_ref, table_ref = refs[:2]
        step = pl.program_id(0)
        total = refs[-1]

        @pl.when(step == 0)
        def _():
            total[...] = refs[2][...] if part else jnp.zeros_like(total)

        total[...] += mm(dense_ref[...], table_ref[...])
        if not last:
            return

        @pl.when(step == groups - 1)
        def _():
            gate_ref, upstream_ref, norms_ref = refs[-8:-5]
            mixed_ref, grad_ref, grad_gate_ref, scale_ref = refs[-5:-1]
            gate, recalled, upstream = gate_ref[...], total[...], upstream_ref[...]
            sigmoid = 1.0 / (1.0 + jnp.exp(-gate))
            act = gate * sigmoid
            mixed_ref[...] = (act * recalled).astype(BF16)
            grad = (upstream * act).astype(BF16)
            grad_ref[...] = grad
            grad_gate_ref[...] = (
                upstream * recalled * sigmoid * (1.0 + gate * (1.0 - sigmoid))
            ).astype(BF16)
            wide = grad.astype(F32)
            bound = jnp.max(norms_ref[...]) * jnp.sum(wide * wide, axis=1, keepdims=True)
            scale_ref[...] = 32000.0 * lax.rsqrt(jnp.maximum(bound, 1e-30))

    one = (tokens, width)
    outs = [(one, BF16)] * 3 + [((tokens, 1), F32)] if last else [(one, F32)]
    more = ([before] if part else []) + (list(after) if last else [])
    return pl.pallas_call(
        body,
        grid=(groups,),
        out_shape=[jax.ShapeDtypeStruct(shape, dtype) for shape, dtype in outs],
        in_specs=[
            pl.BlockSpec((tokens, block), lambda s: (0, s * parts + part)),
            pl.BlockSpec((None, block, width), lambda s: (s, 0, 0)),
        ]
        + [whole(x.shape) for x in more],
        out_specs=[whole(shape) for shape, _ in outs],
        scratch_shapes=[pltpu.VMEM(one, F32)] if last else [],
        compiler_params=pltpu.CompilerParams(vmem_limit_bytes=40 << 20),
    )(dense, table, *more)


def pick_grads(first, second, grads, scale, table, part, parts, before):
    tokens, picks = first.shape
    width = grads.shape[1]
    groups, rows = table.shape[0], table.shape[1]
    per_block = rows // NKEYS
    last = part == parts - 1

    def body(first_ref, second_ref, grads_ref, scale_ref, table_ref, *refs):
        step = pl.program_id(0)
        out_ref, kept = refs[-2], refs[-1]

        @pl.when(step == 0)
        def _():
            kept[...] = refs[0][...] if part else jnp.zeros_like(kept)

        own = first_ref[...]
        low = second_ref[...] & 127
        factor = jnp.broadcast_to(scale_ref[...], (tokens, 128))
        total = kept[...]
        for b in range(per_block):
            every = mt(grads_ref[...], table_ref[b * NKEYS : (b + 1) * NKEYS, :])
            packed = (every[:, 128:] * factor).astype(I32) * 65536 + (
                every[:, :128] * factor
            ).astype(I32)
            found = jnp.take_along_axis(packed, low, axis=1, mode="promise_in_bounds")
            total = jnp.where(own == (step * parts + part) * per_block + b, found, total)
        kept[...] = total

        @pl.when(step == groups - 1)
        def _():
            p = kept[...]
            if not last:
                out_ref[...] = p
                return
            right = lax.shift_right_arithmetic(lax.shift_left(p, 16), 16)
            left = lax.shift_right_arithmetic(p - right, 16)
            both = jnp.where(second_ref[...] >= 128, left, right).astype(F32) / factor
            out_ref[...] = both.T.astype(BF16)

    shape, dtype = ((picks, tokens), BF16) if last else ((tokens, picks), I32)
    more = [before] if part else []
    return pl.pallas_call(
        body,
        grid=(groups,),
        out_shape=jax.ShapeDtypeStruct(shape, dtype),
        in_specs=[whole(x.shape) for x in (first, second, grads, scale)]
        + [pl.BlockSpec((None, rows, width), lambda s: (s, 0, 0))]
        + [whole(x.shape) for x in more],
        out_specs=whole(shape),
        scratch_shapes=[pltpu.VMEM((tokens, picks), I32)],
        compiler_params=pltpu.CompilerParams(vmem_limit_bytes=48 << 20),
    )(first, second, grads, scale, table, *more)


def add_up(up_parts, down_parts, sizes, cut):
    high, tall, wide = up_parts.shape[1], down_parts.shape[1], down_parts.shape[2]

    def body(ups_ref, downs_ref, *out_refs):
        def total(ref, lanes):
            return sum(ref[p, :, lanes].astype(F32) for p in range(ref.shape[0]))

        at = 0
        for size, ref in zip(sizes, out_refs):
            ref[...] = total(ups_ref, slice(at, at + size))
            at += size
        out_refs[-2][...] = total(downs_ref, slice(0, cut))
        out_refs[-1][...] = total(downs_ref, slice(cut, wide))

    return stage(
        body,
        [((high, size), F32) for size in sizes] + [((tall, cut), F32), ((tall, wide - cut), F32)],
        (up_parts, down_parts),
    )


def make_ready(down_input, down_memory, turned, joined):
    def body(input_ref, memory_ref, *refs):
        ins, outs = refs[: len(turned) + len(joined)], refs[len(turned) + len(joined) :]

        def ordered(ref, parts):
            size = NAD * parts * RANK
            row = lax.broadcasted_iota(I32, (size, size), 0)
            column = lax.broadcasted_iota(I32, (size, size), 1)
            part, rest = lax.div(column, NAD * RANK), lax.rem(column, NAD * RANK)
            adapter, rank = lax.div(rest, RANK), lax.rem(rest, RANK)
            came = adapter * (parts * RANK) + part * RANK + rank
            return mm(ref[...], jnp.where(row == came, 1.0, 0.0).astype(BF16)).astype(BF16)

        outs[0][...] = ordered(input_ref, 3)
        outs[1][...] = ordered(memory_ref, 2)
        at = 0
        for ref in ins[len(turned) :]:
            outs[2][:, at : at + ref.shape[1]] = ref[...]
            at += ref.shape[1]
        for ref, out in zip(ins[: len(turned) - 1], outs[3:]):
            out[...] = ref[...].astype(F32).T.astype(BF16)
        outs[2][:, at:] = ins[len(turned) - 1][...].astype(F32).T.astype(BF16)

    small = sum(x.shape[1] for x in joined) + turned[-1].shape[0]
    return stage(
        body,
        [
            (down_input.shape, BF16),
            (down_memory.shape, BF16),
            ((joined[0].shape[0], small), BF16),
        ]
        + [(x.shape[::-1], BF16) for x in turned[:-1]],
        (down_input, down_memory, *turned, *joined),
    )


def by_part(down, parts):
    shaped = down.reshape(down.shape[0], NAD, parts, RANK).transpose(0, 2, 1, 3)
    return shaped.reshape(down.shape)


def on_device(
    inputs,
    cotangent,
    norm_attend,
    norm_memory,
    project_in,
    project_out,
    query_weight,
    gate_weight,
    memory_out,
    half_keys,
    value_table,
    key_picks,
    segment_ids,
    adapter_ids,
    down_input,
    up_input,
    down_attend,
    up_attend,
    down_memory,
    up_query,
    up_gate,
    down_mixed,
    up_mixed,
):
    groups = lax.axis_size(DP)
    ranks = lax.axis_size(TP)
    rank = lax.axis_index(TP)
    local = inputs.shape[0]
    count = segment_ids.shape[0]
    width = project_in.shape[2]
    model = inputs.shape[1]
    own_adapters = NAD // ranks

    flat_in = project_in.reshape(project_in.shape[0], 3 * width)
    joined = (up_input.reshape(up_input.shape[0], 3 * width), up_query, up_gate, up_attend, up_mixed)
    turned = (project_out, memory_out, down_attend, down_mixed)
    if project_out.shape[1] % 128 == 0:
        parted_input, parted_memory, small, out_turned, mixed_turned, attend_turned = make_ready(
            down_input, down_memory, turned, joined
        )
    else:
        parted_input, parted_memory = by_part(down_input, 3), by_part(down_memory, 2)
        out_turned, mixed_turned, attend_turned, low_turned = [x.T for x in turned]
        small = jnp.concatenate(joined + (low_turned,), axis=1)
    share = value_table.shape[0] // PARTS
    tables = [
        lax.all_gather(value_table[p * share : (p + 1) * share], DP, axis=0) for p in range(PARTS)
    ]
    got = exchange(
        [(inputs, SHARE, TP), (cotangent, SHARE, TP)]
        + [(x, TREE, DP) for x in (flat_in, parted_input, small)]
        + [(out_turned, NEST, DP), (attend_turned, NEST, DP)],
        1,
    )
    input_rows = got[0].reshape(count, model)
    cotangent_rows = got[1].reshape(count, model)
    full_in, full_down_input, ups, out_t, attend_t = [x.reshape(-1, x.shape[2]) for x in got[2:]]
    spots, at = [], 0
    for size in (3 * width, up_query.shape[1], width, model, model, width):
        spots.append(slice(at, at + size))
        at += size
    _, query_spot, gate_spot, attend_spot, mixed_spot, low_spot = spots

    owner = jnp.zeros((count,), I32)
    for s in range(adapter_ids.shape[1]):
        owner = jnp.where(segment_ids == s, adapter_ids[0, s], owner)
    owner = owner[:, None]
    owner_own = lax.dynamic_slice_in_dim(owner, rank * local, local, 0)
    across, below = segment_ids[None, :], segment_ids[:, None]
    gain_one = norm_attend.astype(F32)[None, :]
    gain_two = norm_memory.astype(F32)[None, :]
    first_picks = key_picks[:, 0].reshape(-1, count).T
    second_picks = key_picks[:, 1].reshape(-1, count).T
    keys = half_keys[0]

    normed_one, low_one, projected, attended = project_and_attend(
        input_rows, gain_one, full_down_input, ups, full_in, across, below, owner
    )
    (attended_own,) = exchange([(attended.reshape(ranks, local, width), SIDE, TP)], 2)
    middle, normed_two, two_short = after_attention(
        attended_own, attend_t, out_t, ups, attend_spot, inputs, gain_two, owner_own
    )
    largest = jnp.max(jnp.sum(jnp.square(value_table.astype(F32)), axis=1))
    got = exchange(
        [
            (normed_two, SHARE, TP),
            (two_short, SHARE, TP),
            (jnp.broadcast_to(largest, (8, 128)), SHARE, DP),
        ]
        + [(x, TREE, DP) for x in (query_weight, gate_weight, parted_memory, mixed_turned)],
        3,
    )
    normed_rows, two_short, norms = got[0].reshape(count, model), got[1], got[2]
    full_query, full_gate, full_down_memory, mixed_t = [x.reshape(-1, x.shape[2]) for x in got[3:]]
    low_three, gate_pre, weights, narrow = ask_memory(
        normed_rows,
        full_down_memory,
        full_query,
        full_gate,
        ups,
        query_spot,
        gate_spot,
        owner,
        keys,
        key_picks,
    )
    (all_weights,) = exchange([(narrow, SHARE, TP)], 4)
    by_token = all_weights.reshape(-1, count).astype(F32).T
    dense = spread_picks(first_picks, second_picks, by_token)
    grad_low_four, grad_mixed = mixed_upstream(
        cotangent_rows, mixed_t, ups, mixed_spot, low_spot, owner
    )
    recalled = None
    for part in range(PARTS):
        recalled = recall(
            dense, tables[part], part, PARTS, recalled, (gate_pre, grad_mixed, norms)
        )
        if part < PARTS - 1:
            (recalled,) = recalled
    mixed, grad_recalled, grad_gate, scale = recalled
    partial_mixed = mt(mixed, mixed_t).astype(BF16).reshape(ranks, local, model)

    def block_of(blocks, d):
        return lax.dynamic_index_in_dim(blocks, lax.rem(rank + d, ranks), 0, keepdims=False)

    def turn(d):
        return [(p, (p + d) % ranks) for p in range(ranks)]

    mixed_parts = [block_of(partial_mixed, 0)] + [
        lax.ppermute(block_of(partial_mixed, d), TP, turn(d)) for d in range(1, ranks)
    ]
    picked = None
    for part in range(PARTS):
        picked = pick_grads(
            first_picks, second_picks, grad_recalled, scale, tables[part], part, PARTS, picked
        )
    picked, mixed_parts = lax.optimization_barrier((picked, mixed_parts))
    (pick_pieces,) = exchange([(picked.reshape(ranks, -1, count), PIECE, TP)], 5)
    grad_query, partial_normed, three_short, four_short = memory_back(
        weights,
        pick_pieces,
        keys,
        key_picks,
        full_query,
        full_gate,
        grad_gate,
        mixed,
        ups,
        (query_spot, gate_spot, low_spot),
        owner,
    )
    normed_pieces, three_short, four_short = exchange(
        [
            (partial_normed.reshape(ranks, local, model), PIECE, TP),
            (three_short, SHARE, TP),
            (four_short, SHARE, TP),
        ],
        6,
    )
    grad_middle, grad_branch, grad_attended, two_back, three_short, four_short, outputs = (
        residual_back(
            normed_pieces,
            three_short,
            four_short,
            middle,
            cotangent,
            gain_two,
            full_down_memory,
            ups,
            (attend_spot, mixed_spot),
            out_t,
            attend_t,
            owner_own,
            mixed_parts,
        )
    )
    grad_attended, two_back = exchange([(grad_attended, SPLIT, TP), (two_back, SHARE, TP)], 7)
    grad_projected, partial_input, one_short = attend_back(
        projected, grad_attended.reshape(count, width), across, below, full_in, ups, owner
    )
    input_pieces, one_short, own_branch = exchange(
        [
            (partial_input.reshape(ranks, local, model), PIECE, TP),
            (one_short, SHARE, TP),
            (grad_branch, SPLIT, TP),
        ],
        8,
    )
    input_grad, one_short = input_back(
        input_pieces, one_short, grad_middle, inputs, gain_one, full_down_input, owner_own
    )
    up_sent, down_sent = adapter_grads(
        low_one,
        grad_projected,
        low_three,
        grad_query,
        grad_gate,
        two_short,
        own_branch.reshape(count, width),
        four_short,
        cotangent_rows,
        two_back,
        attended,
        grad_low_four,
        mixed,
        normed_one,
        one_short,
        normed_rows,
        three_short,
        owner,
    )
    up_parts, down_parts = exchange(
        [
            (up_sent.reshape(groups, -1, up_sent.shape[1]), PIECE, DP),
            (down_sent.reshape(groups, -1, down_sent.shape[1]), PIECE, DP),
        ],
        9,
    )
    parts = add_up(
        up_parts,
        down_parts,
        (3 * width, up_query.shape[1], width, width, width, width, width),
        own_adapters * 3 * RANK,
    )
    return (
        outputs,
        input_grad,
        parts[7],
        parts[0].reshape(up_input.shape),
        parts[5].T,
        parts[3],
        parts[8],
        parts[1],
        parts[2],
        parts[6].T,
        parts[4],
    )


def solution(mesh):
    rows = P((DP, TP), None)
    both = P(DP, TP)
    wide = P(DP, None)
    turned = P(TP, DP)
    split = P(DP, None, TP)
    return jax.shard_map(
        on_device,
        mesh=mesh,
        in_specs=(
            rows,
            rows,
            P(),
            P(),
            split,
            turned,
            both,
            both,
            turned,
            P(TP, None, None, None),
            both,
            P(None, None, None, DP),
            P(DP),
            wide,
            wide,
            split,
            turned,
            wide,
            wide,
            both,
            both,
            turned,
            wide,
        ),
        out_specs=(rows, rows, both, split, turned, both, both, both, both, turned, both),
        check_vma=False,
    )
```

```python
import types

import jax
import jax.numpy as jnp
from jax import lax
from jax.experimental import pallas as pl
from jax.experimental.pallas import tpu as pltpu
from jax.sharding import PartitionSpec as P

DP, TP = "dp", "tensor"
HD = 64
NKEYS = 256
RANK = 16
NAD = 8
EPS = 1e-06
NEGATIVE = -1e30
F32, BF16, I32 = jnp.float32, jnp.bfloat16, jnp.int32
MESH = pl.DeviceIdType.MESH
ANY = pl.BlockSpec(memory_space=pl.ANY)


def mm(a, b):
    return lax.dot_general(a, b, (((1,), (0,)), ((), ())), preferred_element_type=F32)


def mt(a, b):
    return lax.dot_general(a, b, (((1,), (1,)), ((), ())), preferred_element_type=F32)


def tm(a, b):
    return lax.dot_general(a, b, (((0,), (0,)), ((), ())), preferred_element_type=F32)


def two_parts(x):
    top = x.astype(BF16)
    return top, (x - top.astype(F32)).astype(BF16)


def whole(shape):
    return pl.BlockSpec(shape, lambda *_: (0,) * len(shape))


def stage(body, outs, ins, scratch=(), limit=56):
    return pl.pallas_call(
        body,
        grid=(1,),
        out_shape=[jax.ShapeDtypeStruct(shape, dtype) for shape, dtype in outs],
        in_specs=[whole(x.shape) for x in ins],
        out_specs=[whole(shape) for shape, _ in outs],
        scratch_shapes=list(scratch),
        compiler_params=pltpu.CompilerParams(vmem_limit_bytes=limit << 20),
    )(*ins)


def rms_forward(values, gain):
    factor = lax.rsqrt(jnp.mean(values * values, axis=-1, keepdims=True) + EPS)
    return values * factor * gain


def rms_backward(values, gain, upstream):
    factor = lax.rsqrt(jnp.mean(values * values, axis=-1, keepdims=True) + EPS)
    scaled = upstream * gain
    return factor * scaled - values * (factor * factor * factor) * jnp.mean(
        values * scaled, axis=-1, keepdims=True
    )


def masked(values, owner):
    columns = lax.broadcasted_iota(I32, values.shape, 1)
    adapter = lax.rem(lax.div(columns, RANK), NAD)
    return jnp.where(adapter == owner, values, 0.0).astype(BF16)


def folding(parts):
    shape = (parts * RANK, parts * NAD * RANK)
    short = lax.broadcasted_iota(I32, shape, 0)
    column = lax.broadcasted_iota(I32, shape, 1)
    same = (lax.div(short, RANK) == lax.div(column, NAD * RANK)) & (
        lax.rem(short, RANK) == lax.rem(column, RANK)
    )
    return jnp.where(same, 1.0, 0.0).astype(BF16)


def shorten(values):
    return mt(folding(values.shape[1] // (NAD * RANK)), values).astype(BF16)


def lengthen(short, owner):
    return masked(tm(short, folding(short.shape[0] // RANK)), owner)


def side_by_side(blocks):
    return jnp.concatenate([blocks[p] for p in range(blocks.shape[0])], axis=1)


def block_probs(queries, keys, across_ref, down_ref, r, block):
    top = (r + 1) * block
    at = slice(r * block, top)
    scores = mt(queries[at], keys[:top]) * HD**-0.5
    place = lax.broadcasted_iota(I32, (block, top), 0) + r * block
    other = lax.broadcasted_iota(I32, (block, top), 1)
    ahead = across_ref[:, :top]
    seen = (other <= place) & ((ahead == 0) | (ahead == down_ref[at, :]))
    scores = jnp.where(seen, scores, NEGATIVE)
    raised = jnp.exp(scores - jnp.max(scores, axis=-1, keepdims=True))
    return raised / jnp.sum(raised, axis=-1, keepdims=True)


def wide_lanes(pair, base=0):
    return pl.ds(pl.multiple_of(base + pair * 2 * HD, 2 * HD), 2 * HD)


def own_columns(short, owner, first):
    high, count = short.shape
    adapters = NAD // lax.axis_size(TP)
    pattern = lax.broadcasted_iota(I32, (high, adapters * high), 0) == lax.rem(
        lax.broadcasted_iota(I32, (high, adapters * high), 1), high
    )
    spread = tm(short, jnp.where(pattern, 1.0, 0.0).astype(BF16))
    adapter = lax.div(lax.broadcasted_iota(I32, (count, adapters * high), 1), high) + first
    return jnp.where(adapter == owner, spread, 0.0).astype(BF16)


class Waited:
    def __init__(self, names, refs, loads):
        self._pending = dict(zip(names, zip(refs, loads)))

    def __getattr__(self, name):
        ref, load = self._pending[name]
        load.wait()
        setattr(self, name, ref)
        return ref


def backward(given, mixed_parts, ups_spots, cid, block=128):
    _, query_spot, gate_spot, attend_spot, mixed_spot, low_spot = ups_spots
    shown = types.SimpleNamespace(**given)
    picked = given.pop(next(iter(given)))
    names = list(given)
    arrays = [picked, *given.values(), *mixed_parts]
    ranks, groups = lax.axis_size(TP), lax.axis_size(DP)
    count, width = shown.attended.shape
    local, model = shown.inputs.shape
    number = shown.weights.shape[0]
    half = shown.keys.shape[2]
    space = NAD * RANK
    adapters = NAD // ranks
    lines, share = space // groups, model // groups
    wides = [width] * 3 + [2 * half] + [width] * 5
    tall = [adapters * 2 * RANK, adapters * 3 * RANK]
    vmem = dict(
        pick_in=((ranks, number, count), BF16),
        dense=((NKEYS, count), F32),
        grad_query=((count, 2 * half), BF16),
        normed_out=((ranks, local, model), BF16),
        normed_in=((ranks, local, model), BF16),
        three_in=((ranks, 2 * RANK, count), BF16),
        four_in=((ranks, RANK, count), BF16),
        three_sum=((2 * RANK, count), BF16),
        four_sum=((RANK, count), BF16),
        attended_out=((local, model), BF16),
        attended_in=((ranks, local, width), BF16),
        branch_out=((local, model), BF16),
        branch_in=((ranks, local, width), BF16),
        back_in=((ranks, RANK, local), BF16),
        grad_middle=((local, model), F32),
        grads=((count, 3 * width), BF16),
        key_sum=((2, count, HD), F32),
        value_sum=((2, count, HD), F32),
        input_out=((ranks, local, model), BF16),
        input_in=((ranks, local, model), BF16),
        one_in=((ranks, 3 * RANK, count), BF16),
        one_sum=((3 * RANK, count), BF16),
        ups_out=((groups, lines, sum(wides)), BF16),
        memory_out=((groups, tall[0], share), BF16),
        down_out=((groups, tall[1], share), BF16),
        outputs=((local, model), BF16),
        input_grad=((local, model), F32),
    )
    inputs = arrays[1:]
    results = [
        ((local, model), BF16),
        ((local, model), F32),
        ((groups, lines, sum(wides)), BF16),
        ((groups, tall[0], share), BF16),
        ((groups, tall[1], share), BF16),
    ]

    def body(*refs):
        outs = refs[len(arrays) : len(arrays) + len(results)]
        rest = refs[len(arrays) + len(results) :]
        v = types.SimpleNamespace(**dict(zip(vmem, rest[len(inputs) :])))
        loaded, saved, send, recv, far_send, far_recv = rest[len(inputs) + len(vmem) :]
        rank, group = lax.axis_index(TP), lax.axis_index(DP)
        barrier = pltpu.get_barrier_semaphore()
        for d in range(1, ranks):
            pl.semaphore_signal(
                barrier,
                inc=1,
                device_id={TP: lax.rem(rank + d, ranks)},
                device_id_type=MESH,
            )

        @pl.loop(1, groups)
        def _(d):
            pl.semaphore_signal(
                barrier,
                inc=1,
                device_id={DP: lax.rem(group + d, groups)},
                device_id_type=MESH,
            )

        loads = [
            pltpu.make_async_copy(refs[i + 1], rest[i], loaded.at[i]) for i in range(len(inputs))
        ]
        for load in loads:
            load.start()
        need = Waited(names, rest, loads)

        def near(i, d, src, dst):
            return pltpu.make_async_remote_copy(
                src_ref=src,
                dst_ref=dst,
                send_sem=send.at[i, d],
                recv_sem=recv.at[i, d],
                device_id={TP: lax.rem(rank + d, ranks)},
                device_id_type=MESH,
            )

        def far(i, d, src, dst):
            return pltpu.make_async_remote_copy(
                src_ref=src,
                dst_ref=dst,
                send_sem=far_send.at[i, d],
                recv_sem=far_recv.at[i, d],
                device_id={DP: lax.rem(group + d, groups)},
                device_id_type=MESH,
            )

        def far_piece(i, d, ref):
            return far(i, d, ref.at[lax.rem(group + d, groups)], outs[2 + i].at[group])

        def send_far(i, ref):
            @pl.loop(1, groups)
            def _(d):
                far_piece(i, d, ref).start()

            keep = pltpu.make_async_copy(ref.at[group], outs[2 + i].at[group], saved.at[2 + i])
            keep.start()
            return keep

        def shared(i, ref):
            return [near(i, d, ref.at[rank], ref.at[rank]) for d in range(1, ranks)]

        def columns(ref, p):
            return ref.at[:, pl.ds(pl.multiple_of(p * width, width), width)]

        def split(i, src, dst):
            return [
                near(i, d, columns(src, lax.rem(rank + d, ranks)), dst.at[rank])
                for d in range(1, ranks)
            ]

        def total(ref):
            return sum(ref[p].astype(F32) for p in range(ranks))

        own_tokens = pl.ds(pl.multiple_of(rank * local, local), local)
        own_columns_at = pl.ds(pl.multiple_of(rank * width, width), width)

        pick_in = v.pick_in
        own_pick = pltpu.make_async_copy(refs[0].at[rank], pick_in.at[rank], saved.at[0])
        own_pick.start()
        pl.semaphore_wait(barrier, ranks + groups - 2)
        picks_sent = [
            near(0, d, refs[0].at[lax.rem(rank + d, ranks)], pick_in.at[rank])
            for d in range(1, ranks)
        ]
        for c in picks_sent:
            c.start()
        weights_ref, keys_ref, picks_ref = need.weights, need.keys, need.picks
        own_pick.wait()
        for c in picks_sent:
            c.wait()

        slot = lax.broadcasted_iota(I32, (NKEYS, block), 0)
        for part in range(2):

            @pl.loop(0, count // block)
            def _(c):
                lanes = pl.ds(pl.multiple_of(c * block, block), block)
                weight = weights_ref[:, lanes]
                grad = sum(pick_in[p, :, lanes].astype(F32) for p in range(ranks))
                grad = weight * (grad - jnp.sum(grad * weight, axis=0, keepdims=True))
                grad = grad * (2 * half) ** -0.5
                dense = jnp.zeros((NKEYS, block), F32)
                for k in range(number):
                    hit = slot == picks_ref[part, k : k + 1, lanes]
                    dense += jnp.where(hit, grad[k : k + 1, :], 0.0)
                v.dense[:, lanes] = dense

            top, low = two_parts(v.dense[...])
            v.grad_query[:, part * half : (part + 1) * half] = (
                tm(top, keys_ref[part]) + tm(low, keys_ref[part])
            ).astype(BF16)

        query_ref, gate_ref, ups_ref = need.query, need.gate, need.ups
        grad_gate_ref, mixed_ref, owner_ref = need.grad_gate, need.mixed, need.owner
        normed_sent = []
        for d in list(range(1, ranks)) + [0]:
            at = pl.ds(pl.multiple_of(lax.rem(rank + d, ranks) * local, local), local)
            asked, gates, own = v.grad_query[at, :], grad_gate_ref[at, :], owner_ref[at, :]
            part = (mt(asked, query_ref[...]) + mt(gates, gate_ref[...])).astype(BF16)
            if d:
                v.normed_out[d] = part
                normed_sent.append(near(1, d, v.normed_out.at[d], v.normed_in.at[rank]))
                normed_sent[-1].start()
            else:
                v.normed_in[rank] = part
            three = jnp.concatenate(
                [mt(asked, ups_ref[:, query_spot]), mt(gates, ups_ref[:, gate_spot])], axis=1
            )
            v.three_in[rank, :, at] = shorten(masked(three, own))
            v.four_in[rank, :, at] = shorten(
                masked(mt(mixed_ref[at, :], ups_ref[:, low_spot]), own)
            )
        short_sent = shared(2, v.three_in) + shared(3, v.four_in)
        for c in short_sent:
            c.start()
        owner_own = need.owner_own[...]
        middle_ref, cotangent_ref, gain_two = need.middle, need.cotangent, need.gain_two
        down_ref, out_ref, attend_ref = need.down_memory, need.out_t, need.attend_t
        mixed_refs = []
        for i in range(len(names), len(inputs)):
            loads[i].wait()
            mixed_refs.append(rest[i])
        for c in normed_sent + short_sent:
            c.wait()

        v.three_sum[...] = total(v.three_in).astype(BF16)
        v.four_sum[...] = total(v.four_in).astype(BF16)
        grad_three = lengthen(v.three_sum[:, own_tokens], owner_own)
        upstream = total(v.normed_in) + mt(grad_three, down_ref[...])
        grad = cotangent_ref[...].astype(F32) + rms_backward(
            middle_ref[...], gain_two[...].astype(F32), upstream
        )
        v.grad_middle[...] = grad
        branch = grad.astype(BF16)
        v.branch_out[...] = branch
        low = masked(mt(branch, ups_ref[:, attend_spot]), owner_own)
        v.attended_out[...] = (mm(branch, out_ref[...]) + mm(low, attend_ref[...])).astype(BF16)
        v.back_in[rank] = shorten(low)
        v.attended_in[rank] = v.attended_out[:, own_columns_at]
        v.branch_in[rank] = v.branch_out[:, own_columns_at]
        attended_sent = split(4, v.attended_out, v.attended_in)
        later_sent = shared(5, v.back_in) + split(6, v.branch_out, v.branch_in)
        for c in attended_sent + later_sent:
            c.start()

        low_four = lengthen(v.four_sum[:, own_tokens], owner_own)
        v.outputs[...] = (
            middle_ref[...]
            + sum(ref[...].astype(F32) for ref in mixed_refs)
            + mm(low_four, ups_ref[:, mixed_spot])
        ).astype(BF16)
        stores = [pltpu.make_async_copy(v.outputs, outs[0], saved.at[0])]
        stores[0].start()
        owner = owner_ref[...]
        starts = [sum(wides[:i]) for i in range(len(wides))]

        def put(i, left, rows):
            found = tm(left, rows).astype(F32)
            for g in range(groups):
                v.ups_out[g, :, starts[i] : starts[i] + wides[i]] = found[
                    g * lines : (g + 1) * lines
                ].astype(BF16)

        def put_down(out_ref, short, normed_ref):
            spread = own_columns(short, owner, rank * adapters)
            step = max(share, 128)
            for c in range(model // step):
                found = tm(spread, normed_ref[:, c * step : (c + 1) * step]).astype(BF16)
                for p in range(step // share):
                    out_ref[c * (step // share) + p] = found[:, p * share : (p + 1) * share]

        low_three = need.low_three
        put(3, low_three[:, :space], v.grad_query[...])
        put(4, low_three[:, space:], grad_gate_ref[...])
        put(5, lengthen(v.four_sum[...], owner), need.own_cotangent[...])
        put(7, need.low_four_back[...], mixed_ref[...])
        put_down(v.memory_out, v.three_sum[...], need.normed_rows)
        memory_kept = send_far(1, v.memory_out)
        projected_ref, across_ref, below_ref = need.projected, need.across, need.below
        weight_ref = need.full_in
        for c in attended_sent:
            c.wait()

        @pl.loop(0, width // (2 * HD))
        def _(pair):
            queries, keys, values = [projected_ref[:, wide_lanes(pair, p * width)] for p in range(3)]
            above = jnp.concatenate(
                [v.attended_in[p, :, wide_lanes(pair)] for p in range(ranks)], axis=0
            )
            v.key_sum[...] = jnp.zeros_like(v.key_sum)
            v.value_sum[...] = jnp.zeros_like(v.value_sum)
            for r in range(count // block):
                at, top = slice(r * block, (r + 1) * block), (r + 1) * block
                parts = []
                for h in range(2):
                    lanes = slice(h * HD, (h + 1) * HD)
                    probs = block_probs(
                        queries[:, lanes], keys[:, lanes], across_ref, below_ref, r, block
                    )
                    grad_probs = mt(above[at, lanes], values[:top, lanes])
                    inner = jnp.sum(probs * grad_probs, axis=-1, keepdims=True)
                    grad_scores = (probs * (grad_probs - inner)).astype(BF16)
                    parts.append(mm(grad_scores, keys[:top, lanes]))
                    v.key_sum[h, :top, :] += tm(grad_scores, queries[at, lanes])
                    v.value_sum[h, :top, :] += tm(probs.astype(BF16), above[at, lanes])
                v.grads[at, wide_lanes(pair)] = (
                    jnp.concatenate(parts, axis=1) * HD**-0.5
                ).astype(BF16)
            v.grads[:, wide_lanes(pair, width)] = (
                jnp.concatenate([v.key_sum[0], v.key_sum[1]], axis=1) * HD**-0.5
            ).astype(BF16)
            v.grads[:, wide_lanes(pair, 2 * width)] = jnp.concatenate(
                [v.value_sum[0], v.value_sum[1]], axis=1
            ).astype(BF16)

        input_sent = []
        for d in list(range(1, ranks)) + [0]:
            at = pl.ds(pl.multiple_of(lax.rem(rank + d, ranks) * local, local), local)
            part = mt(v.grads[at, :], weight_ref[...]).astype(BF16)
            if d:
                v.input_out[d] = part
                input_sent.append(near(7, d, v.input_out.at[d], v.input_in.at[rank]))
                input_sent[-1].start()
            else:
                v.input_in[rank] = part
            one = jnp.concatenate(
                [
                    mt(
                        v.grads[at, p * width : (p + 1) * width],
                        ups_ref[:, p * width : (p + 1) * width],
                    )
                    for p in range(3)
                ],
                axis=1,
            )
            v.one_in[rank, :, at] = shorten(masked(one, owner_ref[at, :]))
        one_sent = shared(8, v.one_in)
        for c in one_sent:
            c.start()
        for c in later_sent:
            c.wait()
        low_one = need.low_one
        for p in range(3):
            put(
                p,
                low_one[:, p * space : (p + 1) * space],
                v.grads[:, p * width : (p + 1) * width],
            )
        put(6, lengthen(side_by_side(v.back_in), owner), need.attended[...])
        put(
            8,
            lengthen(side_by_side(need.two_short), owner),
            jnp.concatenate([v.branch_in[p] for p in range(ranks)], axis=0),
        )
        ups_kept = send_far(0, v.ups_out)
        down_input_ref, rows_ref, gain_one = need.down_input, need.inputs, need.gain_one
        normed_one_ref = need.normed_one
        for c in one_sent:
            c.wait()
        v.one_sum[...] = total(v.one_in).astype(BF16)
        put_down(v.down_out, v.one_sum[...], normed_one_ref)
        down_kept = send_far(2, v.down_out)
        for c in input_sent:
            c.wait()
        low = lengthen(v.one_sum[:, own_tokens], owner_own)
        upstream = total(v.input_in) + mt(low, down_input_ref[...])
        v.input_grad[...] = v.grad_middle[...] + rms_backward(
            rows_ref[...].astype(F32), gain_one[...].astype(F32), upstream
        )
        stores.append(pltpu.make_async_copy(v.input_grad, outs[1], saved.at[1]))
        stores[1].start()

        @pl.loop(1, groups)
        def _(d):
            for i, ref in enumerate((v.ups_out, v.memory_out, v.down_out)):
                far_piece(i, d, ref).wait()

        for c in stores + [ups_kept, memory_kept, down_kept]:
            c.wait()

    near_sems = pltpu.SemaphoreType.DMA((9, ranks))
    far_sems = pltpu.SemaphoreType.DMA((3, groups))
    return wides, pl.pallas_call(
        body,
        out_shape=[jax.ShapeDtypeStruct(shape, dtype) for shape, dtype in results],
        in_specs=[ANY] * len(arrays),
        out_specs=[ANY] * len(results),
        scratch_shapes=[pltpu.VMEM(x.shape, x.dtype) for x in inputs]
        + [pltpu.VMEM(shape, dtype) for shape, dtype in vmem.values()]
        + [
            pltpu.SemaphoreType.DMA((len(inputs),)),
            pltpu.SemaphoreType.DMA((5,)),
            near_sems,
            near_sems,
            far_sems,
            far_sems,
        ],
        compiler_params=pltpu.CompilerParams(
            collective_id=cid, has_side_effects=True, vmem_limit_bytes=58 << 20
        ),
    )(*arrays)


def forward(given, table, key_picks, spots, cid, block=128, sub=32, conv=32):
    _, query_spot, gate_spot, attend_spot, mixed_spot, low_spot = spots
    shown = types.SimpleNamespace(**given)
    names = list(given)
    local_arrays = list(given.values())
    ranks, groups = lax.axis_size(TP), lax.axis_size(DP)
    local, model = shown.inputs.shape
    count = shown.owner.shape[0]
    width = shown.gate.shape[1]
    half = shown.keys.shape[2]
    number = key_picks.shape[2]
    picks = key_picks.shape[0] * number
    space = NAD * RANK
    rows = table.shape[0]
    piece = rows // 2
    blocks = 2 * groups
    stride = sub + 1
    chips = groups // 2
    relayed = chips == 4
    hops = max(chips, 4)
    tree = [
        (shown.flat_in, 1),
        (shown.down_input, 2),
        (shown.ups, 2),
        (shown.out_t, 1),
        (shown.attend_t, 2),
        (shown.query, 2),
        (shown.gate, 1),
        (shown.down_memory, 1),
        (shown.mixed_t, 1),
    ]
    early, nested, late = (0, 1, 2), (3, 4), (5, 6, 7, 8)
    cuts = 8
    chunks = tuple(range(len(tree), len(tree) + cuts))
    route = [way for _, way in tree] + [1] * (cuts // 2) + [2] * (cuts // 2)
    tree_shapes = [
        (x.shape[0], x.shape[1] * (ranks if a in nested else 1)) for a, (x, _) in enumerate(tree)
    ]
    full = [((groups, *shape), BF16) for shape in tree_shapes]
    results = dict(
        normed_one=((count, model), BF16),
        low_one=((count, 3 * space), BF16),
        projected=((count, 3 * width), BF16),
        attended=((count, width), BF16),
        middle=((local, model), F32),
        two_short=((ranks, RANK, local), BF16),
        normed_rows=((count, model), BF16),
        low_three=((count, 2 * space), BF16),
        weights=((number, count), F32),
        mixed=((count, width), BF16),
        grad_recalled=((count, width), BF16),
        grad_gate=((count, width), BF16),
        scale=((count, 1), F32),
        low_four_back=((count, space), BF16),
        own_cotangent=((count, width), BF16),
        first=((count, picks), I32),
        second=((count, picks), I32),
    )
    vmem = dict(
        rows_in=((ranks, local, model), BF16),
        cotangent_in=((ranks, local, model), BF16),
        out_stage=(tree_shapes[3], BF16),
        attend_stage=(tree_shapes[4], BF16),
        attended_in=((local, model), BF16),
        normed_two=((local, model), BF16),
        asked=((count, 2 * half), F32),
        every=((NKEYS, count), F32),
        gate_pre=((count, width), F32),
        narrow=((ranks, number, count), BF16),
        grad_mixed=((count, width), F32),
        picks=(key_picks.shape, I32),
        by_token=((count, picks), F32),
        low=((NKEYS * stride, 128), F32),
        high=((NKEYS * stride, 128), F32),
        spread=((2, sub, NKEYS * NKEYS), BF16),
        dense_in=((2, count, piece), BF16),
        table_in=((2, piece, width), BF16),
        total=((count, width), F32),
        largest=((8, 1), F32),
    )
    outs = [
        *full,
        *results.values(),
        ((groups, rows, width), BF16),
        ((count, NKEYS * NKEYS), BF16),
    ]

    def body(*refs):
        inputs = refs[: len(names) + 2]
        out_refs = refs[len(inputs) : len(inputs) + len(outs)]
        rest = list(refs[len(inputs) + len(outs) :])

        def take(n):
            taken = rest[:n]
            del rest[:n]
            return taken

        held = take(len(names))
        gathered = take(len(tree))
        r = types.SimpleNamespace(**dict(zip(results, take(len(results)))))
        v = types.SimpleNamespace(**dict(zip(vmem, take(len(vmem)))))
        loaded, kept, stored, near_send, near_recv, tree_send, tree_recv, pass_send, pass_recv = rest[:9]
        moved = rest[9]
        table_ref, picks_ref = inputs[-2:]
        table_out, dense_out = out_refs[-2:]
        rank, group = lax.axis_index(TP), lax.axis_index(DP)
        barrier = pltpu.get_barrier_semaphore()
        for d in range(1, ranks):
            pl.semaphore_signal(
                barrier,
                inc=1,
                device_id={TP: lax.rem(rank + d, ranks)},
                device_id_type=MESH,
            )

        @pl.loop(1, groups)
        def _(d):
            pl.semaphore_signal(
                barrier,
                inc=1,
                device_id={DP: lax.rem(group + d, groups)},
                device_id_type=MESH,
            )

        loads = [
            pltpu.make_async_copy(inputs[i], held[i], loaded.at[i]) for i in range(len(names))
        ]
        loads.append(pltpu.make_async_copy(picks_ref, v.picks, loaded.at[len(names)]))
        for load in loads:
            load.start()
        need = Waited(names, held, loads)
        raw = types.SimpleNamespace(**dict(zip(names, inputs)))

        def near(i, d, src, dst):
            return pltpu.make_async_remote_copy(
                src_ref=src,
                dst_ref=dst,
                send_sem=near_send.at[i, d],
                recv_sem=near_recv.at[i, d],
                device_id={TP: lax.rem(rank + d, ranks)},
                device_id_type=MESH,
            )

        def columns(ref, p, wide):
            return ref.at[:, pl.ds(pl.multiple_of(p * wide, wide), wide)]

        def cut_of(a):
            return pl.ds((a - len(tree)) * (rows // cuts), rows // cuts)

        def source(a):
            if a in chunks:
                return table_ref.at[cut_of(a)]
            if a in nested:
                return (v.out_stage, v.attend_stage)[a - 3]
            return inputs[names.index(given_names[a])]

        given_names = [names[i] for i in tree_names]

        def place(a, p):
            if a in chunks:
                return table_out.at[p, cut_of(a)]
            return gathered[a].at[p]

        def partner(d):
            if not relayed:
                return lax.rem(group + 2 * d, groups)
            across = 2 - 4 * lax.rem(lax.div(group, 2), 2) if d & 1 else 0
            along = 4 - 8 * lax.div(group, 4) if d & 2 else 0
            return group + across + along

        def holder(d):
            if isinstance(d, int) and d == 0:
                return group
            return partner(d) if relayed else lax.rem(group - 2 * d + groups, groups)

        def to_chip(a, d):
            relay = relayed and d == 3
            shard = place(a, holder(route[a])) if relay else source(a)
            return pltpu.make_async_remote_copy(
                src_ref=shard,
                dst_ref=shard if relay else place(a, group),
                send_sem=tree_send.at[a, d],
                recv_sem=tree_recv.at[a, d],
                device_id={DP: partner(3 - route[a] if relay else d)},
                device_id_type=MESH,
            )

        def to_sibling(a, d):
            first = isinstance(d, int) and d == 0
            return pltpu.make_async_remote_copy(
                src_ref=source(a) if first else place(a, holder(d)),
                dst_ref=place(a, holder(d)),
                send_sem=pass_send.at[a, d],
                recv_sem=pass_recv.at[a, d],
                device_id={DP: group + 1 - 2 * lax.rem(group, 2)},
                device_id_type=MESH,
            )

        def own_copy(a):
            return pltpu.make_async_copy(source(a), place(a, group), kept.at[a])

        def begin(chosen):
            for a in chosen:
                own_copy(a).start()
                if relayed:
                    to_chip(a, 1).start()
                    to_chip(a, 2).start()
                else:

                    @pl.loop(1, chips)
                    def _(d):
                        to_chip(a, d).start()

                to_sibling(a, 0).start()

        def begin_table(chosen):
            if not relayed:
                begin(chosen)
                return
            for a in chosen:
                to_chip(a, route[a]).start()

        def rest_of_table(chosen):
            if relayed:
                for a in chosen:
                    to_chip(a, 3 - route[a]).start()
                for a in chosen:
                    own_copy(a).start()
                    to_sibling(a, 0).start()

        def onward(a, d):
            to_chip(a, d).wait_recv()
            to_sibling(a, d).start()

        def relay(chosen):
            if relayed:
                for a in chosen:
                    onward(a, route[a])
                    to_chip(a, 3).start()

        def other(chosen):
            if relayed:
                for a in chosen:
                    onward(a, 3 - route[a])

        def last(chosen):
            for a in chosen:
                if relayed:
                    onward(a, 3)
                else:

                    @pl.loop(1, chips)
                    def _(d):
                        onward(a, d)

        def settle(chosen):
            for a in chosen:
                own_copy(a).wait()
                to_sibling(a, 0).wait()
                if relayed:
                    for d in range(1, 4):
                        to_sibling(a, d).wait()
                        to_chip(a, d).wait_send()
                else:

                    @pl.loop(1, chips)
                    def _(d):
                        to_sibling(a, d).wait()
                        to_chip(a, d).wait_send()

        stores = []

        def store(src, dst):
            stores.append(pltpu.make_async_copy(src, dst, stored.at[len(stores)]))
            stores[-1].start()

        def store_trees(chosen):
            for a in chosen:
                store(gathered[a], out_refs[a])

        result_refs = dict(zip(results, out_refs[len(tree) :]))

        def flat(ref):
            return ref[...].reshape(-1, ref.shape[2])

        def done(ref):
            for name in results:
                if getattr(r, name) is ref:
                    store(ref, result_refs[name])

        pl.semaphore_wait(barrier, ranks + groups - 2)
        homes = []
        for i, (src, dst) in enumerate(((raw.inputs, v.rows_in), (raw.cotangent, v.cotangent_in))):
            homes.append(pltpu.make_async_copy(src, dst.at[rank], moved.at[i]))
        for i, (src, dst) in enumerate(((raw.out_t, v.out_stage), (raw.attend_t, v.attend_stage))):
            homes.append(
                pltpu.make_async_copy(src, columns(dst, rank, src.shape[1]), moved.at[2 + i])
            )
        for c in homes:
            c.start()
        nest_sent = [
            near(i, d, src, columns(dst, rank, src.shape[1]))
            for i, src, dst in ((0, raw.out_t, v.out_stage), (1, raw.attend_t, v.attend_stage))
            for d in range(1, ranks)
        ]
        rows_sent = [near(2, d, raw.inputs, v.rows_in.at[rank]) for d in range(1, ranks)]
        back_sent = [near(3, d, raw.cotangent, v.cotangent_in.at[rank]) for d in range(1, ranks)]
        for c in nest_sent + rows_sent:
            c.start()
        begin(early)
        for c in nest_sent:
            c.wait()
        homes[2].wait()
        homes[3].wait()
        begin(nested)
        begin(late)
        gain_one, owner_ref = need.gain_one, need.owner
        homes[0].wait()
        for c in rows_sent:
            c.wait()
        for c in range(ranks):
            r.normed_one[c * local : (c + 1) * local, :] = rms_forward(
                v.rows_in[c].astype(F32), gain_one[...].astype(F32)
            ).astype(BF16)
        done(r.normed_one)
        for c in back_sent:
            c.start()
        relay(early)
        other(early)
        relay(nested)
        relay(late)
        last(early)
        begin_table(chunks)
        rest_of_table(chunks)
        settle(early)
        store_trees(early)
        weight_ref, down_ref, ups_ref = gathered[:3]

        def up(spot):
            return ups_ref[:, :, spot].reshape(space, -1)

        @pl.loop(0, ranks)
        def _(c):
            at = pl.ds(pl.multiple_of(c * local, local), local)
            normed = r.normed_one[at, :]
            low = masked(mm(normed, flat(down_ref)), owner_ref[at, :])
            r.low_one[at, :] = low
            for p in range(3):
                lanes = slice(p * width, (p + 1) * width)
                r.projected[at, lanes] = (
                    mm(normed, weight_ref[:, :, lanes].reshape(model, width))
                    + mm(low[:, p * space : (p + 1) * space], up(lanes))
                ).astype(BF16)

        across_ref, below_ref = need.across, need.below

        @pl.loop(0, width // (2 * HD))
        def _(pair):
            queries, keys, values = [r.projected[:, wide_lanes(pair, p * width)] for p in range(3)]
            for q in range(count // block):
                top = (q + 1) * block
                parts = []
                for lanes in (slice(0, HD), slice(HD, 2 * HD)):
                    probs = block_probs(
                        queries[:, lanes], keys[:, lanes], across_ref, below_ref, q, block
                    )
                    parts.append(mm(probs.astype(BF16), values[:top, lanes]))
                r.attended[q * block : top, wide_lanes(pair)] = jnp.concatenate(
                    parts, axis=1
                ).astype(BF16)

        def lines_of(p):
            return r.attended.at[pl.ds(pl.multiple_of(p * local, local), local)]

        attended_sent = [
            near(4, d, lines_of(lax.rem(rank + d, ranks)), columns(v.attended_in, rank, width))
            for d in range(1, ranks)
        ]
        for c in attended_sent:
            c.start()
        own_rows = pl.ds(pl.multiple_of(rank * local, local), local)
        v.attended_in[:, pl.ds(pl.multiple_of(rank * width, width), width)] = r.attended[own_rows, :]
        done(r.low_one)
        done(r.projected)
        done(r.attended)
        other(nested)
        last(nested)
        settle(nested)
        store_trees(nested)
        out_ref, attend_ref = gathered[3:5]
        residual_ref, gain_two, owner_own = need.inputs, need.gain_two, need.owner_own[...]
        for c in attended_sent:
            c.wait()
        low = masked(mt(v.attended_in[...], flat(attend_ref)), owner_own)
        middle = (
            residual_ref[...].astype(F32)
            + mt(v.attended_in[...], flat(out_ref))
            + mm(low, up(attend_spot))
        )
        r.middle[...] = middle
        normed = rms_forward(middle, gain_two[...].astype(F32)).astype(BF16)
        v.normed_two[...] = normed
        r.normed_rows[own_rows, :] = normed
        r.two_short[rank] = shorten(low)
        normed_sent = [
            near(5, d, v.normed_two, r.normed_rows.at[own_rows]) for d in range(1, ranks)
        ] + [near(6, d, r.two_short.at[rank], r.two_short.at[rank]) for d in range(1, ranks)]
        for c in normed_sent:
            c.start()
        done(r.middle)
        loads[-1].wait()
        r.first[...] = jnp.concatenate(
            [v.picks[m, 0] for m in range(key_picks.shape[0])], axis=0
        ).T
        r.second[...] = jnp.concatenate(
            [v.picks[m, 1] for m in range(key_picks.shape[0])], axis=0
        ).T
        done(r.first)
        done(r.second)
        other(late)
        last(late)
        settle(late)
        store_trees(late)
        query_ref, gate_ref, memory_ref, mixed_ref = gathered[5:]
        homes[1].wait()
        for c in back_sent:
            c.wait()
        own_lanes = pl.ds(pl.multiple_of(rank * width, width), width)
        for c in range(ranks):
            at = slice(c * local, (c + 1) * local)
            r.own_cotangent[at, :] = v.cotangent_in[c, :, own_lanes]
            low = masked(mt(v.cotangent_in[c], up(mixed_spot)), owner_ref[at, :])
            r.low_four_back[at, :] = low
            v.grad_mixed[at, :] = mm(v.cotangent_in[c], flat(mixed_ref)) + mm(low, up(low_spot))
        done(r.own_cotangent)
        done(r.low_four_back)
        keys_ref = need.keys
        for c in normed_sent:
            c.wait()
        if relayed:
            for a in chunks:
                onward(a, route[a])
        done(r.normed_rows)
        done(r.two_short)

        @pl.loop(0, ranks)
        def _(c):
            at = pl.ds(pl.multiple_of(c * local, local), local)
            normed = r.normed_rows[at, :]
            low = masked(mm(normed, flat(memory_ref)), owner_ref[at, :])
            r.low_three[at, :] = low
            v.asked[at, :] = mm(normed, flat(query_ref)) + mm(low[:, :space], up(query_spot))
            v.gate_pre[at, :] = mm(normed, flat(gate_ref)) + mm(low[:, space:], up(gate_spot))

        done(r.low_three)
        slot = lax.broadcasted_iota(I32, (NKEYS, block), 0)
        for part in range(2):
            top, low = two_parts(v.asked[:, part * half : (part + 1) * half])
            v.every[...] = mt(keys_ref[part], top) + mt(keys_ref[part], low)

            @pl.loop(0, count // block)
            def _(c):
                lanes = pl.ds(pl.multiple_of(c * block, block), block)
                scores = v.every[:, lanes]
                found = []
                for k in range(number):
                    hit = slot == v.picks[rank, part, k : k + 1, lanes]
                    found.append(jnp.sum(jnp.where(hit, scores, 0.0), axis=0, keepdims=True))
                found = jnp.concatenate(found, axis=0)
                if part == 0:
                    r.weights[:, lanes] = found
                else:
                    added = (r.weights[:, lanes] + found) * (2 * half) ** -0.5
                    raised = jnp.exp(added - jnp.max(added, axis=0, keepdims=True))
                    weights = raised / jnp.sum(raised, axis=0, keepdims=True)
                    r.weights[:, lanes] = weights
                    v.narrow[rank, :, lanes] = weights.astype(BF16)

        narrow_sent = [
            near(7, d, v.narrow.at[rank], v.narrow.at[rank]) for d in range(1, ranks)
        ]
        for c in narrow_sent:
            c.start()
        done(r.weights)
        for c in narrow_sent:
            c.wait()
        v.by_token[...] = (
            jnp.concatenate([v.narrow[p] for p in range(ranks)], axis=0).astype(F32).T
        )

        wide_slot = lax.broadcasted_iota(I32, (NKEYS, picks), 0)
        steps = count // sub

        def spread_out(t, s):
            return pltpu.make_async_copy(
                v.spread.at[s],
                dense_out.at[pl.ds(pl.multiple_of(t * sub, sub), sub)],
                moved.at[4 + s],
            )

        @pl.loop(0, steps)
        def _(t):
            s = lax.rem(t, 2)
            at = pl.ds(pl.multiple_of(t * sub, sub), sub)
            firsts, seconds, weights = r.first[at, :], r.second[at, :], v.by_token[at, :]
            for n in range(sub):
                b = jnp.where(wide_slot == seconds[n : n + 1], 1.0, 0.0).astype(BF16)
                a = jnp.where(wide_slot == firsts[n : n + 1], weights[n : n + 1], 0.0).astype(BF16)
                both = mt(a, b)
                v.low[pl.ds(n, NKEYS, stride=stride), :] = both[:, :128]
                v.high[pl.ds(n, NKEYS, stride=stride), :] = both[:, 128:]

            @pl.when(t >= 2)
            def _():
                spread_out(t - 2, s).wait()

            @pl.loop(0, NKEYS // conv)
            def _(c):
                for q in range(conv):
                    i = c * conv + q
                    lanes = pl.multiple_of(i * NKEYS, NKEYS)
                    lines = pl.ds(i * stride, sub)
                    v.spread[s, :, pl.ds(lanes, 128)] = v.low[lines, :].astype(BF16)
                    v.spread[s, :, pl.ds(lanes + 128, 128)] = v.high[lines, :].astype(BF16)

            spread_out(t, s).start()

            @pl.when(t == steps - 9)
            def _():
                other(chunks)
                if relayed:
                    for a in chunks:
                        to_chip(a, 3).start()

        spread_out(steps - 2, steps % 2).wait()
        spread_out(steps - 1, (steps - 1) % 2).wait()

        def block_at(b):
            if not relayed:
                return lax.div(b, 2), lax.rem(b, 2)
            d = lax.div(b, 4)
            across = (2 - 4 * lax.rem(lax.div(group, 2), 2)) * lax.rem(d, 2)
            along = (4 - 8 * lax.div(group, 4)) * lax.div(d, 2)
            near_by = (1 - 2 * lax.rem(group, 2)) * lax.rem(lax.div(b, 2), 2)
            return group + across + along + near_by, lax.rem(b, 2)

        def fetch(b, s):
            p, h = block_at(b)
            return (
                pltpu.make_async_copy(
                    dense_out.at[:, pl.ds(pl.multiple_of((p * 2 + h) * piece, piece), piece)],
                    v.dense_in.at[s],
                    moved.at[6 + s],
                ),
                pltpu.make_async_copy(
                    table_out.at[p, pl.ds(pl.multiple_of(h * piece, piece), piece)],
                    v.table_in.at[s],
                    moved.at[8 + s],
                ),
            )

        def arrived(d):
            for a in chunks:
                if isinstance(d, int) and d == 0:
                    own_copy(a).wait()
                to_sibling(a, d).wait_recv()

        arrived(0)
        if relayed:
            arrived(1)
            arrived(2)
        else:
            last(chunks)

            @pl.loop(1, chips)
            def _(d):
                arrived(d)

        v.total[...] = jnp.zeros_like(v.total)
        v.largest[...] = jnp.zeros_like(v.largest)
        for c in fetch(0, 0):
            c.start()

        @pl.loop(0, blocks)
        def _(b):
            s = lax.rem(b, 2)
            if relayed:

                @pl.when(b == 7)
                def _():
                    last(chunks)

                @pl.when(b == 11)
                def _():
                    arrived(3)

            @pl.when(b + 1 < blocks)
            def _():
                for c in fetch(b + 1, 1 - s):
                    c.start()

            for c in fetch(b, s):
                c.wait()
            v.total[...] += mm(v.dense_in[s], v.table_in[s])
            peak = v.largest[...]
            for c in range(piece // 512):
                values = v.table_in[s, c * 512 : (c + 1) * 512, :].astype(F32)
                squares = values * values
                norms = jnp.sum(squares[:, :128] + squares[:, 128:], axis=1, keepdims=True)
                peak = jnp.maximum(peak, jnp.max(norms.reshape(-1, 8, 1), axis=0))
            v.largest[...] = peak

        gate, recalled, upstream = v.gate_pre[...], v.total[...], v.grad_mixed[...]
        sigmoid = 1.0 / (1.0 + jnp.exp(-gate))
        act = gate * sigmoid
        r.mixed[...] = (act * recalled).astype(BF16)
        grad = (upstream * act).astype(BF16)
        r.grad_recalled[...] = grad
        r.grad_gate[...] = (
            upstream * recalled * sigmoid * (1.0 + gate * (1.0 - sigmoid))
        ).astype(BF16)
        wide = grad.astype(F32)
        bound = jnp.max(v.largest[...]) * jnp.sum(wide * wide, axis=1, keepdims=True)
        r.scale[...] = 32000.0 * lax.rsqrt(jnp.maximum(bound, 1e-30))
        for ref in (r.mixed, r.grad_recalled, r.grad_gate, r.scale):
            done(ref)
        for a in chunks:
            for d in range(4 if relayed else 1):
                to_sibling(a, d).wait_send()
            if relayed:
                for d in range(1, 4):
                    to_chip(a, d).wait_send()
            else:

                @pl.loop(1, chips)
                def _(d):
                    to_sibling(a, d).wait_send()
                    to_chip(a, d).wait_send()

        for name in names:
            getattr(need, name)
        for c in stores:
            c.wait()

    tree_names = [
        next(i for i, y in enumerate(local_arrays) if y is x) for x, _ in tree
    ]
    arrays = [*local_arrays, table, key_picks]
    near_sems = pltpu.SemaphoreType.DMA((8, ranks))
    tree_sems = pltpu.SemaphoreType.DMA((len(route), hops))
    got = pl.pallas_call(
        body,
        out_shape=[jax.ShapeDtypeStruct(shape, dtype) for shape, dtype in outs],
        in_specs=[ANY] * len(arrays),
        out_specs=[ANY] * len(outs),
        scratch_shapes=[pltpu.VMEM(x.shape, x.dtype) for x in local_arrays]
        + [pltpu.VMEM(shape, dtype) for shape, dtype in full]
        + [pltpu.VMEM(shape, dtype) for shape, dtype in results.values()]
        + [pltpu.VMEM(shape, dtype) for shape, dtype in vmem.values()]
        + [
            pltpu.SemaphoreType.DMA((len(names) + 1,)),
            pltpu.SemaphoreType.DMA((len(route),)),
            pltpu.SemaphoreType.DMA((len(outs),)),
            near_sems,
            near_sems,
            tree_sems,
            tree_sems,
            tree_sems,
            tree_sems,
            pltpu.SemaphoreType.DMA((10,)),
        ],
        compiler_params=pltpu.CompilerParams(
            collective_id=cid, has_side_effects=True, vmem_limit_bytes=61 << 20
        ),
    )(*arrays)
    whole_arrays = [x.reshape(-1, x.shape[2]) for x in got[: len(tree)]]
    return whole_arrays, types.SimpleNamespace(**dict(zip(results, got[len(tree) :]))), got[-2]


def pick_grads(first, second, grads, scale, table):
    tokens, picks = first.shape
    width = grads.shape[1]
    per_block = 16
    rows = per_block * NKEYS
    blocks = table.shape[0] // rows

    def body(first_ref, second_ref, grads_ref, scale_ref, table_ref, out_ref, kept):
        step = pl.program_id(0)

        @pl.when(step == 0)
        def _():
            kept[...] = jnp.zeros_like(kept)

        own = first_ref[...]
        low = second_ref[...] & 127
        factor = jnp.broadcast_to(scale_ref[...], (tokens, 128))
        total = kept[...]
        for b in range(per_block):
            every = mt(grads_ref[...], table_ref[b * NKEYS : (b + 1) * NKEYS, :])
            packed = (every[:, 128:] * factor).astype(I32) * 65536 + (
                every[:, :128] * factor
            ).astype(I32)
            found = jnp.take_along_axis(packed, low, axis=1, mode="promise_in_bounds")
            total = jnp.where(own == step * per_block + b, found, total)
        kept[...] = total

        @pl.when(step == blocks - 1)
        def _():
            p = kept[...]
            right = lax.shift_right_arithmetic(lax.shift_left(p, 16), 16)
            left = lax.shift_right_arithmetic(p - right, 16)
            both = jnp.where(second_ref[...] >= 128, left, right).astype(F32) / factor
            out_ref[...] = both.T.astype(BF16)

    return pl.pallas_call(
        body,
        grid=(blocks,),
        out_shape=jax.ShapeDtypeStruct((picks, tokens), BF16),
        in_specs=[whole(x.shape) for x in (first, second, grads, scale)]
        + [pl.BlockSpec((rows, width), lambda s: (s, 0))],
        out_specs=whole((picks, tokens)),
        scratch_shapes=[pltpu.VMEM((tokens, picks), I32)],
        compiler_params=pltpu.CompilerParams(vmem_limit_bytes=48 << 20),
    )(first, second, grads, scale, table)


def by_part(down, parts):
    shaped = down.reshape(down.shape[0], NAD, parts, RANK).transpose(0, 2, 1, 3)
    return shaped.reshape(down.shape)


def add_up(inputs, plans):
    shapes = []
    for x, (axis, sizes) in zip(inputs, plans):
        for size in sizes:
            if isinstance(size, tuple):
                shapes.append((size[0], x.shape[1], size[1]))
            else:
                shapes.append((x.shape[1], size) if axis else (size, x.shape[2]))

    def body(*refs):
        outs = iter(refs[len(inputs) :])
        for ref, (axis, sizes) in zip(refs, plans):

            def total(start, size):
                cut = slice(start, start + size)
                return sum(
                    (ref[p, :, cut] if axis else ref[p, cut, :]).astype(F32)
                    for p in range(ref.shape[0])
                )

            at = 0
            for size in sizes:
                out = next(outs)
                if isinstance(size, tuple):
                    for q in range(size[0]):
                        out[q] = total(at, size[1])
                        at += size[1]
                else:
                    out[...] = total(at, size)
                    at += size

    return stage(body, [(shape, F32) for shape in shapes], inputs)


def make_ready(segments, adapters, project_in, down_input, down_memory, turned, joined, local):
    count = segments.shape[1]
    parts, lines, width = project_in.shape

    def body(segments_ref, adapters_ref, project_ref, input_ref, memory_ref, *refs):
        ins, outs = refs[: len(turned) + len(joined)], refs[len(turned) + len(joined) :]

        def ordered(ref, parts):
            size = NAD * parts * RANK
            row = lax.broadcasted_iota(I32, (size, size), 0)
            column = lax.broadcasted_iota(I32, (size, size), 1)
            part, rest = lax.div(column, NAD * RANK), lax.rem(column, NAD * RANK)
            adapter, rank = lax.div(rest, RANK), lax.rem(rest, RANK)
            came = adapter * (parts * RANK) + part * RANK + rank
            return mm(ref[...], jnp.where(row == came, 1.0, 0.0).astype(BF16)).astype(BF16)

        for p in range(parts):
            outs[0][:, p * width : (p + 1) * width] = project_ref[p]
        outs[1][...] = ordered(input_ref, 3)
        outs[2][...] = ordered(memory_ref, 2)
        for p in range(parts):
            outs[3][:, p * width : (p + 1) * width] = ins[len(turned)][p]
        at = parts * width
        for ref in ins[len(turned) + 1 :]:
            outs[3][:, at : at + ref.shape[1]] = ref[...]
            at += ref.shape[1]
        for ref, out in zip(ins[: len(turned)], outs[4:]):
            out[...] = ref[...].astype(F32).T.astype(BF16)
        owner_ref, below_ref, owner_own_ref = outs[-3:]
        across = jnp.broadcast_to(segments_ref[...], (8, count))
        owner = jnp.zeros_like(across)
        for s in range(adapters.shape[1]):
            owner = jnp.where(across == s, adapters_ref[0:1, s : s + 1], owner)
        owner_ref[...] = owner.T[:, 0:1]
        below_ref[...] = across.T[:, 0:1]
        own = pl.ds(pl.multiple_of(lax.axis_index(TP) * local, local), local)
        owner_own_ref[...] = owner_ref[own, :]

    small = parts * width + sum(x.shape[1] for x in joined[1:])
    return stage(
        body,
        [
            ((lines, parts * width), BF16),
            (down_input.shape, BF16),
            (down_memory.shape, BF16),
            ((joined[1].shape[0], small), BF16),
        ]
        + [(x.shape[::-1], BF16) for x in turned]
        + [((count, 1), I32), ((count, 1), I32), ((local, 1), I32)],
        (segments, adapters, project_in, down_input, down_memory, *turned, *joined),
    )


def on_device(
    inputs,
    cotangent,
    norm_attend,
    norm_memory,
    project_in,
    project_out,
    query_weight,
    gate_weight,
    memory_out,
    half_keys,
    value_table,
    key_picks,
    segment_ids,
    adapter_ids,
    down_input,
    up_input,
    down_attend,
    up_attend,
    down_memory,
    up_query,
    up_gate,
    down_mixed,
    up_mixed,
):
    groups = lax.axis_size(DP)
    ranks = lax.axis_size(TP)
    rank = lax.axis_index(TP)
    local = inputs.shape[0]
    count = segment_ids.shape[0]
    width = project_in.shape[2]
    model = inputs.shape[1]

    across = segment_ids[None, :]
    attend_turned = down_attend.T
    joined = (up_input.transpose(1, 0, 2), up_query, up_gate, up_attend, up_mixed, down_mixed.T)
    turned = (project_out, memory_out)
    if project_out.shape[1] % 128 == 0:
        ready = make_ready(
            across,
            adapter_ids,
            project_in.transpose(1, 0, 2),
            down_input,
            down_memory,
            turned,
            joined,
            local,
        )
        flat_in, parted_input, parted_memory, small, out_turned, mixed_turned = ready[:6]
        owner, below, owner_own = ready[6:]
    else:
        flat_in = project_in.reshape(project_in.shape[0], 3 * width)
        parted_input, parted_memory = by_part(down_input, 3), by_part(down_memory, 2)
        out_turned, mixed_turned = [x.T for x in turned]
        small = jnp.concatenate((up_input.reshape(-1, 3 * width),) + joined[1:], axis=1)
        below = segment_ids[:, None]
        owner = jnp.zeros_like(below)
        for s in range(adapter_ids.shape[1]):
            owner = jnp.where(below == s, adapter_ids[0, s], owner)
        owner_own = lax.dynamic_slice_in_dim(owner, rank * local, local, 0)
    spots, at = [], 0
    for size in (3 * width, up_query.shape[1], width, model, model, width):
        spots.append(slice(at, at + size))
        at += size
    gain_one, gain_two, keys = norm_attend[None, :], norm_memory[None, :], half_keys[0]
    (
        (
            full_in,
            full_down_input,
            ups,
            out_t,
            attend_t,
            full_query,
            full_gate,
            full_down_memory,
            mixed_t,
        ),
        kept,
        table,
    ) = forward(
        dict(
            flat_in=flat_in,
            down_input=parted_input,
            ups=small,
            out_t=out_turned,
            attend_t=attend_turned,
            query=query_weight,
            gate=gate_weight,
            down_memory=parted_memory,
            mixed_t=mixed_turned,
            inputs=inputs,
            cotangent=cotangent,
            gain_one=gain_one,
            gain_two=gain_two,
            owner=owner,
            owner_own=owner_own,
            across=across,
            below=below,
            keys=keys,
        ),
        value_table,
        key_picks,
        spots,
        1,
    )
    mixed = kept.mixed
    partial_mixed = mt(mixed, mixed_t).astype(BF16).reshape(ranks, local, model)

    def block_of(blocks, d):
        return lax.dynamic_index_in_dim(blocks, lax.rem(rank + d, ranks), 0, keepdims=False)

    def turn(d):
        return [(p, (p + d) % ranks) for p in range(ranks)]

    mixed_parts = [block_of(partial_mixed, 0)] + [
        lax.ppermute(block_of(partial_mixed, d), TP, turn(d)) for d in range(1, ranks)
    ]
    picked = pick_grads(
        kept.first, kept.second, kept.grad_recalled, kept.scale, table.reshape(-1, width)
    )
    picked, mixed_parts = lax.optimization_barrier((picked, mixed_parts))
    given = dict(
        picked=picked.reshape(ranks, -1, count),
        weights=kept.weights,
        keys=keys,
        picks=lax.dynamic_index_in_dim(key_picks, rank, 0, keepdims=False),
        query=full_query,
        gate=full_gate,
        ups=ups,
        grad_gate=kept.grad_gate,
        mixed=mixed,
        owner=owner,
        owner_own=owner_own,
        middle=kept.middle,
        cotangent=cotangent,
        gain_two=gain_two,
        down_memory=full_down_memory,
        out_t=out_t,
        attend_t=attend_t,
        low_three=kept.low_three,
        own_cotangent=kept.own_cotangent,
        low_four_back=kept.low_four_back,
        normed_rows=kept.normed_rows,
        projected=kept.projected,
        across=across,
        below=below,
        full_in=full_in,
        low_one=kept.low_one,
        attended=kept.attended,
        two_short=kept.two_short,
        down_input=full_down_input,
        inputs=inputs,
        gain_one=gain_one,
        normed_one=kept.normed_one,
    )
    wides, (outputs, input_grad, up_parts, memory_parts, down_parts) = backward(
        given, mixed_parts, spots, 5
    )
    (
        grad_up_input,
        grad_up_query,
        grad_up_gate,
        grad_up_mixed,
        grad_down_attend,
        grad_down_mixed,
        grad_up_attend,
        grad_down_memory,
        grad_down_input,
    ) = add_up(
        (up_parts, memory_parts, down_parts),
        (
            (1, ((3, width), *wides[3:])),
            (0, (memory_parts.shape[1],)),
            (0, (down_parts.shape[1],)),
        ),
    )
    return (
        outputs,
        input_grad,
        grad_down_input.T,
        grad_up_input.transpose(1, 0, 2),
        grad_down_attend.T,
        grad_up_attend,
        grad_down_memory.T,
        grad_up_query,
        grad_up_gate,
        grad_down_mixed.T,
        grad_up_mixed,
    )


def solution(mesh):
    rows = P((DP, TP), None)
    both = P(DP, TP)
    wide = P(DP, None)
    turned = P(TP, DP)
    split = P(DP, None, TP)
    return jax.shard_map(
        on_device,
        mesh=mesh,
        in_specs=(
            rows,
            rows,
            P(),
            P(),
            split,
            turned,
            both,
            both,
            turned,
            P(TP, None, None, None),
            both,
            P(None, None, None, DP),
            P(DP),
            wide,
            wide,
            split,
            turned,
            wide,
            wide,
            both,
            both,
            turned,
            wide,
        ),
        out_specs=(rows, rows, both, split, turned, both, both, both, both, turned, both),
        check_vma=False,
    )
```

```python
import types

import jax
import jax.numpy as jnp
from jax import lax
from jax.experimental import pallas as pl
from jax.experimental.pallas import tpu as pltpu
from jax.sharding import PartitionSpec as P

DP, TP = "dp", "tensor"
HD = 64
NKEYS = 256
RANK = 16
NAD = 8
EPS = 1e-06
NEGATIVE = -1e30
F32, BF16, I32 = jnp.float32, jnp.bfloat16, jnp.int32
MESH = pl.DeviceIdType.MESH
ANY = pl.BlockSpec(memory_space=pl.ANY)


def mm(a, b):
    return lax.dot_general(a, b, (((1,), (0,)), ((), ())), preferred_element_type=F32)


def mt(a, b):
    return lax.dot_general(a, b, (((1,), (1,)), ((), ())), preferred_element_type=F32)


def tm(a, b):
    return lax.dot_general(a, b, (((0,), (0,)), ((), ())), preferred_element_type=F32)


def two_parts(x):
    top = x.astype(BF16)
    return top, (x - top.astype(F32)).astype(BF16)


def whole(shape):
    return pl.BlockSpec(shape, lambda *_: (0,) * len(shape))


def stage(body, outs, ins, scratch=(), limit=61):
    return pl.pallas_call(
        body,
        grid=(1,),
        out_shape=[jax.ShapeDtypeStruct(shape, dtype) for shape, dtype in outs],
        in_specs=[whole(x.shape) for x in ins],
        out_specs=[whole(shape) for shape, _ in outs],
        scratch_shapes=list(scratch),
        compiler_params=pltpu.CompilerParams(vmem_limit_bytes=limit << 20),
    )(*ins)


def rms_forward(values, gain):
    factor = lax.rsqrt(jnp.mean(values * values, axis=-1, keepdims=True) + EPS)
    return values * factor * gain


def rms_backward(values, gain, upstream):
    factor = lax.rsqrt(jnp.mean(values * values, axis=-1, keepdims=True) + EPS)
    scaled = upstream * gain
    return factor * scaled - values * (factor * factor * factor) * jnp.mean(
        values * scaled, axis=-1, keepdims=True
    )


def masked(values, owner):
    columns = lax.broadcasted_iota(I32, values.shape, 1)
    adapter = lax.rem(lax.div(columns, RANK), NAD)
    return jnp.where(adapter == owner, values, 0.0).astype(BF16)


def folding(parts):
    shape = (parts * RANK, parts * NAD * RANK)
    short = lax.broadcasted_iota(I32, shape, 0)
    column = lax.broadcasted_iota(I32, shape, 1)
    same = (lax.div(short, RANK) == lax.div(column, NAD * RANK)) & (
        lax.rem(short, RANK) == lax.rem(column, RANK)
    )
    return jnp.where(same, 1.0, 0.0).astype(BF16)


def shorten(values):
    return mt(folding(values.shape[1] // (NAD * RANK)), values).astype(BF16)


def lengthen(short, owner):
    return masked(tm(short, folding(short.shape[0] // RANK)), owner)


def side_by_side(blocks):
    return jnp.concatenate([blocks[p] for p in range(blocks.shape[0])], axis=1)


def block_probs(queries, keys, across_ref, down_ref, r, block):
    top = (r + 1) * block
    at = slice(r * block, top)
    scores = mt(queries[at], keys[:top]) * HD**-0.5
    place = lax.broadcasted_iota(I32, (block, top), 0) + r * block
    other = lax.broadcasted_iota(I32, (block, top), 1)
    ahead = across_ref[:, :top]
    seen = (other <= place) & ((ahead == 0) | (ahead == down_ref[at, :]))
    scores = jnp.where(seen, scores, NEGATIVE)
    raised = jnp.exp(scores - jnp.max(scores, axis=-1, keepdims=True))
    return raised / jnp.sum(raised, axis=-1, keepdims=True)


def wide_lanes(pair, base=0):
    return pl.ds(pl.multiple_of(base + pair * 2 * HD, 2 * HD), 2 * HD)


def own_columns(short, owner, first):
    high, count = short.shape
    adapters = NAD // lax.axis_size(TP)
    pattern = lax.broadcasted_iota(I32, (high, adapters * high), 0) == lax.rem(
        lax.broadcasted_iota(I32, (high, adapters * high), 1), high
    )
    spread = tm(short, jnp.where(pattern, 1.0, 0.0).astype(BF16))
    adapter = lax.div(lax.broadcasted_iota(I32, (count, adapters * high), 1), high) + first
    return jnp.where(adapter == owner, spread, 0.0).astype(BF16)


class Waited:
    def __init__(self, names, refs, loads):
        self._pending = dict(zip(names, zip(refs, loads)))

    def __getattr__(self, name):
        ref, load = self._pending[name]
        load.wait()
        setattr(self, name, ref)
        return ref


def backward(given, mixed_parts, ups_spots, cid, block=128):
    _, query_spot, gate_spot, attend_spot, mixed_spot, low_spot = ups_spots
    shown = types.SimpleNamespace(**given)
    picked = given.pop(next(iter(given)))
    names = list(given)
    arrays = [picked, *given.values(), *mixed_parts]
    ranks, groups = lax.axis_size(TP), lax.axis_size(DP)
    count, width = shown.attended.shape
    local, model = shown.inputs.shape
    number = shown.weights.shape[0]
    half = shown.keys.shape[2]
    space = NAD * RANK
    adapters = NAD // ranks
    lines, share = space // groups, model // groups
    wides = [width] * 3 + [2 * half] + [width] * 5
    tall = [adapters * 2 * RANK, adapters * 3 * RANK]
    vmem = dict(
        pick_in=((ranks, number, count), BF16),
        dense=((NKEYS, count), F32),
        grad_query=((count, 2 * half), BF16),
        normed_out=((ranks, local, model), BF16),
        normed_in=((ranks, local, model), BF16),
        three_in=((ranks, 2 * RANK, count), BF16),
        four_in=((ranks, RANK, count), BF16),
        three_sum=((2 * RANK, count), BF16),
        four_sum=((RANK, count), BF16),
        attended_out=((local, model), BF16),
        attended_in=((ranks, local, width), BF16),
        branch_out=((local, model), BF16),
        branch_in=((ranks, local, width), BF16),
        back_in=((ranks, RANK, local), BF16),
        grad_middle=((local, model), F32),
        grads=((count, 3 * width), BF16),
        key_sum=((2, count, HD), F32),
        value_sum=((2, count, HD), F32),
        input_out=((ranks, local, model), BF16),
        input_in=((ranks, local, model), BF16),
        one_in=((ranks, 3 * RANK, count), BF16),
        one_sum=((3 * RANK, count), BF16),
        ups_out=((groups, lines, sum(wides)), BF16),
        memory_out=((groups, tall[0], share), BF16),
        down_out=((groups, tall[1], share), BF16),
        outputs=((local, model), BF16),
        input_grad=((local, model), F32),
    )
    inputs = arrays[1:]
    results = [
        ((local, model), BF16),
        ((local, model), F32),
        ((groups, lines, sum(wides)), BF16),
        ((groups, tall[0], share), BF16),
        ((groups, tall[1], share), BF16),
    ]

    def body(*refs):
        outs = refs[len(arrays) : len(arrays) + len(results)]
        rest = refs[len(arrays) + len(results) :]
        v = types.SimpleNamespace(**dict(zip(vmem, rest[len(inputs) :])))
        loaded, saved, send, recv, far_send, far_recv = rest[len(inputs) + len(vmem) :]
        rank, group = lax.axis_index(TP), lax.axis_index(DP)
        barrier = pltpu.get_barrier_semaphore()
        for d in range(1, ranks):
            pl.semaphore_signal(
                barrier,
                inc=1,
                device_id={TP: lax.rem(rank + d, ranks)},
                device_id_type=MESH,
            )

        @pl.loop(1, groups)
        def _(d):
            pl.semaphore_signal(
                barrier,
                inc=1,
                device_id={DP: lax.rem(group + d, groups)},
                device_id_type=MESH,
            )

        loads = [
            pltpu.make_async_copy(
                refs[i + 1].at[rank] if x is shown.picks else refs[i + 1], rest[i], loaded.at[i]
            )
            for i, x in enumerate(inputs)
        ]
        for load in loads:
            load.start()
        need = Waited(names, rest, loads)

        def near(i, d, src, dst):
            return pltpu.make_async_remote_copy(
                src_ref=src,
                dst_ref=dst,
                send_sem=send.at[i, d],
                recv_sem=recv.at[i, d],
                device_id={TP: lax.rem(rank + d, ranks)},
                device_id_type=MESH,
            )

        def far(i, d, src, dst):
            return pltpu.make_async_remote_copy(
                src_ref=src,
                dst_ref=dst,
                send_sem=far_send.at[i, d],
                recv_sem=far_recv.at[i, d],
                device_id={DP: lax.rem(group + d, groups)},
                device_id_type=MESH,
            )

        def far_piece(i, d, ref):
            return far(i, d, ref.at[lax.rem(group + d, groups)], outs[2 + i].at[group])

        def send_far(i, ref):
            @pl.loop(1, groups)
            def _(d):
                far_piece(i, d, ref).start()

            keep = pltpu.make_async_copy(ref.at[group], outs[2 + i].at[group], saved.at[2 + i])
            keep.start()
            return keep

        def shared(i, ref):
            return [near(i, d, ref.at[rank], ref.at[rank]) for d in range(1, ranks)]

        def columns(ref, p):
            return ref.at[:, pl.ds(pl.multiple_of(p * width, width), width)]

        def split(i, src, dst):
            return [
                near(i, d, columns(src, lax.rem(rank + d, ranks)), dst.at[rank])
                for d in range(1, ranks)
            ]

        def total(ref):
            return sum(ref[p].astype(F32) for p in range(ranks))

        own_tokens = pl.ds(pl.multiple_of(rank * local, local), local)
        own_columns_at = pl.ds(pl.multiple_of(rank * width, width), width)

        pick_in = v.pick_in
        own_pick = pltpu.make_async_copy(refs[0].at[rank], pick_in.at[rank], saved.at[0])
        own_pick.start()
        pl.semaphore_wait(barrier, ranks + groups - 2)
        picks_sent = [
            near(0, d, refs[0].at[lax.rem(rank + d, ranks)], pick_in.at[rank])
            for d in range(1, ranks)
        ]
        for c in picks_sent:
            c.start()
        weights_ref, keys_ref, picks_ref = need.weights, need.keys, need.picks
        own_pick.wait()
        for c in picks_sent:
            c.wait()

        slot = lax.broadcasted_iota(I32, (NKEYS, block), 0)
        for part in range(2):

            @pl.loop(0, count // block)
            def _(c):
                lanes = pl.ds(pl.multiple_of(c * block, block), block)
                weight = weights_ref[:, lanes]
                grad = sum(pick_in[p, :, lanes].astype(F32) for p in range(ranks))
                grad = weight * (grad - jnp.sum(grad * weight, axis=0, keepdims=True))
                grad = grad * (2 * half) ** -0.5
                dense = jnp.zeros((NKEYS, block), F32)
                for k in range(number):
                    hit = slot == picks_ref[part, k : k + 1, lanes]
                    dense += jnp.where(hit, grad[k : k + 1, :], 0.0)
                v.dense[:, lanes] = dense

            top, low = two_parts(v.dense[...])
            v.grad_query[:, part * half : (part + 1) * half] = (
                tm(top, keys_ref[part]) + tm(low, keys_ref[part])
            ).astype(BF16)

        query_ref, gate_ref, ups_ref = need.query, need.gate, need.ups
        grad_gate_ref, mixed_ref, owner_ref = need.grad_gate, need.mixed, need.owner
        normed_sent = []
        for d in list(range(1, ranks)) + [0]:
            at = pl.ds(pl.multiple_of(lax.rem(rank + d, ranks) * local, local), local)
            asked, gates, own = v.grad_query[at, :], grad_gate_ref[at, :], owner_ref[at, :]
            part = (mt(asked, query_ref[...]) + mt(gates, gate_ref[...])).astype(BF16)
            if d:
                v.normed_out[d] = part
                normed_sent.append(near(1, d, v.normed_out.at[d], v.normed_in.at[rank]))
                normed_sent[-1].start()
            else:
                v.normed_in[rank] = part
            three = jnp.concatenate(
                [mt(asked, ups_ref[:, query_spot]), mt(gates, ups_ref[:, gate_spot])], axis=1
            )
            v.three_in[rank, :, at] = shorten(masked(three, own))
            v.four_in[rank, :, at] = shorten(
                masked(mt(mixed_ref[at, :], ups_ref[:, low_spot]), own)
            )
        short_sent = shared(2, v.three_in) + shared(3, v.four_in)
        for c in short_sent:
            c.start()
        owner_own = need.owner_own[...]
        middle_ref, cotangent_ref, gain_two = need.middle, need.cotangent, need.gain_two
        down_ref, out_ref, attend_ref = need.down_memory, need.out_t, need.attend_t
        mixed_refs = []
        for i in range(len(names), len(inputs)):
            loads[i].wait()
            mixed_refs.append(rest[i])
        for c in normed_sent + short_sent:
            c.wait()

        v.three_sum[...] = total(v.three_in).astype(BF16)
        v.four_sum[...] = total(v.four_in).astype(BF16)
        grad_three = lengthen(v.three_sum[:, own_tokens], owner_own)
        upstream = total(v.normed_in) + mt(grad_three, down_ref[...])
        grad = cotangent_ref[...].astype(F32) + rms_backward(
            middle_ref[...], gain_two[...].astype(F32)[None, :], upstream
        )
        v.grad_middle[...] = grad
        branch = grad.astype(BF16)
        v.branch_out[...] = branch
        low = masked(mt(branch, ups_ref[:, attend_spot]), owner_own)
        v.attended_out[...] = (mm(branch, out_ref[...]) + mm(low, attend_ref[...])).astype(BF16)
        v.back_in[rank] = shorten(low)
        v.attended_in[rank] = v.attended_out[:, own_columns_at]
        v.branch_in[rank] = v.branch_out[:, own_columns_at]
        attended_sent = split(4, v.attended_out, v.attended_in)
        later_sent = shared(5, v.back_in) + split(6, v.branch_out, v.branch_in)
        for c in attended_sent + later_sent:
            c.start()

        low_four = lengthen(v.four_sum[:, own_tokens], owner_own)
        v.outputs[...] = (
            middle_ref[...]
            + sum(ref[...].astype(F32) for ref in mixed_refs)
            + mm(low_four, ups_ref[:, mixed_spot])
        ).astype(BF16)
        stores = [pltpu.make_async_copy(v.outputs, outs[0], saved.at[0])]
        stores[0].start()
        owner = owner_ref[...]
        starts = [sum(wides[:i]) for i in range(len(wides))]

        def put(i, left, rows):
            found = tm(left, rows).astype(F32)
            for g in range(groups):
                v.ups_out[g, :, starts[i] : starts[i] + wides[i]] = found[
                    g * lines : (g + 1) * lines
                ].astype(BF16)

        def put_down(out_ref, short, normed_ref):
            spread = own_columns(short, owner, rank * adapters)
            step = max(share, 128)
            for c in range(model // step):
                found = tm(spread, normed_ref[:, c * step : (c + 1) * step]).astype(BF16)
                for p in range(step // share):
                    out_ref[c * (step // share) + p] = found[:, p * share : (p + 1) * share]

        low_three = need.low_three
        put(3, low_three[:, :space], v.grad_query[...])
        put(4, low_three[:, space:], grad_gate_ref[...])
        put(5, lengthen(v.four_sum[...], owner), need.own_cotangent[...])
        put(7, need.low_four_back[...], mixed_ref[...])
        put_down(v.memory_out, v.three_sum[...], need.normed_rows)
        memory_kept = send_far(1, v.memory_out)
        projected_ref, across_ref, below_ref = need.projected, need.across, need.below
        weight_ref = need.full_in
        for c in attended_sent:
            c.wait()

        @pl.loop(0, width // (2 * HD))
        def _(pair):
            queries, keys, values = [projected_ref[:, wide_lanes(pair, p * width)] for p in range(3)]
            above = jnp.concatenate(
                [v.attended_in[p, :, wide_lanes(pair)] for p in range(ranks)], axis=0
            )
            v.key_sum[...] = jnp.zeros_like(v.key_sum)
            v.value_sum[...] = jnp.zeros_like(v.value_sum)
            for r in range(count // block):
                at, top = slice(r * block, (r + 1) * block), (r + 1) * block
                parts = []
                for h in range(2):
                    lanes = slice(h * HD, (h + 1) * HD)
                    probs = block_probs(
                        queries[:, lanes], keys[:, lanes], across_ref, below_ref, r, block
                    )
                    grad_probs = mt(above[at, lanes], values[:top, lanes])
                    inner = jnp.sum(probs * grad_probs, axis=-1, keepdims=True)
                    grad_scores = (probs * (grad_probs - inner)).astype(BF16)
                    parts.append(mm(grad_scores, keys[:top, lanes]))
                    v.key_sum[h, :top, :] += tm(grad_scores, queries[at, lanes])
                    v.value_sum[h, :top, :] += tm(probs.astype(BF16), above[at, lanes])
                v.grads[at, wide_lanes(pair)] = (
                    jnp.concatenate(parts, axis=1) * HD**-0.5
                ).astype(BF16)
            v.grads[:, wide_lanes(pair, width)] = (
                jnp.concatenate([v.key_sum[0], v.key_sum[1]], axis=1) * HD**-0.5
            ).astype(BF16)
            v.grads[:, wide_lanes(pair, 2 * width)] = jnp.concatenate(
                [v.value_sum[0], v.value_sum[1]], axis=1
            ).astype(BF16)

        input_sent = []
        for d in list(range(1, ranks)) + [0]:
            at = pl.ds(pl.multiple_of(lax.rem(rank + d, ranks) * local, local), local)
            part = mt(v.grads[at, :], weight_ref[...]).astype(BF16)
            if d:
                v.input_out[d] = part
                input_sent.append(near(7, d, v.input_out.at[d], v.input_in.at[rank]))
                input_sent[-1].start()
            else:
                v.input_in[rank] = part
            one = jnp.concatenate(
                [
                    mt(
                        v.grads[at, p * width : (p + 1) * width],
                        ups_ref[:, p * width : (p + 1) * width],
                    )
                    for p in range(3)
                ],
                axis=1,
            )
            v.one_in[rank, :, at] = shorten(masked(one, owner_ref[at, :]))
        one_sent = shared(8, v.one_in)
        for c in one_sent:
            c.start()
        for c in later_sent:
            c.wait()
        low_one = need.low_one
        for p in range(3):
            put(
                p,
                low_one[:, p * space : (p + 1) * space],
                v.grads[:, p * width : (p + 1) * width],
            )
        put(6, lengthen(side_by_side(v.back_in), owner), need.attended[...])
        put(
            8,
            lengthen(side_by_side(need.two_short), owner),
            jnp.concatenate([v.branch_in[p] for p in range(ranks)], axis=0),
        )
        ups_kept = send_far(0, v.ups_out)
        down_input_ref, rows_ref, gain_one = need.down_input, need.inputs, need.gain_one
        normed_one_ref = need.normed_one
        for c in one_sent:
            c.wait()
        v.one_sum[...] = total(v.one_in).astype(BF16)
        put_down(v.down_out, v.one_sum[...], normed_one_ref)
        down_kept = send_far(2, v.down_out)
        for c in input_sent:
            c.wait()
        low = lengthen(v.one_sum[:, own_tokens], owner_own)
        upstream = total(v.input_in) + mt(low, down_input_ref[...])
        v.input_grad[...] = v.grad_middle[...] + rms_backward(
            rows_ref[...].astype(F32), gain_one[...].astype(F32)[None, :], upstream
        )
        stores.append(pltpu.make_async_copy(v.input_grad, outs[1], saved.at[1]))
        stores[1].start()

        @pl.loop(1, groups)
        def _(d):
            for i, ref in enumerate((v.ups_out, v.memory_out, v.down_out)):
                far_piece(i, d, ref).wait()

        for c in stores + [ups_kept, memory_kept, down_kept]:
            c.wait()

    near_sems = pltpu.SemaphoreType.DMA((9, ranks))
    far_sems = pltpu.SemaphoreType.DMA((3, groups))
    return wides, pl.pallas_call(
        body,
        out_shape=[jax.ShapeDtypeStruct(shape, dtype) for shape, dtype in results],
        in_specs=[ANY] * len(arrays),
        out_specs=[ANY] * len(results),
        scratch_shapes=[
            pltpu.VMEM(x.shape[1:] if x is shown.picks else x.shape, x.dtype) for x in inputs
        ]
        + [pltpu.VMEM(shape, dtype) for shape, dtype in vmem.values()]
        + [
            pltpu.SemaphoreType.DMA((len(inputs),)),
            pltpu.SemaphoreType.DMA((5,)),
            near_sems,
            near_sems,
            far_sems,
            far_sems,
        ],
        compiler_params=pltpu.CompilerParams(
            collective_id=cid, has_side_effects=True, vmem_limit_bytes=61 << 20
        ),
    )(*arrays)


def forward(given, table, key_picks, spots, cid, block=128, sub=32, conv=32):
    _, query_spot, gate_spot, attend_spot, mixed_spot, low_spot = spots
    shown = types.SimpleNamespace(**given)
    names = list(given)
    local_arrays = list(given.values())
    ranks, groups = lax.axis_size(TP), lax.axis_size(DP)
    local, model = shown.inputs.shape
    count = shown.owner.shape[0]
    width = shown.gate.shape[1]
    half = shown.keys.shape[2]
    number = key_picks.shape[2]
    picks = key_picks.shape[0] * number
    space = NAD * RANK
    rows = table.shape[0]
    piece = rows // 2
    blocks = 2 * groups
    stride = sub + 1
    chips = groups // 2
    relayed = chips == 4
    hops = max(chips, 4)
    tree = [
        shown.flat_in,
        shown.down_input,
        shown.ups,
        shown.out_t,
        shown.attend_t,
        shown.query,
        shown.gate,
        shown.down_memory,
        shown.mixed_t,
    ]
    early, nested, late = (0, 1, 2), (3, 4), (5, 6, 7, 8)
    cuts = 2
    chunks = tuple(range(len(tree), len(tree) + cuts))
    tree_shapes = [
        (x.shape[0], x.shape[1] * (ranks if a in nested else 1)) for a, x in enumerate(tree)
    ]
    full = [((groups, *shape), BF16) for shape in tree_shapes]
    results = dict(
        normed_one=((count, model), BF16),
        low_one=((count, 3 * space), BF16),
        projected=((count, 3 * width), BF16),
        attended=((count, width), BF16),
        middle=((local, model), F32),
        two_short=((ranks, RANK, local), BF16),
        normed_rows=((count, model), BF16),
        low_three=((count, 2 * space), BF16),
        weights=((number, count), F32),
        mixed=((count, width), BF16),
        grad_recalled=((count, width), BF16),
        grad_gate=((count, width), BF16),
        scale=((count, 1), F32),
        low_four_back=((count, space), BF16),
        own_cotangent=((count, width), BF16),
        first=((count, picks), I32),
        second=((count, picks), I32),
    )
    vmem = dict(
        rows_in=((ranks, local, model), BF16),
        cotangent_in=((ranks, local, model), BF16),
        out_stage=(tree_shapes[3], BF16),
        attend_stage=(tree_shapes[4], BF16),
        attended_in=((local, model), BF16),
        normed_two=((local, model), BF16),
        asked=((count, 2 * half), F32),
        every=((NKEYS, count), F32),
        gate_pre=((count, width), F32),
        narrow=((ranks, number, count), BF16),
        grad_mixed=((count, width), F32),
        picks=(key_picks.shape, I32),
        by_token=((count, picks), F32),
        low=((NKEYS * stride, 128), F32),
        high=((NKEYS * stride, 128), F32),
        spread=((2, sub, NKEYS * NKEYS), BF16),
        dense_in=((2, count, piece), BF16),
        table_in=((2, piece, width), BF16),
        total=((count, width), F32),
        largest=((8, 1), F32),
    )
    outs = [
        *full,
        *results.values(),
        ((groups, rows, width), BF16),
        ((count, NKEYS * NKEYS), BF16),
    ]

    def body(*refs):
        inputs = refs[: len(names) + 2]
        out_refs = refs[len(inputs) : len(inputs) + len(outs)]
        rest = list(refs[len(inputs) + len(outs) :])

        def take(n):
            taken = rest[:n]
            del rest[:n]
            return taken

        held = take(len(names))
        gathered = take(len(tree))
        r = types.SimpleNamespace(**dict(zip(results, take(len(results)))))
        v = types.SimpleNamespace(**dict(zip(vmem, take(len(vmem)))))
        loaded, kept, stored, near_send, near_recv, tree_send, tree_recv, pass_send, pass_recv = rest[:9]
        moved = rest[9]
        table_ref, picks_ref = inputs[-2:]
        table_out, dense_out = out_refs[-2:]
        rank, group = lax.axis_index(TP), lax.axis_index(DP)
        barrier = pltpu.get_barrier_semaphore()
        for d in range(1, ranks):
            pl.semaphore_signal(
                barrier,
                inc=1,
                device_id={TP: lax.rem(rank + d, ranks)},
                device_id_type=MESH,
            )

        @pl.loop(1, groups)
        def _(d):
            pl.semaphore_signal(
                barrier,
                inc=1,
                device_id={DP: lax.rem(group + d, groups)},
                device_id_type=MESH,
            )

        loads = [
            pltpu.make_async_copy(inputs[i], held[i], loaded.at[i]) for i in range(len(names))
        ]
        loads.append(pltpu.make_async_copy(picks_ref, v.picks, loaded.at[len(names)]))
        for load in loads:
            load.start()
        need = Waited(names, held, loads)
        raw = types.SimpleNamespace(**dict(zip(names, inputs)))

        def near(i, d, src, dst):
            return pltpu.make_async_remote_copy(
                src_ref=src,
                dst_ref=dst,
                send_sem=near_send.at[i, d],
                recv_sem=near_recv.at[i, d],
                device_id={TP: lax.rem(rank + d, ranks)},
                device_id_type=MESH,
            )

        def columns(ref, p, wide):
            return ref.at[:, pl.ds(pl.multiple_of(p * wide, wide), wide)]

        def way(a):
            return 1 if a - len(tree) < cuts // 2 else 2

        def cut_of(a):
            return pl.ds((a - len(tree)) * (rows // cuts), rows // cuts)

        def source(a):
            if a in chunks:
                return table_ref.at[cut_of(a)]
            if a in nested:
                return (v.out_stage, v.attend_stage)[a - 3]
            return inputs[names.index(given_names[a])]

        given_names = [names[i] for i in tree_names]

        def place(a, p):
            if a in chunks:
                return table_out.at[p, cut_of(a)]
            return gathered[a].at[p]

        def partner(d):
            if not relayed:
                return lax.rem(group + 2 * d, groups)
            across = 2 - 4 * lax.rem(lax.div(group, 2), 2) if d & 1 else 0
            along = 4 - 8 * lax.div(group, 4) if d & 2 else 0
            return group + across + along

        def holder(d):
            if isinstance(d, int) and d == 0:
                return group
            return partner(d) if relayed else lax.rem(group - 2 * d + groups, groups)

        def to_chip(a, d):
            relay = relayed and a in chunks and d == 3
            shard = place(a, holder(way(a))) if relay else source(a)
            return pltpu.make_async_remote_copy(
                src_ref=shard,
                dst_ref=shard if relay else place(a, group),
                send_sem=tree_send.at[a, d],
                recv_sem=tree_recv.at[a, d],
                device_id={DP: partner(3 - way(a) if relay else d)},
                device_id_type=MESH,
            )

        def to_sibling(a, d):
            first = isinstance(d, int) and d == 0
            return pltpu.make_async_remote_copy(
                src_ref=source(a) if first else place(a, holder(d)),
                dst_ref=place(a, holder(d)),
                send_sem=pass_send.at[a, d],
                recv_sem=pass_recv.at[a, d],
                device_id={DP: group + 1 - 2 * lax.rem(group, 2)},
                device_id_type=MESH,
            )

        def own_copy(a):
            return pltpu.make_async_copy(source(a), place(a, group), kept.at[a])

        def begin(chosen):
            for a in chosen:
                own_copy(a).start()
                if relayed:
                    for d in range(1, 4):
                        to_chip(a, d).start()
                else:

                    @pl.loop(1, chips)
                    def _(d):
                        to_chip(a, d).start()

                to_sibling(a, 0).start()

        def begin_table(chosen):
            if not relayed:
                begin(chosen)
                return
            for a in chosen:
                to_chip(a, way(a)).start()
                own_copy(a).start()
                to_sibling(a, 0).start()

        def rest_of_table(chosen):
            if relayed:
                for a in chosen:
                    to_chip(a, 3 - way(a)).start()

        def onward(a, d):
            to_chip(a, d).wait_recv()
            to_sibling(a, d).start()

        def other(chosen):
            if relayed:
                for a in chosen:
                    onward(a, 3 - way(a))

        def last(chosen):
            for a in chosen:
                if relayed:
                    onward(a, 3)
                else:

                    @pl.loop(1, chips)
                    def _(d):
                        onward(a, d)

        def collect(chosen):
            if relayed:
                for d in range(1, 3):
                    for a in chosen:
                        onward(a, d)
            last(chosen)

        def settle(chosen):
            for a in chosen:
                own_copy(a).wait()
                to_sibling(a, 0).wait()
                if relayed:
                    for d in range(1, 4):
                        to_sibling(a, d).wait()
                        to_chip(a, d).wait_send()
                else:

                    @pl.loop(1, chips)
                    def _(d):
                        to_sibling(a, d).wait()
                        to_chip(a, d).wait_send()

        stores = []

        def store(src, dst):
            stores.append(pltpu.make_async_copy(src, dst, stored.at[len(stores)]))
            stores[-1].start()

        def store_trees(chosen):
            for a in chosen:
                store(gathered[a], out_refs[a])

        result_refs = dict(zip(results, out_refs[len(tree) :]))

        def flat(ref):
            return ref[...].reshape(-1, ref.shape[2])

        def done(ref):
            for name in results:
                if getattr(r, name) is ref:
                    store(ref, result_refs[name])

        pl.semaphore_wait(barrier, ranks + groups - 2)
        homes = []
        for i, (src, dst) in enumerate(((raw.inputs, v.rows_in), (raw.cotangent, v.cotangent_in))):
            homes.append(pltpu.make_async_copy(src, dst.at[rank], moved.at[i]))
        for i, (src, dst) in enumerate(((raw.out_t, v.out_stage), (raw.attend_t, v.attend_stage))):
            homes.append(
                pltpu.make_async_copy(src, columns(dst, rank, src.shape[1]), moved.at[2 + i])
            )
        for c in homes:
            c.start()
        nest_sent = [
            near(i, d, src, columns(dst, rank, src.shape[1]))
            for i, src, dst in ((0, raw.out_t, v.out_stage), (1, raw.attend_t, v.attend_stage))
            for d in range(1, ranks)
        ]
        rows_sent = [near(2, d, raw.inputs, v.rows_in.at[rank]) for d in range(1, ranks)]
        back_sent = [near(3, d, raw.cotangent, v.cotangent_in.at[rank]) for d in range(1, ranks)]
        for c in nest_sent + rows_sent:
            c.start()
        begin(early)
        begin(late)
        for c in nest_sent:
            c.wait()
        homes[2].wait()
        homes[3].wait()
        begin(nested)
        begin_table(chunks)
        gain_one, owner_ref = need.gain_one, need.owner
        homes[0].wait()
        for c in rows_sent:
            c.wait()
        for c in range(ranks):
            r.normed_one[c * local : (c + 1) * local, :] = rms_forward(
                v.rows_in[c].astype(F32), gain_one[...].astype(F32)[None, :]
            ).astype(BF16)
        done(r.normed_one)
        for c in back_sent:
            c.start()
        collect(early)
        settle(early)
        store_trees(early)
        weight_ref, down_ref, ups_ref = gathered[:3]

        def up(spot):
            return ups_ref[:, :, spot].reshape(space, -1)

        @pl.loop(0, ranks)
        def _(c):
            at = pl.ds(pl.multiple_of(c * local, local), local)
            normed = r.normed_one[at, :]
            low = masked(mm(normed, flat(down_ref)), owner_ref[at, :])
            r.low_one[at, :] = low
            for p in range(3):
                lanes = slice(p * width, (p + 1) * width)
                r.projected[at, lanes] = (
                    mm(normed, weight_ref[:, :, lanes].reshape(model, width))
                    + mm(low[:, p * space : (p + 1) * space], up(lanes))
                ).astype(BF16)

        across_ref, below_ref = need.across, need.below

        @pl.loop(0, width // (2 * HD))
        def _(pair):
            queries, keys, values = [r.projected[:, wide_lanes(pair, p * width)] for p in range(3)]
            for q in range(count // block):
                top = (q + 1) * block
                parts = []
                for lanes in (slice(0, HD), slice(HD, 2 * HD)):
                    probs = block_probs(
                        queries[:, lanes], keys[:, lanes], across_ref, below_ref, q, block
                    )
                    parts.append(mm(probs.astype(BF16), values[:top, lanes]))
                r.attended[q * block : top, wide_lanes(pair)] = jnp.concatenate(
                    parts, axis=1
                ).astype(BF16)

        def lines_of(p):
            return r.attended.at[pl.ds(pl.multiple_of(p * local, local), local)]

        attended_sent = [
            near(4, d, lines_of(lax.rem(rank + d, ranks)), columns(v.attended_in, rank, width))
            for d in range(1, ranks)
        ]
        for c in attended_sent:
            c.start()
        rest_of_table(chunks)
        own_rows = pl.ds(pl.multiple_of(rank * local, local), local)
        v.attended_in[:, pl.ds(pl.multiple_of(rank * width, width), width)] = r.attended[own_rows, :]
        done(r.low_one)
        done(r.projected)
        done(r.attended)
        collect(nested)
        settle(nested)
        store_trees(nested)
        out_ref, attend_ref = gathered[3:5]
        residual_ref, gain_two, owner_own = need.inputs, need.gain_two, need.owner_own[...]
        for c in attended_sent:
            c.wait()
        low = masked(mt(v.attended_in[...], flat(attend_ref)), owner_own)
        middle = (
            residual_ref[...].astype(F32)
            + mt(v.attended_in[...], flat(out_ref))
            + mm(low, up(attend_spot))
        )
        r.middle[...] = middle
        normed = rms_forward(middle, gain_two[...].astype(F32)[None, :]).astype(BF16)
        v.normed_two[...] = normed
        r.normed_rows[own_rows, :] = normed
        r.two_short[rank] = shorten(low)
        normed_sent = [
            near(5, d, v.normed_two, r.normed_rows.at[own_rows]) for d in range(1, ranks)
        ] + [near(6, d, r.two_short.at[rank], r.two_short.at[rank]) for d in range(1, ranks)]
        for c in normed_sent:
            c.start()
        done(r.middle)
        loads[-1].wait()
        r.first[...] = jnp.concatenate(
            [v.picks[m, 0] for m in range(key_picks.shape[0])], axis=0
        ).T
        r.second[...] = jnp.concatenate(
            [v.picks[m, 1] for m in range(key_picks.shape[0])], axis=0
        ).T
        done(r.first)
        done(r.second)
        collect(late)
        settle(late)
        store_trees(late)
        query_ref, gate_ref, memory_ref, mixed_ref = gathered[5:]
        homes[1].wait()
        for c in back_sent:
            c.wait()
        own_lanes = pl.ds(pl.multiple_of(rank * width, width), width)
        for c in range(ranks):
            at = slice(c * local, (c + 1) * local)
            r.own_cotangent[at, :] = v.cotangent_in[c, :, own_lanes]
            low = masked(mt(v.cotangent_in[c], up(mixed_spot)), owner_ref[at, :])
            r.low_four_back[at, :] = low
            v.grad_mixed[at, :] = mm(v.cotangent_in[c], flat(mixed_ref)) + mm(low, up(low_spot))
        done(r.own_cotangent)
        done(r.low_four_back)
        keys_ref = need.keys
        for c in normed_sent:
            c.wait()
        if relayed:
            for a in chunks:
                onward(a, way(a))
                to_chip(a, 3).start()
        done(r.normed_rows)
        done(r.two_short)

        @pl.loop(0, ranks)
        def _(c):
            at = pl.ds(pl.multiple_of(c * local, local), local)
            normed = r.normed_rows[at, :]
            low = masked(mm(normed, flat(memory_ref)), owner_ref[at, :])
            r.low_three[at, :] = low
            v.asked[at, :] = mm(normed, flat(query_ref)) + mm(low[:, :space], up(query_spot))
            v.gate_pre[at, :] = mm(normed, flat(gate_ref)) + mm(low[:, space:], up(gate_spot))

        done(r.low_three)
        slot = lax.broadcasted_iota(I32, (NKEYS, block), 0)
        for part in range(2):
            top, low = two_parts(v.asked[:, part * half : (part + 1) * half])
            v.every[...] = mt(keys_ref[part], top) + mt(keys_ref[part], low)

            @pl.loop(0, count // block)
            def _(c):
                lanes = pl.ds(pl.multiple_of(c * block, block), block)
                scores = v.every[:, lanes]
                found = []
                for k in range(number):
                    hit = slot == v.picks[rank, part, k : k + 1, lanes]
                    found.append(jnp.sum(jnp.where(hit, scores, 0.0), axis=0, keepdims=True))
                found = jnp.concatenate(found, axis=0)
                if part == 0:
                    r.weights[:, lanes] = found
                else:
                    added = (r.weights[:, lanes] + found) * (2 * half) ** -0.5
                    raised = jnp.exp(added - jnp.max(added, axis=0, keepdims=True))
                    weights = raised / jnp.sum(raised, axis=0, keepdims=True)
                    r.weights[:, lanes] = weights
                    v.narrow[rank, :, lanes] = weights.astype(BF16)

        narrow_sent = [
            near(7, d, v.narrow.at[rank], v.narrow.at[rank]) for d in range(1, ranks)
        ]
        for c in narrow_sent:
            c.start()
        done(r.weights)
        for c in narrow_sent:
            c.wait()
        v.by_token[...] = (
            jnp.concatenate([v.narrow[p] for p in range(ranks)], axis=0).astype(F32).T
        )

        wide_slot = lax.broadcasted_iota(I32, (NKEYS, picks), 0)
        steps = count // sub

        def spread_out(t, s):
            return pltpu.make_async_copy(
                v.spread.at[s],
                dense_out.at[pl.ds(pl.multiple_of(t * sub, sub), sub)],
                moved.at[4 + s],
            )

        @pl.loop(0, steps)
        def _(t):
            s = lax.rem(t, 2)
            at = pl.ds(pl.multiple_of(t * sub, sub), sub)
            firsts, seconds, weights = r.first[at, :], r.second[at, :], v.by_token[at, :]
            for n in range(sub):
                b = jnp.where(wide_slot == seconds[n : n + 1], 1.0, 0.0).astype(BF16)
                a = jnp.where(wide_slot == firsts[n : n + 1], weights[n : n + 1], 0.0).astype(BF16)
                both = mt(a, b)
                v.low[pl.ds(n, NKEYS, stride=stride), :] = both[:, :128]
                v.high[pl.ds(n, NKEYS, stride=stride), :] = both[:, 128:]

            @pl.when(t >= 2)
            def _():
                spread_out(t - 2, s).wait()

            @pl.loop(0, NKEYS // conv)
            def _(c):
                for q in range(conv):
                    i = c * conv + q
                    lanes = pl.multiple_of(i * NKEYS, NKEYS)
                    lines = pl.ds(i * stride, sub)
                    v.spread[s, :, pl.ds(lanes, 128)] = v.low[lines, :].astype(BF16)
                    v.spread[s, :, pl.ds(lanes + 128, 128)] = v.high[lines, :].astype(BF16)

            spread_out(t, s).start()

            @pl.when(t == steps - 7)
            def _():
                other(chunks)

        spread_out(steps - 2, steps % 2).wait()
        spread_out(steps - 1, (steps - 1) % 2).wait()

        def block_at(b):
            if not relayed:
                return lax.div(b, 2), lax.rem(b, 2)
            d = lax.div(b, 4)
            across = (2 - 4 * lax.rem(lax.div(group, 2), 2)) * lax.rem(d, 2)
            along = (4 - 8 * lax.div(group, 4)) * lax.div(d, 2)
            near_by = (1 - 2 * lax.rem(group, 2)) * lax.rem(lax.div(b, 2), 2)
            return group + across + along + near_by, lax.rem(b, 2)

        def fetch(b, s):
            p, h = block_at(b)
            return (
                pltpu.make_async_copy(
                    dense_out.at[:, pl.ds(pl.multiple_of((p * 2 + h) * piece, piece), piece)],
                    v.dense_in.at[s],
                    moved.at[6 + s],
                ),
                pltpu.make_async_copy(
                    table_out.at[p, pl.ds(pl.multiple_of(h * piece, piece), piece)],
                    v.table_in.at[s],
                    moved.at[8 + s],
                ),
            )

        def arrived(d):
            for a in chunks:
                if isinstance(d, int) and d == 0:
                    own_copy(a).wait()
                to_sibling(a, d).wait_recv()

        arrived(0)
        if relayed:
            arrived(1)
            arrived(2)
        else:
            last(chunks)

            @pl.loop(1, chips)
            def _(d):
                arrived(d)

        v.total[...] = jnp.zeros_like(v.total)
        v.largest[...] = jnp.zeros_like(v.largest)
        for c in fetch(0, 0):
            c.start()

        @pl.loop(0, blocks)
        def _(b):
            s = lax.rem(b, 2)
            if relayed:

                @pl.when(b == 11)
                def _():
                    last(chunks)

                @pl.when(b == 13)
                def _():
                    arrived(3)

            @pl.when(b + 1 < blocks)
            def _():
                for c in fetch(b + 1, 1 - s):
                    c.start()

            for c in fetch(b, s):
                c.wait()
            v.total[...] += mm(v.dense_in[s], v.table_in[s])
            peak = v.largest[...]
            for c in range(piece // 512):
                values = v.table_in[s, c * 512 : (c + 1) * 512, :].astype(F32)
                squares = values * values
                norms = jnp.sum(squares[:, :128] + squares[:, 128:], axis=1, keepdims=True)
                peak = jnp.maximum(peak, jnp.max(norms.reshape(-1, 8, 1), axis=0))
            v.largest[...] = peak

        gate, recalled, upstream = v.gate_pre[...], v.total[...], v.grad_mixed[...]
        sigmoid = 1.0 / (1.0 + jnp.exp(-gate))
        act = gate * sigmoid
        r.mixed[...] = (act * recalled).astype(BF16)
        grad = (upstream * act).astype(BF16)
        r.grad_recalled[...] = grad
        r.grad_gate[...] = (
            upstream * recalled * sigmoid * (1.0 + gate * (1.0 - sigmoid))
        ).astype(BF16)
        wide = grad.astype(F32)
        bound = jnp.max(v.largest[...]) * jnp.sum(wide * wide, axis=1, keepdims=True)
        r.scale[...] = 32000.0 * lax.rsqrt(jnp.maximum(bound, 1e-30))
        for ref in (r.mixed, r.grad_recalled, r.grad_gate, r.scale):
            done(ref)
        for a in chunks:
            for d in range(4 if relayed else 1):
                to_sibling(a, d).wait_send()
            if relayed:
                for d in range(1, 4):
                    to_chip(a, d).wait_send()
            else:

                @pl.loop(1, chips)
                def _(d):
                    to_sibling(a, d).wait_send()
                    to_chip(a, d).wait_send()

        for name in names:
            getattr(need, name)
        for c in stores:
            c.wait()

    tree_names = [
        next(i for i, y in enumerate(local_arrays) if y is x) for x in tree
    ]
    arrays = [*local_arrays, table, key_picks]
    near_sems = pltpu.SemaphoreType.DMA((8, ranks))
    tree_sems = pltpu.SemaphoreType.DMA((len(tree) + cuts, hops))
    got = pl.pallas_call(
        body,
        out_shape=[jax.ShapeDtypeStruct(shape, dtype) for shape, dtype in outs],
        in_specs=[ANY] * len(arrays),
        out_specs=[ANY] * len(outs),
        scratch_shapes=[pltpu.VMEM(x.shape, x.dtype) for x in local_arrays]
        + [pltpu.VMEM(shape, dtype) for shape, dtype in full]
        + [pltpu.VMEM(shape, dtype) for shape, dtype in results.values()]
        + [pltpu.VMEM(shape, dtype) for shape, dtype in vmem.values()]
        + [
            pltpu.SemaphoreType.DMA((len(names) + 1,)),
            pltpu.SemaphoreType.DMA((len(tree) + cuts,)),
            pltpu.SemaphoreType.DMA((len(outs),)),
            near_sems,
            near_sems,
            tree_sems,
            tree_sems,
            tree_sems,
            tree_sems,
            pltpu.SemaphoreType.DMA((10,)),
        ],
        compiler_params=pltpu.CompilerParams(
            collective_id=cid, has_side_effects=True, vmem_limit_bytes=61 << 20
        ),
    )(*arrays)
    whole_arrays = [x.reshape(-1, x.shape[2]) for x in got[: len(tree)]]
    return whole_arrays, types.SimpleNamespace(**dict(zip(results, got[len(tree) :]))), got[-2]


def pick_grads(first, second, grads, scale, table):
    tokens, picks = first.shape
    width = grads.shape[1]
    per_block = 16
    rows = per_block * NKEYS
    blocks = table.shape[0] // rows

    def body(*refs):
        table_ref, out_ref, kept, sems = refs[4], refs[5], refs[6], refs[11]
        first_ref, second_ref, grads_ref, scale_ref = refs[7:11]
        step = pl.program_id(0)

        @pl.when(step == 0)
        def _():
            copies = [pltpu.make_async_copy(refs[i], refs[7 + i], sems.at[i]) for i in range(4)]
            for c in copies:
                c.start()
            kept[...] = jnp.zeros_like(kept)
            for c in copies:
                c.wait()

        own = first_ref[...]
        low = second_ref[...] & 127
        factor = jnp.broadcast_to(scale_ref[...], (tokens, 128))
        total = kept[...]
        for b in range(per_block):
            every = mt(grads_ref[...], table_ref[b * NKEYS : (b + 1) * NKEYS, :])
            packed = (every[:, 128:] * factor).astype(I32) * 65536 + (
                every[:, :128] * factor
            ).astype(I32)
            found = jnp.take_along_axis(packed, low, axis=1, mode="promise_in_bounds")
            total = jnp.where(own == step * per_block + b, found, total)
        kept[...] = total

        @pl.when(step == blocks - 1)
        def _():
            p = kept[...]
            right = lax.shift_right_arithmetic(lax.shift_left(p, 16), 16)
            left = lax.shift_right_arithmetic(p - right, 16)
            both = jnp.where(second_ref[...] >= 128, left, right).astype(F32) / factor
            out_ref[...] = both.T.astype(BF16)

    return pl.pallas_call(
        body,
        grid=(blocks,),
        out_shape=jax.ShapeDtypeStruct((picks, tokens), BF16),
        in_specs=[ANY] * 4 + [pl.BlockSpec((rows, width), lambda s: (s, 0))],
        out_specs=whole((picks, tokens)),
        scratch_shapes=[pltpu.VMEM((tokens, picks), I32)]
        + [pltpu.VMEM(x.shape, x.dtype) for x in (first, second, grads, scale)]
        + [pltpu.SemaphoreType.DMA((4,))],
        compiler_params=pltpu.CompilerParams(vmem_limit_bytes=61 << 20),
    )(first, second, grads, scale, table)


def by_part(down, parts):
    shaped = down.reshape(down.shape[0], NAD, parts, RANK).transpose(0, 2, 1, 3)
    return shaped.reshape(down.shape)


def add_up(inputs, plans, through):
    shapes = []
    for x, (axis, sizes) in zip(inputs, plans):
        for size in sizes:
            if isinstance(size, tuple):
                shapes.append((size[0], x.shape[1], size[1]))
            else:
                shapes.append((x.shape[1], size) if axis else (size, x.shape[2]))

    def body(*refs):
        outs = iter(refs[len(inputs) + len(through) :])
        for ref in refs[len(inputs) : len(inputs) + len(through)]:
            next(outs)[...] = ref[...]
        for ref, (axis, sizes) in zip(refs, plans):

            def total(start, size):
                cut = slice(start, start + size)
                return sum(
                    (ref[p, :, cut] if axis else ref[p, cut, :]).astype(F32)
                    for p in range(ref.shape[0])
                )

            at = 0
            for size in sizes:
                out = next(outs)
                if isinstance(size, tuple):
                    for q in range(size[0]):
                        out[q] = total(at, size[1])
                        at += size[1]
                else:
                    out[...] = total(at, size)
                    at += size

    kept = [(x.shape, x.dtype) for x in through]
    return stage(body, kept + [(shape, F32) for shape in shapes], (*inputs, *through))


def make_ready(segments, adapters, project_in, down_input, down_memory, turned, joined, local):
    count = segments.shape[1]
    parts, lines, width = project_in.shape

    def body(segments_ref, adapters_ref, project_ref, input_ref, memory_ref, *refs):
        ins, outs = refs[: len(turned) + len(joined)], refs[len(turned) + len(joined) :]

        def ordered(ref, parts):
            size = NAD * parts * RANK
            row = lax.broadcasted_iota(I32, (size, size), 0)
            column = lax.broadcasted_iota(I32, (size, size), 1)
            part, rest = lax.div(column, NAD * RANK), lax.rem(column, NAD * RANK)
            adapter, rank = lax.div(rest, RANK), lax.rem(rest, RANK)
            came = adapter * (parts * RANK) + part * RANK + rank
            return mm(ref[...], jnp.where(row == came, 1.0, 0.0).astype(BF16)).astype(BF16)

        for p in range(parts):
            outs[0][:, p * width : (p + 1) * width] = project_ref[p]
        outs[1][...] = ordered(input_ref, 3)
        outs[2][...] = ordered(memory_ref, 2)
        for p in range(parts):
            outs[3][:, p * width : (p + 1) * width] = ins[len(turned)][p]
        at = parts * width
        for ref in ins[len(turned) + 1 :]:
            outs[3][:, at : at + ref.shape[1]] = ref[...]
            at += ref.shape[1]
        for ref, out in zip(ins[: len(turned)], outs[4:]):
            out[...] = ref[...].astype(F32).T.astype(BF16)
        owner_ref, below_ref, owner_own_ref = outs[-3:]
        across = jnp.broadcast_to(segments_ref[...], (8, count))
        owner = jnp.zeros_like(across)
        for s in range(adapters.shape[1]):
            owner = jnp.where(across == s, adapters_ref[0:1, s : s + 1], owner)
        owner_ref[...] = owner.T[:, 0:1]
        below_ref[...] = across.T[:, 0:1]
        own = pl.ds(pl.multiple_of(lax.axis_index(TP) * local, local), local)
        owner_own_ref[...] = owner_ref[own, :]

    small = parts * width + sum(x.shape[1] for x in joined[1:])
    return stage(
        body,
        [
            ((lines, parts * width), BF16),
            (down_input.shape, BF16),
            (down_memory.shape, BF16),
            ((joined[1].shape[0], small), BF16),
        ]
        + [(x.shape[::-1], BF16) for x in turned]
        + [((count, 1), I32), ((count, 1), I32), ((local, 1), I32)],
        (segments, adapters, project_in, down_input, down_memory, *turned, *joined),
    )


def on_device(
    inputs,
    cotangent,
    norm_attend,
    norm_memory,
    project_in,
    project_out,
    query_weight,
    gate_weight,
    memory_out,
    half_keys,
    value_table,
    key_picks,
    segment_ids,
    adapter_ids,
    down_input,
    up_input,
    down_attend,
    up_attend,
    down_memory,
    up_query,
    up_gate,
    down_mixed,
    up_mixed,
):
    groups = lax.axis_size(DP)
    ranks = lax.axis_size(TP)
    rank = lax.axis_index(TP)
    local = inputs.shape[0]
    count = segment_ids.shape[0]
    width = project_in.shape[2]
    model = inputs.shape[1]

    across = segment_ids[None, :]
    attend_turned = down_attend.T
    joined = (up_input.transpose(1, 0, 2), up_query, up_gate, up_attend, up_mixed, down_mixed.T)
    turned = (project_out, memory_out)
    if project_out.shape[1] % 128 == 0:
        ready = make_ready(
            across,
            adapter_ids,
            project_in.transpose(1, 0, 2),
            down_input,
            down_memory,
            turned,
            joined,
            local,
        )
        flat_in, parted_input, parted_memory, small, out_turned, mixed_turned = ready[:6]
        owner, below, owner_own = ready[6:]
    else:
        flat_in = project_in.reshape(project_in.shape[0], 3 * width)
        parted_input, parted_memory = by_part(down_input, 3), by_part(down_memory, 2)
        out_turned, mixed_turned = [x.T for x in turned]
        small = jnp.concatenate((up_input.reshape(-1, 3 * width),) + joined[1:], axis=1)
        below = segment_ids[:, None]
        owner = jnp.zeros_like(below)
        for s in range(adapter_ids.shape[1]):
            owner = jnp.where(below == s, adapter_ids[0, s], owner)
        owner_own = lax.dynamic_slice_in_dim(owner, rank * local, local, 0)
    spots, at = [], 0
    for size in (3 * width, up_query.shape[1], width, model, model, width):
        spots.append(slice(at, at + size))
        at += size
    gain_one, gain_two, keys = norm_attend, norm_memory, half_keys[0]
    (
        (
            full_in,
            full_down_input,
            ups,
            out_t,
            attend_t,
            full_query,
            full_gate,
            full_down_memory,
            mixed_t,
        ),
        kept,
        table,
    ) = forward(
        dict(
            flat_in=flat_in,
            down_input=parted_input,
            ups=small,
            out_t=out_turned,
            attend_t=attend_turned,
            query=query_weight,
            gate=gate_weight,
            down_memory=parted_memory,
            mixed_t=mixed_turned,
            inputs=inputs,
            cotangent=cotangent,
            gain_one=gain_one,
            gain_two=gain_two,
            owner=owner,
            owner_own=owner_own,
            across=across,
            below=below,
            keys=keys,
        ),
        value_table,
        key_picks,
        spots,
        1,
    )
    mixed = kept.mixed
    partial_mixed = mt(mixed, mixed_t).astype(BF16).reshape(ranks, local, model)

    def block_of(blocks, d):
        return lax.dynamic_index_in_dim(blocks, lax.rem(rank + d, ranks), 0, keepdims=False)

    def turn(d):
        return [(p, (p + d) % ranks) for p in range(ranks)]

    mixed_parts = [block_of(partial_mixed, 0)] + [
        lax.ppermute(block_of(partial_mixed, d), TP, turn(d)) for d in range(1, ranks)
    ]
    picked = pick_grads(
        kept.first, kept.second, kept.grad_recalled, kept.scale, table.reshape(-1, width)
    )
    picked, mixed_parts = lax.optimization_barrier((picked, mixed_parts))
    given = dict(
        picked=picked.reshape(ranks, -1, count),
        weights=kept.weights,
        keys=keys,
        picks=key_picks,
        query=full_query,
        gate=full_gate,
        ups=ups,
        grad_gate=kept.grad_gate,
        mixed=mixed,
        owner=owner,
        owner_own=owner_own,
        middle=kept.middle,
        cotangent=cotangent,
        gain_two=gain_two,
        down_memory=full_down_memory,
        out_t=out_t,
        attend_t=attend_t,
        low_three=kept.low_three,
        own_cotangent=kept.own_cotangent,
        low_four_back=kept.low_four_back,
        normed_rows=kept.normed_rows,
        projected=kept.projected,
        across=across,
        below=below,
        full_in=full_in,
        low_one=kept.low_one,
        attended=kept.attended,
        two_short=kept.two_short,
        down_input=full_down_input,
        inputs=inputs,
        gain_one=gain_one,
        normed_one=kept.normed_one,
    )
    wides, (outputs, input_grad, up_parts, memory_parts, down_parts) = backward(
        given, mixed_parts, spots, 5
    )
    (
        outputs,
        input_grad,
        grad_up_input,
        grad_up_query,
        grad_up_gate,
        grad_up_mixed,
        grad_down_attend,
        grad_down_mixed,
        grad_up_attend,
        grad_down_memory,
        grad_down_input,
    ) = add_up(
        (up_parts, memory_parts, down_parts),
        (
            (1, ((3, width), *wides[3:])),
            (0, (memory_parts.shape[1],)),
            (0, (down_parts.shape[1],)),
        ),
        (outputs, input_grad),
    )
    return (
        outputs,
        input_grad,
        grad_down_input.T,
        grad_up_input.transpose(1, 0, 2),
        grad_down_attend.T,
        grad_up_attend,
        grad_down_memory.T,
        grad_up_query,
        grad_up_gate,
        grad_down_mixed.T,
        grad_up_mixed,
    )


def solution(mesh):
    rows = P((DP, TP), None)
    both = P(DP, TP)
    wide = P(DP, None)
    turned = P(TP, DP)
    split = P(DP, None, TP)
    return jax.shard_map(
        on_device,
        mesh=mesh,
        in_specs=(
            rows,
            rows,
            P(),
            P(),
            split,
            turned,
            both,
            both,
            turned,
            P(TP, None, None, None),
            both,
            P(None, None, None, DP),
            P(DP),
            wide,
            wide,
            split,
            turned,
            wide,
            wide,
            both,
            both,
            turned,
            wide,
        ),
        out_specs=(rows, rows, both, split, turned, both, both, both, both, turned, both),
        check_vma=False,
    )
```

```python
import types

import jax
import jax.numpy as jnp
from jax import lax
from jax.experimental import pallas as pl
from jax.experimental.pallas import tpu as pltpu
from jax.sharding import PartitionSpec as P

DP, TP = "dp", "tensor"
HD = 64
NKEYS = 256
RANK = 16
NAD = 8
EPS = 1e-06
NEGATIVE = -1e30
F32, BF16, I32 = jnp.float32, jnp.bfloat16, jnp.int32
MESH = pl.DeviceIdType.MESH
ANY = pl.BlockSpec(memory_space=pl.ANY)


def mm(a, b):
    return lax.dot_general(a, b, (((1,), (0,)), ((), ())), preferred_element_type=F32)


def mt(a, b):
    return lax.dot_general(a, b, (((1,), (1,)), ((), ())), preferred_element_type=F32)


def tm(a, b):
    return lax.dot_general(a, b, (((0,), (0,)), ((), ())), preferred_element_type=F32)


def two_parts(x):
    top = x.astype(BF16)
    return top, (x - top.astype(F32)).astype(BF16)


def whole(shape):
    return pl.BlockSpec(shape, lambda *_: (0,) * len(shape))


def stage(body, outs, ins, scratch=(), limit=61):
    return pl.pallas_call(
        body,
        grid=(1,),
        out_shape=[jax.ShapeDtypeStruct(shape, dtype) for shape, dtype in outs],
        in_specs=[whole(x.shape) for x in ins],
        out_specs=[whole(shape) for shape, _ in outs],
        scratch_shapes=list(scratch),
        compiler_params=pltpu.CompilerParams(vmem_limit_bytes=limit << 20),
    )(*ins)


def rms_forward(values, gain):
    factor = lax.rsqrt(jnp.mean(values * values, axis=-1, keepdims=True) + EPS)
    return values * factor * gain


def rms_backward(values, gain, upstream):
    factor = lax.rsqrt(jnp.mean(values * values, axis=-1, keepdims=True) + EPS)
    scaled = upstream * gain
    return factor * scaled - values * (factor * factor * factor) * jnp.mean(
        values * scaled, axis=-1, keepdims=True
    )


def masked(values, owner):
    columns = lax.broadcasted_iota(I32, values.shape, 1)
    adapter = lax.rem(lax.div(columns, RANK), NAD)
    return jnp.where(adapter == owner, values, 0.0).astype(BF16)


def folding(parts):
    shape = (parts * RANK, parts * NAD * RANK)
    short = lax.broadcasted_iota(I32, shape, 0)
    column = lax.broadcasted_iota(I32, shape, 1)
    same = (lax.div(short, RANK) == lax.div(column, NAD * RANK)) & (
        lax.rem(short, RANK) == lax.rem(column, RANK)
    )
    return jnp.where(same, 1.0, 0.0).astype(BF16)


def shorten(values):
    return mt(folding(values.shape[1] // (NAD * RANK)), values).astype(BF16)


def lengthen(short, owner):
    return masked(tm(short, folding(short.shape[0] // RANK)), owner)


def side_by_side(blocks):
    return jnp.concatenate([blocks[p] for p in range(blocks.shape[0])], axis=1)


def block_probs(queries, keys, across_ref, down_ref, r, block):
    top = (r + 1) * block
    at = slice(r * block, top)
    scores = mt(queries[at], keys[:top]) * HD**-0.5
    place = lax.broadcasted_iota(I32, (block, top), 0) + r * block
    other = lax.broadcasted_iota(I32, (block, top), 1)
    ahead = across_ref[:, :top]
    seen = (other <= place) & ((ahead == 0) | (ahead == down_ref[at, :]))
    scores = jnp.where(seen, scores, NEGATIVE)
    raised = jnp.exp(scores - jnp.max(scores, axis=-1, keepdims=True))
    return raised / jnp.sum(raised, axis=-1, keepdims=True)


def wide_lanes(pair, base=0):
    return pl.ds(pl.multiple_of(base + pair * 2 * HD, 2 * HD), 2 * HD)


def own_columns(short, owner, first):
    high, count = short.shape
    adapters = NAD // lax.axis_size(TP)
    pattern = lax.broadcasted_iota(I32, (high, adapters * high), 0) == lax.rem(
        lax.broadcasted_iota(I32, (high, adapters * high), 1), high
    )
    spread = tm(short, jnp.where(pattern, 1.0, 0.0).astype(BF16))
    adapter = lax.div(lax.broadcasted_iota(I32, (count, adapters * high), 1), high) + first
    return jnp.where(adapter == owner, spread, 0.0).astype(BF16)


class Waited:
    def __init__(self, names, refs, loads):
        self._pending = dict(zip(names, zip(refs, loads)))

    def __getattr__(self, name):
        ref, load = self._pending[name]
        load.wait()
        setattr(self, name, ref)
        return ref


def backward(given, mixed_parts, ups_spots, cid, block=128):
    _, query_spot, gate_spot, attend_spot, mixed_spot, low_spot = ups_spots
    shown = types.SimpleNamespace(**given)
    picked = given.pop(next(iter(given)))
    names = list(given)
    arrays = [picked, *given.values(), *mixed_parts]
    ranks, groups = lax.axis_size(TP), lax.axis_size(DP)
    count, width = shown.attended.shape
    local, model = shown.inputs.shape
    number = shown.weights.shape[0]
    half = shown.keys.shape[2]
    space = NAD * RANK
    adapters = NAD // ranks
    lines, share = space // groups, model // groups
    wides = [width] * 3 + [2 * half] + [width] * 5
    tall = [adapters * 2 * RANK, adapters * 3 * RANK]
    vmem = dict(
        pick_in=((ranks, number, count), BF16),
        dense=((NKEYS, count), F32),
        grad_query=((count, 2 * half), BF16),
        normed_out=((ranks, local, model), BF16),
        normed_in=((ranks, local, model), BF16),
        three_in=((ranks, 2 * RANK, count), BF16),
        four_in=((ranks, RANK, count), BF16),
        three_sum=((2 * RANK, count), BF16),
        four_sum=((RANK, count), BF16),
        attended_out=((local, model), BF16),
        attended_in=((ranks, local, width), BF16),
        branch_out=((local, model), BF16),
        branch_in=((ranks, local, width), BF16),
        back_in=((ranks, RANK, local), BF16),
        grad_middle=((local, model), F32),
        grads=((count, 3 * width), BF16),
        key_sum=((2, count, HD), F32),
        value_sum=((2, count, HD), F32),
        input_out=((ranks, local, model), BF16),
        input_in=((ranks, local, model), BF16),
        one_in=((ranks, 3 * RANK, count), BF16),
        one_sum=((3 * RANK, count), BF16),
        ups_out=((groups, lines, sum(wides)), BF16),
        memory_out=((groups, tall[0], share), BF16),
        down_out=((groups, tall[1], share), BF16),
        outputs=((local, model), BF16),
        input_grad=((local, model), F32),
    )
    inputs = arrays[1:]
    results = [
        ((local, model), BF16),
        ((local, model), F32),
        ((groups, lines, sum(wides)), BF16),
        ((groups, tall[0], share), BF16),
        ((groups, tall[1], share), BF16),
    ]

    def body(*refs):
        outs = refs[len(arrays) : len(arrays) + len(results)]
        rest = refs[len(arrays) + len(results) :]
        v = types.SimpleNamespace(**dict(zip(vmem, rest[len(inputs) :])))
        loaded, saved, send, recv, far_send, far_recv = rest[len(inputs) + len(vmem) :]
        rank, group = lax.axis_index(TP), lax.axis_index(DP)
        barrier = pltpu.get_barrier_semaphore()
        for d in range(1, ranks):
            pl.semaphore_signal(
                barrier,
                inc=1,
                device_id={TP: lax.rem(rank + d, ranks)},
                device_id_type=MESH,
            )

        @pl.loop(1, groups)
        def _(d):
            pl.semaphore_signal(
                barrier,
                inc=1,
                device_id={DP: lax.rem(group + d, groups)},
                device_id_type=MESH,
            )

        loads = [
            pltpu.make_async_copy(
                refs[i + 1].at[rank] if x is shown.picks else refs[i + 1], rest[i], loaded.at[i]
            )
            for i, x in enumerate(inputs)
        ]
        for load in loads:
            load.start()
        need = Waited(names, rest, loads)

        def near(i, d, src, dst):
            return pltpu.make_async_remote_copy(
                src_ref=src,
                dst_ref=dst,
                send_sem=send.at[i, d],
                recv_sem=recv.at[i, d],
                device_id={TP: lax.rem(rank + d, ranks)},
                device_id_type=MESH,
            )

        def far(i, d, src, dst):
            return pltpu.make_async_remote_copy(
                src_ref=src,
                dst_ref=dst,
                send_sem=far_send.at[i, d],
                recv_sem=far_recv.at[i, d],
                device_id={DP: lax.rem(group + d, groups)},
                device_id_type=MESH,
            )

        def far_piece(i, d, ref):
            return far(i, d, ref.at[lax.rem(group + d, groups)], outs[2 + i].at[group])

        def send_far(i, ref):
            @pl.loop(1, groups)
            def _(d):
                far_piece(i, d, ref).start()

            keep = pltpu.make_async_copy(ref.at[group], outs[2 + i].at[group], saved.at[2 + i])
            keep.start()
            return keep

        def shared(i, ref):
            return [near(i, d, ref.at[rank], ref.at[rank]) for d in range(1, ranks)]

        def columns(ref, p):
            return ref.at[:, pl.ds(pl.multiple_of(p * width, width), width)]

        def split(i, src, dst):
            return [
                near(i, d, columns(src, lax.rem(rank + d, ranks)), dst.at[rank])
                for d in range(1, ranks)
            ]

        def total(ref):
            return sum(ref[p].astype(F32) for p in range(ranks))

        own_tokens = pl.ds(pl.multiple_of(rank * local, local), local)
        own_columns_at = pl.ds(pl.multiple_of(rank * width, width), width)

        pick_in = v.pick_in
        own_pick = pltpu.make_async_copy(refs[0].at[rank], pick_in.at[rank], saved.at[0])
        own_pick.start()
        pl.semaphore_wait(barrier, ranks + groups - 2)
        picks_sent = [
            near(0, d, refs[0].at[lax.rem(rank + d, ranks)], pick_in.at[rank])
            for d in range(1, ranks)
        ]
        for c in picks_sent:
            c.start()
        weights_ref, keys_ref, picks_ref = need.weights, need.keys, need.picks
        own_pick.wait()
        for c in picks_sent:
            c.wait()

        slot = lax.broadcasted_iota(I32, (NKEYS, block), 0)
        for part in range(2):

            @pl.loop(0, count // block)
            def _(c):
                lanes = pl.ds(pl.multiple_of(c * block, block), block)
                weight = weights_ref[:, lanes]
                grad = sum(pick_in[p, :, lanes].astype(F32) for p in range(ranks))
                grad = weight * (grad - jnp.sum(grad * weight, axis=0, keepdims=True))
                grad = grad * (2 * half) ** -0.5
                dense = jnp.zeros((NKEYS, block), F32)
                for k in range(number):
                    hit = slot == picks_ref[part, k : k + 1, lanes]
                    dense += jnp.where(hit, grad[k : k + 1, :], 0.0)
                v.dense[:, lanes] = dense

            top, low = two_parts(v.dense[...])
            v.grad_query[:, part * half : (part + 1) * half] = (
                tm(top, keys_ref[part]) + tm(low, keys_ref[part])
            ).astype(BF16)

        query_ref, gate_ref, ups_ref = need.query, need.gate, need.ups
        grad_gate_ref, mixed_ref, owner_ref = need.grad_gate, need.mixed, need.owner
        normed_sent = []
        for d in [ranks // 2] + [d for d in range(1, ranks) if d != ranks // 2] + [0]:
            at = pl.ds(pl.multiple_of(lax.rem(rank + d, ranks) * local, local), local)
            asked, gates, own = v.grad_query[at, :], grad_gate_ref[at, :], owner_ref[at, :]
            part = (mt(asked, query_ref[...]) + mt(gates, gate_ref[...])).astype(BF16)
            if d:
                v.normed_out[d] = part
                normed_sent.append(near(1, d, v.normed_out.at[d], v.normed_in.at[rank]))
                normed_sent[-1].start()
            else:
                v.normed_in[rank] = part
            three = jnp.concatenate(
                [mt(asked, ups_ref[:, query_spot]), mt(gates, ups_ref[:, gate_spot])], axis=1
            )
            v.three_in[rank, :, at] = shorten(masked(three, own))
            v.four_in[rank, :, at] = shorten(
                masked(mt(mixed_ref[at, :], ups_ref[:, low_spot]), own)
            )
        short_sent = shared(2, v.three_in) + shared(3, v.four_in)
        for c in short_sent:
            c.start()
        owner_own = need.owner_own[...]
        middle_ref, cotangent_ref, gain_two = need.middle, need.cotangent, need.gain_two
        down_ref, out_ref, attend_ref = need.down_memory, need.out_t, need.attend_t
        mixed_refs = []
        for i in range(len(names), len(inputs)):
            loads[i].wait()
            mixed_refs.append(rest[i])
        for c in normed_sent + short_sent:
            c.wait()

        v.three_sum[...] = total(v.three_in).astype(BF16)
        v.four_sum[...] = total(v.four_in).astype(BF16)
        grad_three = lengthen(v.three_sum[:, own_tokens], owner_own)
        upstream = total(v.normed_in) + mt(grad_three, down_ref[...])
        grad = cotangent_ref[...].astype(F32) + rms_backward(
            middle_ref[...], gain_two[...].astype(F32)[None, :], upstream
        )
        v.grad_middle[...] = grad
        branch = grad.astype(BF16)
        v.branch_out[...] = branch
        low = masked(mt(branch, ups_ref[:, attend_spot]), owner_own)
        v.attended_out[...] = (mm(branch, out_ref[...]) + mm(low, attend_ref[...])).astype(BF16)
        v.back_in[rank] = shorten(low)
        v.attended_in[rank] = v.attended_out[:, own_columns_at]
        v.branch_in[rank] = v.branch_out[:, own_columns_at]
        attended_sent = split(4, v.attended_out, v.attended_in)
        later_sent = shared(5, v.back_in) + split(6, v.branch_out, v.branch_in)
        for c in attended_sent:
            c.start()

        low_four = lengthen(v.four_sum[:, own_tokens], owner_own)
        v.outputs[...] = (
            middle_ref[...]
            + sum(ref[...].astype(F32) for ref in mixed_refs)
            + mm(low_four, ups_ref[:, mixed_spot])
        ).astype(BF16)
        stores = [pltpu.make_async_copy(v.outputs, outs[0], saved.at[0])]
        stores[0].start()
        owner = owner_ref[...]
        starts = [sum(wides[:i]) for i in range(len(wides))]

        def put(i, left, rows):
            found = tm(left, rows).astype(F32)
            for g in range(groups):
                v.ups_out[g, :, starts[i] : starts[i] + wides[i]] = found[
                    g * lines : (g + 1) * lines
                ].astype(BF16)

        def put_down(out_ref, short, normed_ref):
            spread = own_columns(short, owner, rank * adapters)
            step = max(share, 128)
            for c in range(model // step):
                found = tm(spread, normed_ref[:, c * step : (c + 1) * step]).astype(BF16)
                for p in range(step // share):
                    out_ref[c * (step // share) + p] = found[:, p * share : (p + 1) * share]

        low_three = need.low_three
        put(3, low_three[:, :space], v.grad_query[...])
        put(4, low_three[:, space:], grad_gate_ref[...])
        put(5, lengthen(v.four_sum[...], owner), need.own_cotangent[...])
        put(7, need.low_four_back[...], mixed_ref[...])
        put_down(v.memory_out, v.three_sum[...], need.normed_rows)
        memory_kept = send_far(1, v.memory_out)
        projected_ref, across_ref, below_ref = need.projected, need.across, need.below
        weight_ref = need.full_in
        for c in attended_sent:
            c.wait()
        for c in later_sent:
            c.start()

        @pl.loop(0, width // (2 * HD))
        def _(pair):
            queries, keys, values = [projected_ref[:, wide_lanes(pair, p * width)] for p in range(3)]
            above = jnp.concatenate(
                [v.attended_in[p, :, wide_lanes(pair)] for p in range(ranks)], axis=0
            )
            v.key_sum[...] = jnp.zeros_like(v.key_sum)
            v.value_sum[...] = jnp.zeros_like(v.value_sum)
            for r in range(count // block):
                at, top = slice(r * block, (r + 1) * block), (r + 1) * block
                parts = []
                for h in range(2):
                    lanes = slice(h * HD, (h + 1) * HD)
                    probs = block_probs(
                        queries[:, lanes], keys[:, lanes], across_ref, below_ref, r, block
                    )
                    grad_probs = mt(above[at, lanes], values[:top, lanes])
                    inner = jnp.sum(probs * grad_probs, axis=-1, keepdims=True)
                    grad_scores = (probs * (grad_probs - inner)).astype(BF16)
                    parts.append(mm(grad_scores, keys[:top, lanes]))
                    v.key_sum[h, :top, :] += tm(grad_scores, queries[at, lanes])
                    v.value_sum[h, :top, :] += tm(probs.astype(BF16), above[at, lanes])
                v.grads[at, wide_lanes(pair)] = (
                    jnp.concatenate(parts, axis=1) * HD**-0.5
                ).astype(BF16)
            v.grads[:, wide_lanes(pair, width)] = (
                jnp.concatenate([v.key_sum[0], v.key_sum[1]], axis=1) * HD**-0.5
            ).astype(BF16)
            v.grads[:, wide_lanes(pair, 2 * width)] = jnp.concatenate(
                [v.value_sum[0], v.value_sum[1]], axis=1
            ).astype(BF16)

        input_sent = []
        for d in [ranks // 2] + [d for d in range(1, ranks) if d != ranks // 2] + [0]:
            at = pl.ds(pl.multiple_of(lax.rem(rank + d, ranks) * local, local), local)
            part = mt(v.grads[at, :], weight_ref[...]).astype(BF16)
            if d:
                v.input_out[d] = part
                input_sent.append(near(7, d, v.input_out.at[d], v.input_in.at[rank]))
                input_sent[-1].start()
            else:
                v.input_in[rank] = part
            one = jnp.concatenate(
                [
                    mt(
                        v.grads[at, p * width : (p + 1) * width],
                        ups_ref[:, p * width : (p + 1) * width],
                    )
                    for p in range(3)
                ],
                axis=1,
            )
            v.one_in[rank, :, at] = shorten(masked(one, owner_ref[at, :]))
        one_sent = shared(8, v.one_in)
        for c in one_sent:
            c.start()
        for c in later_sent:
            c.wait()
        low_one = need.low_one
        for p in range(3):
            put(
                p,
                low_one[:, p * space : (p + 1) * space],
                v.grads[:, p * width : (p + 1) * width],
            )
        put(6, lengthen(side_by_side(v.back_in), owner), need.attended[...])
        put(
            8,
            lengthen(side_by_side(need.two_short), owner),
            jnp.concatenate([v.branch_in[p] for p in range(ranks)], axis=0),
        )
        ups_kept = send_far(0, v.ups_out)
        down_input_ref, rows_ref, gain_one = need.down_input, need.inputs, need.gain_one
        normed_one_ref = need.normed_one
        for c in one_sent:
            c.wait()
        v.one_sum[...] = total(v.one_in).astype(BF16)
        put_down(v.down_out, v.one_sum[...], normed_one_ref)
        down_kept = send_far(2, v.down_out)
        for c in input_sent:
            c.wait()
        low = lengthen(v.one_sum[:, own_tokens], owner_own)
        upstream = total(v.input_in) + mt(low, down_input_ref[...])
        v.input_grad[...] = v.grad_middle[...] + rms_backward(
            rows_ref[...].astype(F32), gain_one[...].astype(F32)[None, :], upstream
        )
        stores.append(pltpu.make_async_copy(v.input_grad, outs[1], saved.at[1]))
        stores[1].start()

        @pl.loop(1, groups)
        def _(d):
            for i, ref in enumerate((v.ups_out, v.memory_out, v.down_out)):
                far_piece(i, d, ref).wait()

        for c in stores + [ups_kept, memory_kept, down_kept]:
            c.wait()

    near_sems = pltpu.SemaphoreType.DMA((9, ranks))
    far_sems = pltpu.SemaphoreType.DMA((3, groups))
    return wides, pl.pallas_call(
        body,
        out_shape=[jax.ShapeDtypeStruct(shape, dtype) for shape, dtype in results],
        in_specs=[ANY] * len(arrays),
        out_specs=[ANY] * len(results),
        scratch_shapes=[
            pltpu.VMEM(x.shape[1:] if x is shown.picks else x.shape, x.dtype) for x in inputs
        ]
        + [pltpu.VMEM(shape, dtype) for shape, dtype in vmem.values()]
        + [
            pltpu.SemaphoreType.DMA((len(inputs),)),
            pltpu.SemaphoreType.DMA((5,)),
            near_sems,
            near_sems,
            far_sems,
            far_sems,
        ],
        compiler_params=pltpu.CompilerParams(
            collective_id=cid, has_side_effects=True, vmem_limit_bytes=61 << 20
        ),
    )(*arrays)


def forward(given, table, key_picks, spots, cid, block=128, sub=32, conv=32):
    _, query_spot, gate_spot, attend_spot, mixed_spot, low_spot = spots
    shown = types.SimpleNamespace(**given)
    names = list(given)
    local_arrays = list(given.values())
    ranks, groups = lax.axis_size(TP), lax.axis_size(DP)
    local, model = shown.inputs.shape
    count = shown.owner.shape[0]
    width = shown.gate.shape[1]
    half = shown.keys.shape[2]
    number = key_picks.shape[2]
    picks = key_picks.shape[0] * number
    space = NAD * RANK
    rows = table.shape[0]
    piece = rows // 2
    blocks = 2 * groups
    stride = sub + 1
    chips = groups // 2
    relayed = chips == 4
    hops = max(chips, 4)
    tree = [
        shown.flat_in,
        shown.down_input,
        shown.ups,
        shown.out_t,
        shown.attend_t,
        shown.query,
        shown.gate,
        shown.down_memory,
        shown.mixed_t,
    ]
    early, nested, late = (0, 1, 2), (3, 4), (5, 6, 7, 8)
    cuts = 2
    chunks = tuple(range(len(tree), len(tree) + cuts))
    tree_shapes = [
        (x.shape[0], x.shape[1] * (ranks if a in nested else 1)) for a, x in enumerate(tree)
    ]
    full = [((groups, *shape), BF16) for shape in tree_shapes]
    results = dict(
        normed_one=((count, model), BF16),
        low_one=((count, 3 * space), BF16),
        projected=((count, 3 * width), BF16),
        attended=((count, width), BF16),
        middle=((local, model), F32),
        two_short=((ranks, RANK, local), BF16),
        normed_rows=((count, model), BF16),
        low_three=((count, 2 * space), BF16),
        weights=((number, count), F32),
        mixed=((count, width), BF16),
        grad_recalled=((count, width), BF16),
        grad_gate=((count, width), BF16),
        scale=((count, 1), F32),
        low_four_back=((count, space), BF16),
        own_cotangent=((count, width), BF16),
        first=((count, picks), I32),
        second=((count, picks), I32),
        block_0=((local, model), BF16),
        block_1=((local, model), BF16),
        block_2=((local, model), BF16),
        block_3=((local, model), BF16),
    )
    vmem = dict(
        rows_in=((ranks, local, model), BF16),
        cotangent_in=((ranks, local, model), BF16),
        out_stage=(tree_shapes[3], BF16),
        attend_stage=(tree_shapes[4], BF16),
        attended_in=((local, model), BF16),
        normed_two=((local, model), BF16),
        asked=((count, 2 * half), F32),
        every=((NKEYS, count), F32),
        gate_pre=((count, width), F32),
        narrow=((ranks, number, count), BF16),
        grad_mixed=((count, width), F32),
        picks=(key_picks.shape, I32),
        by_token=((count, picks), F32),
        low=((NKEYS * stride + sub, 128), F32),
        high=((NKEYS * stride + sub, 128), F32),
        spread=((2, sub, NKEYS * NKEYS), BF16),
        dense_in=((2, count, piece), BF16),
        table_in=((2, piece, width), BF16),
        total=((count, width), F32),
        largest=((8, 1), F32),
    )
    outs = [
        *full,
        *results.values(),
        ((groups, rows, width), BF16),
        ((count, NKEYS * NKEYS), BF16),
    ]

    def body(*refs):
        inputs = refs[: len(names) + 2]
        out_refs = refs[len(inputs) : len(inputs) + len(outs)]
        rest = list(refs[len(inputs) + len(outs) :])

        def take(n):
            taken = rest[:n]
            del rest[:n]
            return taken

        held = take(len(names))
        gathered = take(len(tree))
        r = types.SimpleNamespace(**dict(zip(results, take(len(results)))))
        v = types.SimpleNamespace(**dict(zip(vmem, take(len(vmem)))))
        loaded, kept, stored, near_send, near_recv, tree_send, tree_recv, pass_send, pass_recv = rest[:9]
        moved = rest[9]
        table_ref, picks_ref = inputs[-2:]
        table_out, dense_out = out_refs[-2:]
        rank, group = lax.axis_index(TP), lax.axis_index(DP)
        barrier = pltpu.get_barrier_semaphore()
        for d in range(1, ranks):
            pl.semaphore_signal(
                barrier,
                inc=1,
                device_id={TP: lax.rem(rank + d, ranks)},
                device_id_type=MESH,
            )

        @pl.loop(1, groups)
        def _(d):
            pl.semaphore_signal(
                barrier,
                inc=1,
                device_id={DP: lax.rem(group + d, groups)},
                device_id_type=MESH,
            )

        loads = [
            pltpu.make_async_copy(inputs[i], held[i], loaded.at[i]) for i in range(len(names))
        ]
        loads.append(pltpu.make_async_copy(picks_ref, v.picks, loaded.at[len(names)]))
        for load in loads:
            load.start()
        need = Waited(names, held, loads)
        raw = types.SimpleNamespace(**dict(zip(names, inputs)))

        def near(i, d, src, dst):
            return pltpu.make_async_remote_copy(
                src_ref=src,
                dst_ref=dst,
                send_sem=near_send.at[i, d],
                recv_sem=near_recv.at[i, d],
                device_id={TP: lax.rem(rank + d, ranks)},
                device_id_type=MESH,
            )

        def columns(ref, p, wide):
            return ref.at[:, pl.ds(pl.multiple_of(p * wide, wide), wide)]

        def way(a):
            return 1 if a - len(tree) < cuts // 2 else 2

        def cut_of(a):
            return pl.ds((a - len(tree)) * (rows // cuts), rows // cuts)

        def source(a):
            if a in chunks:
                return table_ref.at[cut_of(a)]
            if a in nested:
                return (v.out_stage, v.attend_stage)[a - 3]
            return inputs[names.index(given_names[a])]

        given_names = [names[i] for i in tree_names]

        def place(a, p):
            if a in chunks:
                return table_out.at[p, cut_of(a)]
            return gathered[a].at[p]

        def partner(d):
            if not relayed:
                return lax.rem(group + 2 * d, groups)
            across = 2 - 4 * lax.rem(lax.div(group, 2), 2) if d & 1 else 0
            along = 4 - 8 * lax.div(group, 4) if d & 2 else 0
            return group + across + along

        def holder(d):
            if isinstance(d, int) and d == 0:
                return group
            return partner(d) if relayed else lax.rem(group - 2 * d + groups, groups)

        def to_chip(a, d):
            relay = relayed and a in chunks and d == 3
            shard = place(a, holder(way(a))) if relay else source(a)
            return pltpu.make_async_remote_copy(
                src_ref=shard,
                dst_ref=shard if relay else place(a, group),
                send_sem=tree_send.at[a, d],
                recv_sem=tree_recv.at[a, d],
                device_id={DP: partner(3 - way(a) if relay else d)},
                device_id_type=MESH,
            )

        def to_sibling(a, d):
            first = isinstance(d, int) and d == 0
            return pltpu.make_async_remote_copy(
                src_ref=source(a) if first else place(a, holder(d)),
                dst_ref=place(a, holder(d)),
                send_sem=pass_send.at[a, d],
                recv_sem=pass_recv.at[a, d],
                device_id={DP: group + 1 - 2 * lax.rem(group, 2)},
                device_id_type=MESH,
            )

        def own_copy(a):
            return pltpu.make_async_copy(source(a), place(a, group), kept.at[a])

        def begin(chosen):
            for a in chosen:
                own_copy(a).start()
                if relayed:
                    for d in range(1, 4):
                        to_chip(a, d).start()
                else:

                    @pl.loop(1, chips)
                    def _(d):
                        to_chip(a, d).start()

                to_sibling(a, 0).start()

        def begin_table(chosen):
            if not relayed:
                begin(chosen)
                return
            for a in chosen:
                to_chip(a, way(a)).start()
                own_copy(a).start()
                to_sibling(a, 0).start()

        def rest_of_table(chosen):
            if relayed:
                for a in chosen:
                    to_chip(a, 3 - way(a)).start()

        def onward(a, d):
            to_chip(a, d).wait_recv()
            to_sibling(a, d).start()

        def other(chosen):
            if relayed:
                for a in chosen:
                    onward(a, 3 - way(a))

        def last(chosen):
            for a in chosen:
                if relayed:
                    onward(a, 3)
                else:

                    @pl.loop(1, chips)
                    def _(d):
                        onward(a, d)

        def collect(chosen):
            if relayed:
                for d in range(1, 3):
                    for a in chosen:
                        onward(a, d)
            last(chosen)

        def settle(chosen):
            for a in chosen:
                own_copy(a).wait()
                to_sibling(a, 0).wait()
                if relayed:
                    for d in range(1, 4):
                        to_sibling(a, d).wait()
                        to_chip(a, d).wait_send()
                else:

                    @pl.loop(1, chips)
                    def _(d):
                        to_sibling(a, d).wait()
                        to_chip(a, d).wait_send()

        stores = []

        def store(src, dst):
            stores.append(pltpu.make_async_copy(src, dst, stored.at[len(stores)]))
            stores[-1].start()

        def store_trees(chosen):
            for a in chosen:
                store(gathered[a], out_refs[a])

        result_refs = dict(zip(results, out_refs[len(tree) :]))

        def flat(ref):
            return ref[...].reshape(-1, ref.shape[2])

        def done(ref):
            for name in results:
                if getattr(r, name) is ref:
                    store(ref, result_refs[name])

        pl.semaphore_wait(barrier, ranks + groups - 2)
        homes = []
        for i, (src, dst) in enumerate(((raw.inputs, v.rows_in), (raw.cotangent, v.cotangent_in))):
            homes.append(pltpu.make_async_copy(src, dst.at[rank], moved.at[i]))
        for i, (src, dst) in enumerate(((raw.out_t, v.out_stage), (raw.attend_t, v.attend_stage))):
            homes.append(
                pltpu.make_async_copy(src, columns(dst, rank, src.shape[1]), moved.at[2 + i])
            )
        for c in homes:
            c.start()
        nest_sent = [
            near(i, d, src, columns(dst, rank, src.shape[1]))
            for i, src, dst in ((0, raw.out_t, v.out_stage), (1, raw.attend_t, v.attend_stage))
            for d in range(1, ranks)
        ]
        rows_sent = [near(2, d, raw.inputs, v.rows_in.at[rank]) for d in range(1, ranks)]
        back_sent = [near(3, d, raw.cotangent, v.cotangent_in.at[rank]) for d in range(1, ranks)]
        for c in nest_sent + rows_sent:
            c.start()
        begin(early)
        begin(late)
        for c in nest_sent:
            c.wait()
        homes[2].wait()
        homes[3].wait()
        begin(nested)
        begin_table(chunks)
        gain_one, owner_ref = need.gain_one, need.owner
        homes[0].wait()
        for c in rows_sent:
            c.wait()
        for c in range(ranks):
            r.normed_one[c * local : (c + 1) * local, :] = rms_forward(
                v.rows_in[c].astype(F32), gain_one[...].astype(F32)[None, :]
            ).astype(BF16)
        done(r.normed_one)
        for c in back_sent:
            c.start()
        collect(early)
        settle(early)
        store_trees(early)
        weight_ref, down_ref, ups_ref = gathered[:3]

        def up(spot):
            return ups_ref[:, :, spot].reshape(space, -1)

        @pl.loop(0, ranks)
        def _(c):
            at = pl.ds(pl.multiple_of(c * local, local), local)
            normed = r.normed_one[at, :]
            low = masked(mm(normed, flat(down_ref)), owner_ref[at, :])
            r.low_one[at, :] = low
            for p in range(3):
                lanes = slice(p * width, (p + 1) * width)
                r.projected[at, lanes] = (
                    mm(normed, weight_ref[:, :, lanes].reshape(model, width))
                    + mm(low[:, p * space : (p + 1) * space], up(lanes))
                ).astype(BF16)

        across_ref, below_ref = need.across, need.below

        @pl.loop(0, width // (2 * HD))
        def _(pair):
            queries, keys, values = [r.projected[:, wide_lanes(pair, p * width)] for p in range(3)]
            for q in range(count // block):
                top = (q + 1) * block
                parts = []
                for lanes in (slice(0, HD), slice(HD, 2 * HD)):
                    probs = block_probs(
                        queries[:, lanes], keys[:, lanes], across_ref, below_ref, q, block
                    )
                    parts.append(mm(probs.astype(BF16), values[:top, lanes]))
                r.attended[q * block : top, wide_lanes(pair)] = jnp.concatenate(
                    parts, axis=1
                ).astype(BF16)

        def lines_of(p):
            return r.attended.at[pl.ds(pl.multiple_of(p * local, local), local)]

        attended_sent = [
            near(4, d, lines_of(lax.rem(rank + d, ranks)), columns(v.attended_in, rank, width))
            for d in range(1, ranks)
        ]
        for c in attended_sent:
            c.start()
        rest_of_table(chunks)
        own_rows = pl.ds(pl.multiple_of(rank * local, local), local)
        v.attended_in[:, pl.ds(pl.multiple_of(rank * width, width), width)] = r.attended[own_rows, :]
        done(r.low_one)
        done(r.projected)
        done(r.attended)
        collect(nested)
        settle(nested)
        store_trees(nested)
        out_ref, attend_ref = gathered[3:5]
        residual_ref, gain_two, owner_own = need.inputs, need.gain_two, need.owner_own[...]
        for c in attended_sent:
            c.wait()
        low = masked(mt(v.attended_in[...], flat(attend_ref)), owner_own)
        middle = (
            residual_ref[...].astype(F32)
            + mt(v.attended_in[...], flat(out_ref))
            + mm(low, up(attend_spot))
        )
        r.middle[...] = middle
        normed = rms_forward(middle, gain_two[...].astype(F32)[None, :]).astype(BF16)
        v.normed_two[...] = normed
        r.normed_rows[own_rows, :] = normed
        r.two_short[rank] = shorten(low)
        normed_sent = [
            near(5, d, v.normed_two, r.normed_rows.at[own_rows]) for d in range(1, ranks)
        ] + [near(6, d, r.two_short.at[rank], r.two_short.at[rank]) for d in range(1, ranks)]
        for c in normed_sent:
            c.start()
        done(r.middle)
        loads[-1].wait()
        r.first[...] = jnp.concatenate(
            [v.picks[m, 0] for m in range(key_picks.shape[0])], axis=0
        ).T
        r.second[...] = jnp.concatenate(
            [v.picks[m, 1] for m in range(key_picks.shape[0])], axis=0
        ).T
        done(r.first)
        done(r.second)
        collect(late)
        settle(late)
        store_trees(late)
        query_ref, gate_ref, memory_ref, mixed_ref = gathered[5:]
        homes[1].wait()
        for c in back_sent:
            c.wait()
        own_lanes = pl.ds(pl.multiple_of(rank * width, width), width)
        for c in range(ranks):
            at = slice(c * local, (c + 1) * local)
            r.own_cotangent[at, :] = v.cotangent_in[c, :, own_lanes]
            low = masked(mt(v.cotangent_in[c], up(mixed_spot)), owner_ref[at, :])
            r.low_four_back[at, :] = low
            v.grad_mixed[at, :] = mm(v.cotangent_in[c], flat(mixed_ref)) + mm(low, up(low_spot))
        done(r.own_cotangent)
        done(r.low_four_back)
        keys_ref = need.keys
        for c in normed_sent:
            c.wait()
        if relayed:
            for a in chunks:
                onward(a, way(a))
                to_chip(a, 3).start()
        done(r.normed_rows)
        done(r.two_short)

        @pl.loop(0, ranks)
        def _(c):
            at = pl.ds(pl.multiple_of(c * local, local), local)
            normed = r.normed_rows[at, :]
            low = masked(mm(normed, flat(memory_ref)), owner_ref[at, :])
            r.low_three[at, :] = low
            v.asked[at, :] = mm(normed, flat(query_ref)) + mm(low[:, :space], up(query_spot))
            v.gate_pre[at, :] = mm(normed, flat(gate_ref)) + mm(low[:, space:], up(gate_spot))

        done(r.low_three)
        slot = lax.broadcasted_iota(I32, (NKEYS, block), 0)
        for part in range(2):
            top, low = two_parts(v.asked[:, part * half : (part + 1) * half])
            v.every[...] = mt(keys_ref[part], top) + mt(keys_ref[part], low)

            @pl.loop(0, count // block)
            def _(c):
                lanes = pl.ds(pl.multiple_of(c * block, block), block)
                scores = v.every[:, lanes]
                found = []
                for k in range(number):
                    hit = slot == v.picks[rank, part, k : k + 1, lanes]
                    found.append(jnp.sum(jnp.where(hit, scores, 0.0), axis=0, keepdims=True))
                found = jnp.concatenate(found, axis=0)
                if part == 0:
                    r.weights[:, lanes] = found
                else:
                    added = (r.weights[:, lanes] + found) * (2 * half) ** -0.5
                    raised = jnp.exp(added - jnp.max(added, axis=0, keepdims=True))
                    weights = raised / jnp.sum(raised, axis=0, keepdims=True)
                    r.weights[:, lanes] = weights
                    v.narrow[rank, :, lanes] = weights.astype(BF16)

        narrow_sent = [
            near(7, d, v.narrow.at[rank], v.narrow.at[rank]) for d in range(1, ranks)
        ]
        for c in narrow_sent:
            c.start()
        done(r.weights)
        for c in narrow_sent:
            c.wait()
        v.by_token[...] = (
            jnp.concatenate([v.narrow[p] for p in range(ranks)], axis=0).astype(F32).T
        )

        wide_slot = lax.broadcasted_iota(I32, (NKEYS, picks), 0)
        steps = count // sub

        def spread_out(t, s):
            return pltpu.make_async_copy(
                v.spread.at[s],
                dense_out.at[pl.ds(pl.multiple_of(t * sub, sub), sub)],
                moved.at[4 + s],
            )

        @pl.loop(0, steps)
        def _(t):
            s = lax.rem(t, 2)
            at = pl.ds(pl.multiple_of(t * sub, sub), sub)
            firsts, seconds, weights = r.first[at, :], r.second[at, :], v.by_token[at, :]
            for n in range(sub):
                b = jnp.where(wide_slot == seconds[n : n + 1], 1.0, 0.0).astype(BF16)
                a = jnp.where(wide_slot == firsts[n : n + 1], weights[n : n + 1], 0.0).astype(BF16)
                both = mt(a, b)
                v.low[pl.ds(n, NKEYS, stride=stride), :] = both[:, :128]
                v.high[pl.ds(n, NKEYS, stride=stride), :] = both[:, 128:]

            @pl.when(t >= 2)
            def _():
                spread_out(t - 2, s).wait()

            @pl.loop(0, NKEYS // conv)
            def _(c):
                for q in range(conv):
                    i = c * conv + q
                    lanes = pl.multiple_of(i * NKEYS, NKEYS)
                    lines = pl.ds(i * stride, sub)
                    v.spread[s, :, pl.ds(lanes, 128)] = v.low[lines, :].astype(BF16)
                    v.spread[s, :, pl.ds(lanes + 128, 128)] = v.high[lines, :].astype(BF16)

            spread_out(t, s).start()

            @pl.when(t == steps - 7)
            def _():
                other(chunks)

        spread_out(steps - 2, steps % 2).wait()
        spread_out(steps - 1, (steps - 1) % 2).wait()

        def block_at(b):
            if not relayed:
                return lax.div(b, 2), lax.rem(b, 2)
            d = lax.div(b, 4)
            across = (2 - 4 * lax.rem(lax.div(group, 2), 2)) * lax.rem(d, 2)
            along = (4 - 8 * lax.div(group, 4)) * lax.div(d, 2)
            near_by = (1 - 2 * lax.rem(group, 2)) * lax.rem(lax.div(b, 2), 2)
            return group + across + along + near_by, lax.rem(b, 2)

        def fetch(b, s):
            p, h = block_at(b)
            return (
                pltpu.make_async_copy(
                    dense_out.at[:, pl.ds(pl.multiple_of((p * 2 + h) * piece, piece), piece)],
                    v.dense_in.at[s],
                    moved.at[6 + s],
                ),
                pltpu.make_async_copy(
                    table_out.at[p, pl.ds(pl.multiple_of(h * piece, piece), piece)],
                    v.table_in.at[s],
                    moved.at[8 + s],
                ),
            )

        def arrived(d):
            for a in chunks:
                if isinstance(d, int) and d == 0:
                    own_copy(a).wait()
                to_sibling(a, d).wait_recv()

        arrived(0)
        if relayed:
            arrived(1)
            arrived(2)
        else:
            last(chunks)

            @pl.loop(1, chips)
            def _(d):
                arrived(d)

        v.total[...] = jnp.zeros_like(v.total)
        v.largest[...] = jnp.zeros_like(v.largest)
        for c in fetch(0, 0):
            c.start()

        @pl.loop(0, blocks)
        def _(b):
            s = lax.rem(b, 2)
            if relayed:

                @pl.when(b == 11)
                def _():
                    last(chunks)

                @pl.when(b == 13)
                def _():
                    arrived(3)

            @pl.when(b + 1 < blocks)
            def _():
                for c in fetch(b + 1, 1 - s):
                    c.start()

            for c in fetch(b, s):
                c.wait()
            v.total[...] += mm(v.dense_in[s], v.table_in[s])
            peak = v.largest[...]
            for c in range(piece // 512):
                values = v.table_in[s, c * 512 : (c + 1) * 512, :].astype(F32)
                squares = values * values
                norms = jnp.sum(squares[:, :128] + squares[:, 128:], axis=1, keepdims=True)
                peak = jnp.maximum(peak, jnp.max(norms.reshape(-1, 8, 1), axis=0))
            v.largest[...] = peak

        gate, recalled, upstream = v.gate_pre[...], v.total[...], v.grad_mixed[...]
        sigmoid = 1.0 / (1.0 + jnp.exp(-gate))
        act = gate * sigmoid
        r.mixed[...] = (act * recalled).astype(BF16)
        grad = (upstream * act).astype(BF16)
        r.grad_recalled[...] = grad
        r.grad_gate[...] = (
            upstream * recalled * sigmoid * (1.0 + gate * (1.0 - sigmoid))
        ).astype(BF16)
        wide = grad.astype(F32)
        bound = jnp.max(v.largest[...]) * jnp.sum(wide * wide, axis=1, keepdims=True)
        r.scale[...] = 32000.0 * lax.rsqrt(jnp.maximum(bound, 1e-30))
        for ref in (r.mixed, r.grad_recalled, r.grad_gate, r.scale):
            done(ref)
        for d, ref in enumerate((r.block_0, r.block_1, r.block_2, r.block_3)):
            at = pl.ds(pl.multiple_of(lax.rem(rank + d, ranks) * local, local), local)
            ref[...] = mt(r.mixed[at, :], flat(mixed_ref)).astype(BF16)
            done(ref)
        for a in chunks:
            for d in range(4 if relayed else 1):
                to_sibling(a, d).wait_send()
            if relayed:
                for d in range(1, 4):
                    to_chip(a, d).wait_send()
            else:

                @pl.loop(1, chips)
                def _(d):
                    to_sibling(a, d).wait_send()
                    to_chip(a, d).wait_send()

        for name in names:
            getattr(need, name)
        for c in stores:
            c.wait()

    tree_names = [
        next(i for i, y in enumerate(local_arrays) if y is x) for x in tree
    ]
    arrays = [*local_arrays, table, key_picks]
    near_sems = pltpu.SemaphoreType.DMA((8, ranks))
    tree_sems = pltpu.SemaphoreType.DMA((len(tree) + cuts, hops))
    got = pl.pallas_call(
        body,
        out_shape=[jax.ShapeDtypeStruct(shape, dtype) for shape, dtype in outs],
        in_specs=[ANY] * len(arrays),
        out_specs=[ANY] * len(outs),
        scratch_shapes=[pltpu.VMEM(x.shape, x.dtype) for x in local_arrays]
        + [pltpu.VMEM(shape, dtype) for shape, dtype in full]
        + [pltpu.VMEM(shape, dtype) for shape, dtype in results.values()]
        + [pltpu.VMEM(shape, dtype) for shape, dtype in vmem.values()]
        + [
            pltpu.SemaphoreType.DMA((len(names) + 1,)),
            pltpu.SemaphoreType.DMA((len(tree) + cuts,)),
            pltpu.SemaphoreType.DMA((len(outs),)),
            near_sems,
            near_sems,
            tree_sems,
            tree_sems,
            tree_sems,
            tree_sems,
            pltpu.SemaphoreType.DMA((10,)),
        ],
        compiler_params=pltpu.CompilerParams(
            collective_id=cid, has_side_effects=True, vmem_limit_bytes=61 << 20
        ),
    )(*arrays)
    whole_arrays = [x.reshape(-1, x.shape[2]) for x in got[: len(tree)]]
    return whole_arrays, types.SimpleNamespace(**dict(zip(results, got[len(tree) :]))), got[-2]


def pick_grads(first, second, grads, scale, table):
    tokens, picks = first.shape
    width = grads.shape[1]
    per_block = 16
    rows = per_block * NKEYS
    blocks = table.shape[0] // rows

    def body(*refs):
        table_ref, out_ref, kept, sems = refs[4], refs[5], refs[6], refs[11]
        first_ref, second_ref, grads_ref, scale_ref = refs[7:11]
        step = pl.program_id(0)

        @pl.when(step == 0)
        def _():
            copies = [pltpu.make_async_copy(refs[i], refs[7 + i], sems.at[i]) for i in range(4)]
            for c in copies:
                c.start()
            kept[...] = jnp.zeros_like(kept)
            for c in copies:
                c.wait()

        own = first_ref[...]
        low = second_ref[...] & 127
        factor = jnp.broadcast_to(scale_ref[...], (tokens, 128))
        total = kept[...]
        for b in range(per_block):
            every = mt(grads_ref[...], table_ref[b * NKEYS : (b + 1) * NKEYS, :])
            packed = (every[:, 128:] * factor).astype(I32) * 65536 + (
                every[:, :128] * factor
            ).astype(I32)
            found = jnp.take_along_axis(packed, low, axis=1, mode="promise_in_bounds")
            total = jnp.where(own == step * per_block + b, found, total)
        kept[...] = total

        @pl.when(step == blocks - 1)
        def _():
            p = kept[...]
            right = lax.shift_right_arithmetic(lax.shift_left(p, 16), 16)
            left = lax.shift_right_arithmetic(p - right, 16)
            both = jnp.where(second_ref[...] >= 128, left, right).astype(F32) / factor
            out_ref[...] = both.T.astype(BF16)

    return pl.pallas_call(
        body,
        grid=(blocks,),
        out_shape=jax.ShapeDtypeStruct((picks, tokens), BF16),
        in_specs=[ANY] * 4 + [pl.BlockSpec((rows, width), lambda s: (s, 0))],
        out_specs=whole((picks, tokens)),
        scratch_shapes=[pltpu.VMEM((tokens, picks), I32)]
        + [pltpu.VMEM(x.shape, x.dtype) for x in (first, second, grads, scale)]
        + [pltpu.SemaphoreType.DMA((4,))],
        compiler_params=pltpu.CompilerParams(vmem_limit_bytes=61 << 20),
    )(first, second, grads, scale, table)


def by_part(down, parts):
    shaped = down.reshape(down.shape[0], NAD, parts, RANK).transpose(0, 2, 1, 3)
    return shaped.reshape(down.shape)


def add_up(inputs, plans, through):
    shapes = []
    for x, (axis, sizes) in zip(inputs, plans):
        for size in sizes:
            if isinstance(size, tuple):
                shapes.append((size[0], x.shape[1], size[1]))
            else:
                shapes.append((x.shape[1], size) if axis else (size, x.shape[2]))

    def body(*refs):
        outs = iter(refs[len(inputs) + len(through) :])
        for ref in refs[len(inputs) : len(inputs) + len(through)]:
            next(outs)[...] = ref[...]
        for ref, (axis, sizes) in zip(refs, plans):

            def total(start, size):
                cut = slice(start, start + size)
                return sum(
                    (ref[p, :, cut] if axis else ref[p, cut, :]).astype(F32)
                    for p in range(ref.shape[0])
                )

            at = 0
            for size in sizes:
                out = next(outs)
                if isinstance(size, tuple):
                    for q in range(size[0]):
                        out[q] = total(at, size[1])
                        at += size[1]
                else:
                    out[...] = total(at, size)
                    at += size

    kept = [(x.shape, x.dtype) for x in through]
    return stage(body, kept + [(shape, F32) for shape in shapes], (*inputs, *through))


def make_ready(segments, adapters, project_in, down_input, down_memory, turned, joined, local):
    count = segments.shape[1]
    parts, lines, width = project_in.shape

    def body(segments_ref, adapters_ref, project_ref, input_ref, memory_ref, *refs):
        ins, outs = refs[: len(turned) + len(joined)], refs[len(turned) + len(joined) :]

        def ordered(ref, parts):
            size = NAD * parts * RANK
            row = lax.broadcasted_iota(I32, (size, size), 0)
            column = lax.broadcasted_iota(I32, (size, size), 1)
            part, rest = lax.div(column, NAD * RANK), lax.rem(column, NAD * RANK)
            adapter, rank = lax.div(rest, RANK), lax.rem(rest, RANK)
            came = adapter * (parts * RANK) + part * RANK + rank
            return mm(ref[...], jnp.where(row == came, 1.0, 0.0).astype(BF16)).astype(BF16)

        for p in range(parts):
            outs[0][:, p * width : (p + 1) * width] = project_ref[p]
        outs[1][...] = ordered(input_ref, 3)
        outs[2][...] = ordered(memory_ref, 2)
        for p in range(parts):
            outs[3][:, p * width : (p + 1) * width] = ins[len(turned)][p]
        at = parts * width
        for ref in ins[len(turned) + 1 :]:
            outs[3][:, at : at + ref.shape[1]] = ref[...]
            at += ref.shape[1]
        for ref, out in zip(ins[: len(turned)], outs[4:]):
            out[...] = ref[...].astype(F32).T.astype(BF16)
        owner_ref, below_ref, owner_own_ref = outs[-3:]
        across = jnp.broadcast_to(segments_ref[...], (8, count))
        owner = jnp.zeros_like(across)
        for s in range(adapters.shape[1]):
            owner = jnp.where(across == s, adapters_ref[0:1, s : s + 1], owner)
        owner_ref[...] = owner.T[:, 0:1]
        below_ref[...] = across.T[:, 0:1]
        own = pl.ds(pl.multiple_of(lax.axis_index(TP) * local, local), local)
        owner_own_ref[...] = owner_ref[own, :]

    small = parts * width + sum(x.shape[1] for x in joined[1:])
    return stage(
        body,
        [
            ((lines, parts * width), BF16),
            (down_input.shape, BF16),
            (down_memory.shape, BF16),
            ((joined[1].shape[0], small), BF16),
        ]
        + [(x.shape[::-1], BF16) for x in turned]
        + [((count, 1), I32), ((count, 1), I32), ((local, 1), I32)],
        (segments, adapters, project_in, down_input, down_memory, *turned, *joined),
    )


def on_device(
    inputs,
    cotangent,
    norm_attend,
    norm_memory,
    project_in,
    project_out,
    query_weight,
    gate_weight,
    memory_out,
    half_keys,
    value_table,
    key_picks,
    segment_ids,
    adapter_ids,
    down_input,
    up_input,
    down_attend,
    up_attend,
    down_memory,
    up_query,
    up_gate,
    down_mixed,
    up_mixed,
):
    groups = lax.axis_size(DP)
    ranks = lax.axis_size(TP)
    rank = lax.axis_index(TP)
    local = inputs.shape[0]
    count = segment_ids.shape[0]
    width = project_in.shape[2]
    model = inputs.shape[1]

    across = segment_ids[None, :]
    attend_turned = down_attend.T
    joined = (up_input.transpose(1, 0, 2), up_query, up_gate, up_attend, up_mixed, down_mixed.T)
    turned = (project_out, memory_out)
    if project_out.shape[1] % 128 == 0:
        ready = make_ready(
            across,
            adapter_ids,
            project_in.transpose(1, 0, 2),
            down_input,
            down_memory,
            turned,
            joined,
            local,
        )
        flat_in, parted_input, parted_memory, small, out_turned, mixed_turned = ready[:6]
        owner, below, owner_own = ready[6:]
    else:
        flat_in = project_in.reshape(project_in.shape[0], 3 * width)
        parted_input, parted_memory = by_part(down_input, 3), by_part(down_memory, 2)
        out_turned, mixed_turned = [x.T for x in turned]
        small = jnp.concatenate((up_input.reshape(-1, 3 * width),) + joined[1:], axis=1)
        below = segment_ids[:, None]
        owner = jnp.zeros_like(below)
        for s in range(adapter_ids.shape[1]):
            owner = jnp.where(below == s, adapter_ids[0, s], owner)
        owner_own = lax.dynamic_slice_in_dim(owner, rank * local, local, 0)
    spots, at = [], 0
    for size in (3 * width, up_query.shape[1], width, model, model, width):
        spots.append(slice(at, at + size))
        at += size
    gain_one, gain_two, keys = norm_attend, norm_memory, half_keys[0]
    (
        (
            full_in,
            full_down_input,
            ups,
            out_t,
            attend_t,
            full_query,
            full_gate,
            full_down_memory,
            _,
        ),
        kept,
        table,
    ) = forward(
        dict(
            flat_in=flat_in,
            down_input=parted_input,
            ups=small,
            out_t=out_turned,
            attend_t=attend_turned,
            query=query_weight,
            gate=gate_weight,
            down_memory=parted_memory,
            mixed_t=mixed_turned,
            inputs=inputs,
            cotangent=cotangent,
            gain_one=gain_one,
            gain_two=gain_two,
            owner=owner,
            owner_own=owner_own,
            across=across,
            below=below,
            keys=keys,
        ),
        value_table,
        key_picks,
        spots,
        1,
    )

    def turn(d):
        return [(p, (p + d) % ranks) for p in range(ranks)]

    mixed_parts = [kept.block_0] + [
        lax.ppermute(block, TP, turn(d))
        for d, block in ((1, kept.block_1), (2, kept.block_2), (3, kept.block_3))
    ]
    picked = pick_grads(
        kept.first, kept.second, kept.grad_recalled, kept.scale, table.reshape(-1, width)
    )
    picked, mixed_parts = lax.optimization_barrier((picked, mixed_parts))
    given = dict(
        picked=picked.reshape(ranks, -1, count),
        weights=kept.weights,
        keys=keys,
        picks=key_picks,
        query=full_query,
        gate=full_gate,
        ups=ups,
        grad_gate=kept.grad_gate,
        mixed=kept.mixed,
        owner=owner,
        owner_own=owner_own,
        middle=kept.middle,
        cotangent=cotangent,
        gain_two=gain_two,
        down_memory=full_down_memory,
        out_t=out_t,
        attend_t=attend_t,
        low_three=kept.low_three,
        own_cotangent=kept.own_cotangent,
        low_four_back=kept.low_four_back,
        normed_rows=kept.normed_rows,
        projected=kept.projected,
        across=across,
        below=below,
        full_in=full_in,
        low_one=kept.low_one,
        attended=kept.attended,
        two_short=kept.two_short,
        down_input=full_down_input,
        inputs=inputs,
        gain_one=gain_one,
        normed_one=kept.normed_one,
    )
    wides, (outputs, input_grad, up_parts, memory_parts, down_parts) = backward(
        given, mixed_parts, spots, 5
    )
    (
        outputs,
        input_grad,
        grad_up_input,
        grad_up_query,
        grad_up_gate,
        grad_up_mixed,
        grad_down_attend,
        grad_down_mixed,
        grad_up_attend,
        grad_down_memory,
        grad_down_input,
    ) = add_up(
        (up_parts, memory_parts, down_parts),
        (
            (1, ((3, width), *wides[3:])),
            (0, (memory_parts.shape[1],)),
            (0, (down_parts.shape[1],)),
        ),
        (outputs, input_grad),
    )
    return (
        outputs,
        input_grad,
        grad_down_input.T,
        grad_up_input.transpose(1, 0, 2),
        grad_down_attend.T,
        grad_up_attend,
        grad_down_memory.T,
        grad_up_query,
        grad_up_gate,
        grad_down_mixed.T,
        grad_up_mixed,
    )


def solution(mesh):
    rows = P((DP, TP), None)
    both = P(DP, TP)
    wide = P(DP, None)
    turned = P(TP, DP)
    split = P(DP, None, TP)
    return jax.shard_map(
        on_device,
        mesh=mesh,
        in_specs=(
            rows,
            rows,
            P(),
            P(),
            split,
            turned,
            both,
            both,
            turned,
            P(TP, None, None, None),
            both,
            P(None, None, None, DP),
            P(DP),
            wide,
            wide,
            split,
            turned,
            wide,
            wide,
            both,
            both,
            turned,
            wide,
        ),
        out_specs=(rows, rows, both, split, turned, both, both, both, both, turned, both),
        check_vma=False,
    )
```

```python
import types

import jax
import jax.numpy as jnp
from jax import lax
from jax.experimental import pallas as pl
from jax.experimental.pallas import tpu as pltpu
from jax.sharding import PartitionSpec as P

DP, TP = "dp", "tensor"
HD = 64
NKEYS = 256
RANK = 16
NAD = 8
EPS = 1e-06
NEGATIVE = -1e30
F32, BF16, I32 = jnp.float32, jnp.bfloat16, jnp.int32
MESH = pl.DeviceIdType.MESH
ANY = pl.BlockSpec(memory_space=pl.ANY)


def mm(a, b):
    return lax.dot_general(a, b, (((1,), (0,)), ((), ())), preferred_element_type=F32)


def mt(a, b):
    return lax.dot_general(a, b, (((1,), (1,)), ((), ())), preferred_element_type=F32)


def tm(a, b):
    return lax.dot_general(a, b, (((0,), (0,)), ((), ())), preferred_element_type=F32)


def two_parts(x):
    top = x.astype(BF16)
    return top, (x - top.astype(F32)).astype(BF16)


def whole(shape):
    return pl.BlockSpec(shape, lambda *_: (0,) * len(shape))


def stage(body, outs, ins, scratch=(), limit=61):
    return pl.pallas_call(
        body,
        grid=(1,),
        out_shape=[jax.ShapeDtypeStruct(shape, dtype) for shape, dtype in outs],
        in_specs=[whole(x.shape) for x in ins],
        out_specs=[whole(shape) for shape, _ in outs],
        scratch_shapes=list(scratch),
        compiler_params=pltpu.CompilerParams(vmem_limit_bytes=limit << 20),
    )(*ins)


def rms_forward(values, gain):
    factor = lax.rsqrt(jnp.mean(values * values, axis=-1, keepdims=True) + EPS)
    return values * factor * gain


def rms_backward(values, gain, upstream):
    factor = lax.rsqrt(jnp.mean(values * values, axis=-1, keepdims=True) + EPS)
    scaled = upstream * gain
    return factor * scaled - values * (factor * factor * factor) * jnp.mean(
        values * scaled, axis=-1, keepdims=True
    )


def masked(values, owner):
    columns = lax.broadcasted_iota(I32, values.shape, 1)
    adapter = lax.rem(lax.div(columns, RANK), NAD)
    return jnp.where(adapter == owner, values, 0.0).astype(BF16)


def folding(parts):
    shape = (parts * RANK, parts * NAD * RANK)
    short = lax.broadcasted_iota(I32, shape, 0)
    column = lax.broadcasted_iota(I32, shape, 1)
    same = (lax.div(short, RANK) == lax.div(column, NAD * RANK)) & (
        lax.rem(short, RANK) == lax.rem(column, RANK)
    )
    return jnp.where(same, 1.0, 0.0).astype(BF16)


def shorten(values):
    return mt(folding(values.shape[1] // (NAD * RANK)), values).astype(BF16)


def lengthen(short, owner):
    return masked(tm(short, folding(short.shape[0] // RANK)), owner)


def side_by_side(blocks):
    return jnp.concatenate([blocks[p] for p in range(blocks.shape[0])], axis=1)


def block_probs(queries, keys, across_ref, down_ref, r, block):
    top = (r + 1) * block
    at = slice(r * block, top)
    scores = mt(queries[at], keys[:top]) * HD**-0.5
    place = lax.broadcasted_iota(I32, (block, top), 0) + r * block
    other = lax.broadcasted_iota(I32, (block, top), 1)
    ahead = across_ref[:, :top]
    seen = (other <= place) & ((ahead == 0) | (ahead == down_ref[at, :]))
    scores = jnp.where(seen, scores, NEGATIVE)
    raised = jnp.exp(scores - jnp.max(scores, axis=-1, keepdims=True))
    return raised / jnp.sum(raised, axis=-1, keepdims=True)


def wide_lanes(pair, base=0):
    return pl.ds(pl.multiple_of(base + pair * 2 * HD, 2 * HD), 2 * HD)


def own_columns(short, owner, first):
    high, count = short.shape
    adapters = NAD // lax.axis_size(TP)
    pattern = lax.broadcasted_iota(I32, (high, adapters * high), 0) == lax.rem(
        lax.broadcasted_iota(I32, (high, adapters * high), 1), high
    )
    spread = tm(short, jnp.where(pattern, 1.0, 0.0).astype(BF16))
    adapter = lax.div(lax.broadcasted_iota(I32, (count, adapters * high), 1), high) + first
    return jnp.where(adapter == owner, spread, 0.0).astype(BF16)


class Waited:
    def __init__(self, names, refs, loads):
        self._pending = dict(zip(names, zip(refs, loads)))

    def __getattr__(self, name):
        ref, load = self._pending[name]
        load.wait()
        setattr(self, name, ref)
        return ref


def backward(given, mixed_parts, ups_spots, cid, block=128):
    _, query_spot, gate_spot, attend_spot, mixed_spot, low_spot = ups_spots
    shown = types.SimpleNamespace(**given)
    picked = given.pop(next(iter(given)))
    names = list(given)
    arrays = [picked, *given.values(), *mixed_parts]
    ranks, groups = lax.axis_size(TP), lax.axis_size(DP)
    count, width = shown.attended.shape
    local, model = shown.inputs.shape
    number = shown.weights.shape[0]
    half = shown.keys.shape[2]
    space = NAD * RANK
    adapters = NAD // ranks
    lines, share = space // groups, model // groups
    wides = [width] * 3 + [2 * half] + [width] * 5
    tall = [adapters * 2 * RANK, adapters * 3 * RANK]
    vmem = dict(
        pick_in=((ranks, number, count), BF16),
        dense=((NKEYS, count), F32),
        grad_query=((count, 2 * half), BF16),
        normed_out=((ranks, local, model), BF16),
        normed_in=((ranks, local, model), BF16),
        three_in=((ranks, 2 * RANK, count), BF16),
        four_in=((ranks, RANK, count), BF16),
        three_sum=((2 * RANK, count), BF16),
        four_sum=((RANK, count), BF16),
        attended_out=((local, model), BF16),
        attended_in=((ranks, local, width), BF16),
        branch_out=((local, model), BF16),
        branch_in=((ranks, local, width), BF16),
        back_in=((ranks, RANK, local), BF16),
        grad_middle=((local, model), F32),
        grads=((count, 3 * width), BF16),
        key_sum=((2, count, HD), F32),
        value_sum=((2, count, HD), F32),
        input_out=((ranks, local, model), BF16),
        input_in=((ranks, local, model), BF16),
        one_in=((ranks, 3 * RANK, count), BF16),
        one_sum=((3 * RANK, count), BF16),
        ups_out=((groups, lines, sum(wides)), BF16),
        memory_out=((groups, tall[0], share), BF16),
        down_out=((groups, tall[1], share), BF16),
        outputs=((local, model), BF16),
        input_grad=((local, model), F32),
    )
    inputs = arrays[1:]
    results = [
        ((local, model), BF16),
        ((local, model), F32),
        ((groups, lines, sum(wides)), BF16),
        ((groups, tall[0], share), BF16),
        ((groups, tall[1], share), BF16),
    ]

    def body(*refs):
        outs = refs[len(arrays) : len(arrays) + len(results)]
        rest = refs[len(arrays) + len(results) :]
        v = types.SimpleNamespace(**dict(zip(vmem, rest[len(inputs) :])))
        loaded, saved, send, recv, far_send, far_recv = rest[len(inputs) + len(vmem) :]
        rank, group = lax.axis_index(TP), lax.axis_index(DP)
        barrier = pltpu.get_barrier_semaphore()
        for d in range(1, ranks):
            pl.semaphore_signal(
                barrier,
                inc=1,
                device_id={TP: lax.rem(rank + d, ranks)},
                device_id_type=MESH,
            )

        @pl.loop(1, groups)
        def _(d):
            pl.semaphore_signal(
                barrier,
                inc=1,
                device_id={DP: lax.rem(group + d, groups)},
                device_id_type=MESH,
            )

        loads = [
            pltpu.make_async_copy(
                refs[i + 1].at[rank] if x is shown.picks else refs[i + 1], rest[i], loaded.at[i]
            )
            for i, x in enumerate(inputs)
        ]
        for load in loads:
            load.start()
        need = Waited(names, rest, loads)

        def near(i, d, src, dst):
            return pltpu.make_async_remote_copy(
                src_ref=src,
                dst_ref=dst,
                send_sem=send.at[i, d],
                recv_sem=recv.at[i, d],
                device_id={TP: lax.rem(rank + d, ranks)},
                device_id_type=MESH,
            )

        def far(i, d, src, dst):
            return pltpu.make_async_remote_copy(
                src_ref=src,
                dst_ref=dst,
                send_sem=far_send.at[i, d],
                recv_sem=far_recv.at[i, d],
                device_id={DP: lax.rem(group + d, groups)},
                device_id_type=MESH,
            )

        def far_piece(i, d, ref):
            return far(i, d, ref.at[lax.rem(group + d, groups)], outs[2 + i].at[group])

        def send_far(i, ref):
            @pl.loop(1, groups)
            def _(d):
                far_piece(i, d, ref).start()

            keep = pltpu.make_async_copy(ref.at[group], outs[2 + i].at[group], saved.at[2 + i])
            keep.start()
            return keep

        def shared(i, ref):
            return [near(i, d, ref.at[rank], ref.at[rank]) for d in range(1, ranks)]

        def columns(ref, p):
            return ref.at[:, pl.ds(pl.multiple_of(p * width, width), width)]

        def split(i, src, dst):
            return [
                near(i, d, columns(src, lax.rem(rank + d, ranks)), dst.at[rank])
                for d in range(1, ranks)
            ]

        def total(ref):
            return sum(ref[p].astype(F32) for p in range(ranks))

        own_tokens = pl.ds(pl.multiple_of(rank * local, local), local)
        own_columns_at = pl.ds(pl.multiple_of(rank * width, width), width)

        pick_in = v.pick_in
        own_pick = pltpu.make_async_copy(refs[0].at[rank], pick_in.at[rank], saved.at[0])
        own_pick.start()
        pl.semaphore_wait(barrier, ranks + groups - 2)
        picks_sent = [
            near(0, d, refs[0].at[lax.rem(rank + d, ranks)], pick_in.at[rank])
            for d in range(1, ranks)
        ]
        for c in picks_sent:
            c.start()
        weights_ref, keys_ref, picks_ref = need.weights, need.keys, need.picks
        own_pick.wait()
        for c in picks_sent:
            c.wait()

        slot = lax.broadcasted_iota(I32, (NKEYS, block), 0)
        for part in range(2):

            @pl.loop(0, count // block)
            def _(c):
                lanes = pl.ds(pl.multiple_of(c * block, block), block)
                weight = weights_ref[:, lanes]
                grad = sum(pick_in[p, :, lanes].astype(F32) for p in range(ranks))
                grad = weight * (grad - jnp.sum(grad * weight, axis=0, keepdims=True))
                grad = grad * (2 * half) ** -0.5
                dense = jnp.zeros((NKEYS, block), F32)
                for k in range(number):
                    hit = slot == picks_ref[part, k : k + 1, lanes]
                    dense += jnp.where(hit, grad[k : k + 1, :], 0.0)
                v.dense[:, lanes] = dense

            top, low = two_parts(v.dense[...])
            v.grad_query[:, part * half : (part + 1) * half] = (
                tm(top, keys_ref[part]) + tm(low, keys_ref[part])
            ).astype(BF16)

        query_ref, gate_ref, ups_ref = need.query, need.gate, need.ups
        grad_gate_ref, mixed_ref, owner_ref = need.grad_gate, need.mixed, need.owner
        normed_sent = []
        for d in [ranks // 2] + [d for d in range(1, ranks) if d != ranks // 2] + [0]:
            at = pl.ds(pl.multiple_of(lax.rem(rank + d, ranks) * local, local), local)
            asked, gates, own = v.grad_query[at, :], grad_gate_ref[at, :], owner_ref[at, :]
            part = (mt(asked, query_ref[...]) + mt(gates, gate_ref[...])).astype(BF16)
            if d:
                v.normed_out[d] = part
                normed_sent.append(near(1, d, v.normed_out.at[d], v.normed_in.at[rank]))
                normed_sent[-1].start()
            else:
                v.normed_in[rank] = part
            three = jnp.concatenate(
                [mt(asked, ups_ref[:, query_spot]), mt(gates, ups_ref[:, gate_spot])], axis=1
            )
            v.three_in[rank, :, at] = shorten(masked(three, own))
            v.four_in[rank, :, at] = shorten(
                masked(mt(mixed_ref[at, :], ups_ref[:, low_spot]), own)
            )
        short_sent = shared(2, v.three_in) + shared(3, v.four_in)
        for c in short_sent:
            c.start()
        owner_own = need.owner_own[...]
        middle_ref, cotangent_ref, gain_two = need.middle, need.cotangent, need.gain_two
        down_ref, out_ref, attend_ref = need.down_memory, need.out_t, need.attend_t
        mixed_refs = []
        for i in range(len(names), len(inputs)):
            loads[i].wait()
            mixed_refs.append(rest[i])
        for c in normed_sent + short_sent:
            c.wait()

        v.three_sum[...] = total(v.three_in).astype(BF16)
        v.four_sum[...] = total(v.four_in).astype(BF16)
        grad_three = lengthen(v.three_sum[:, own_tokens], owner_own)
        upstream = total(v.normed_in) + mt(grad_three, down_ref[...])
        grad = cotangent_ref[...].astype(F32) + rms_backward(
            middle_ref[...], gain_two[...].astype(F32)[None, :], upstream
        )
        v.grad_middle[...] = grad
        branch = grad.astype(BF16)
        v.branch_out[...] = branch
        low = masked(mt(branch, ups_ref[:, attend_spot]), owner_own)
        v.attended_out[...] = (mm(branch, out_ref[...]) + mm(low, attend_ref[...])).astype(BF16)
        v.back_in[rank] = shorten(low)
        v.attended_in[rank] = v.attended_out[:, own_columns_at]
        v.branch_in[rank] = v.branch_out[:, own_columns_at]
        attended_sent = split(4, v.attended_out, v.attended_in)
        later_sent = shared(5, v.back_in) + split(6, v.branch_out, v.branch_in)
        for c in attended_sent:
            c.start()

        low_four = lengthen(v.four_sum[:, own_tokens], owner_own)
        v.outputs[...] = (
            middle_ref[...]
            + sum(ref[...].astype(F32) for ref in mixed_refs)
            + mm(low_four, ups_ref[:, mixed_spot])
        ).astype(BF16)
        stores = [pltpu.make_async_copy(v.outputs, outs[0], saved.at[0])]
        stores[0].start()
        owner = owner_ref[...]
        starts = [sum(wides[:i]) for i in range(len(wides))]

        def put(i, left, rows):
            found = tm(left, rows).astype(F32)
            for g in range(groups):
                v.ups_out[g, :, starts[i] : starts[i] + wides[i]] = found[
                    g * lines : (g + 1) * lines
                ].astype(BF16)

        def put_down(out_ref, short, normed_ref):
            spread = own_columns(short, owner, rank * adapters)
            step = max(share, 128)
            for c in range(model // step):
                found = tm(spread, normed_ref[:, c * step : (c + 1) * step]).astype(BF16)
                for p in range(step // share):
                    out_ref[c * (step // share) + p] = found[:, p * share : (p + 1) * share]

        low_three = need.low_three
        put(3, low_three[:, :space], v.grad_query[...])
        put(4, low_three[:, space:], grad_gate_ref[...])
        put(5, lengthen(v.four_sum[...], owner), need.own_cotangent[...])
        put(7, need.low_four_back[...], mixed_ref[...])
        put_down(v.memory_out, v.three_sum[...], need.normed_rows)
        memory_kept = send_far(1, v.memory_out)
        projected_ref, across_ref, below_ref = need.projected, need.across, need.below
        weight_ref = need.full_in
        for c in attended_sent:
            c.wait()
        for c in later_sent:
            c.start()

        @pl.loop(0, width // (2 * HD))
        def _(pair):
            queries, keys, values = [projected_ref[:, wide_lanes(pair, p * width)] for p in range(3)]
            above = jnp.concatenate(
                [v.attended_in[p, :, wide_lanes(pair)] for p in range(ranks)], axis=0
            )
            v.key_sum[...] = jnp.zeros_like(v.key_sum)
            v.value_sum[...] = jnp.zeros_like(v.value_sum)
            for r in range(count // block):
                at, top = slice(r * block, (r + 1) * block), (r + 1) * block
                parts = []
                for h in range(2):
                    lanes = slice(h * HD, (h + 1) * HD)
                    probs = block_probs(
                        queries[:, lanes], keys[:, lanes], across_ref, below_ref, r, block
                    )
                    grad_probs = mt(above[at, lanes], values[:top, lanes])
                    inner = jnp.sum(probs * grad_probs, axis=-1, keepdims=True)
                    grad_scores = (probs * (grad_probs - inner)).astype(BF16)
                    parts.append(mm(grad_scores, keys[:top, lanes]))
                    v.key_sum[h, :top, :] += tm(grad_scores, queries[at, lanes])
                    v.value_sum[h, :top, :] += tm(probs.astype(BF16), above[at, lanes])
                v.grads[at, wide_lanes(pair)] = (
                    jnp.concatenate(parts, axis=1) * HD**-0.5
                ).astype(BF16)
            v.grads[:, wide_lanes(pair, width)] = (
                jnp.concatenate([v.key_sum[0], v.key_sum[1]], axis=1) * HD**-0.5
            ).astype(BF16)
            v.grads[:, wide_lanes(pair, 2 * width)] = jnp.concatenate(
                [v.value_sum[0], v.value_sum[1]], axis=1
            ).astype(BF16)

        input_sent = []
        for d in [ranks // 2] + [d for d in range(1, ranks) if d != ranks // 2] + [0]:
            at = pl.ds(pl.multiple_of(lax.rem(rank + d, ranks) * local, local), local)
            part = mt(v.grads[at, :], weight_ref[...]).astype(BF16)
            if d:
                v.input_out[d] = part
                input_sent.append(near(7, d, v.input_out.at[d], v.input_in.at[rank]))
                input_sent[-1].start()
            else:
                v.input_in[rank] = part
            one = jnp.concatenate(
                [
                    mt(
                        v.grads[at, p * width : (p + 1) * width],
                        ups_ref[:, p * width : (p + 1) * width],
                    )
                    for p in range(3)
                ],
                axis=1,
            )
            v.one_in[rank, :, at] = shorten(masked(one, owner_ref[at, :]))
        one_sent = shared(8, v.one_in)
        for c in one_sent:
            c.start()
        for c in later_sent:
            c.wait()
        low_one = need.low_one
        for p in range(3):
            put(
                p,
                low_one[:, p * space : (p + 1) * space],
                v.grads[:, p * width : (p + 1) * width],
            )
        put(6, lengthen(side_by_side(v.back_in), owner), need.attended[...])
        put(
            8,
            lengthen(side_by_side(need.two_short), owner),
            jnp.concatenate([v.branch_in[p] for p in range(ranks)], axis=0),
        )
        ups_kept = send_far(0, v.ups_out)
        down_input_ref, rows_ref, gain_one = need.down_input, need.inputs, need.gain_one
        normed_one_ref = need.normed_one
        for c in one_sent:
            c.wait()
        v.one_sum[...] = total(v.one_in).astype(BF16)
        put_down(v.down_out, v.one_sum[...], normed_one_ref)
        down_kept = send_far(2, v.down_out)
        for c in input_sent:
            c.wait()
        low = lengthen(v.one_sum[:, own_tokens], owner_own)
        upstream = total(v.input_in) + mt(low, down_input_ref[...])
        v.input_grad[...] = v.grad_middle[...] + rms_backward(
            rows_ref[...].astype(F32), gain_one[...].astype(F32)[None, :], upstream
        )
        stores.append(pltpu.make_async_copy(v.input_grad, outs[1], saved.at[1]))
        stores[1].start()

        @pl.loop(1, groups)
        def _(d):
            for i, ref in enumerate((v.ups_out, v.memory_out, v.down_out)):
                far_piece(i, d, ref).wait()

        for c in stores + [ups_kept, memory_kept, down_kept]:
            c.wait()

    near_sems = pltpu.SemaphoreType.DMA((9, ranks))
    far_sems = pltpu.SemaphoreType.DMA((3, groups))
    return wides, pl.pallas_call(
        body,
        out_shape=[jax.ShapeDtypeStruct(shape, dtype) for shape, dtype in results],
        in_specs=[ANY] * len(arrays),
        out_specs=[ANY] * len(results),
        scratch_shapes=[
            pltpu.VMEM(x.shape[1:] if x is shown.picks else x.shape, x.dtype) for x in inputs
        ]
        + [pltpu.VMEM(shape, dtype) for shape, dtype in vmem.values()]
        + [
            pltpu.SemaphoreType.DMA((len(inputs),)),
            pltpu.SemaphoreType.DMA((5,)),
            near_sems,
            near_sems,
            far_sems,
            far_sems,
        ],
        compiler_params=pltpu.CompilerParams(
            collective_id=cid, has_side_effects=True, vmem_limit_bytes=61 << 20
        ),
    )(*arrays)


def forward(given, table, key_picks, spots, cid, block=128, sub=32, conv=32):
    _, query_spot, gate_spot, attend_spot, mixed_spot, low_spot = spots
    shown = types.SimpleNamespace(**given)
    names = list(given)
    local_arrays = list(given.values())
    ranks, groups = lax.axis_size(TP), lax.axis_size(DP)
    local, model = shown.inputs.shape
    count = shown.owner.shape[0]
    width = shown.gate.shape[1]
    half = shown.keys.shape[2]
    number = key_picks.shape[2]
    picks = key_picks.shape[0] * number
    space = NAD * RANK
    rows = table.shape[0]
    piece = rows // 2
    blocks = 2 * groups
    stride = sub + 1
    chips = groups // 2
    relayed = chips == 4
    hops = max(chips, 4)
    tree = [
        shown.flat_in,
        shown.down_input,
        shown.ups,
        shown.out_t,
        shown.attend_t,
        shown.query,
        shown.gate,
        shown.down_memory,
        shown.mixed_t,
    ]
    early, nested, late = (0, 1, 2), (3, 4), (5, 6, 7, 8)
    cuts = 4
    chunks = tuple(range(len(tree), len(tree) + cuts))
    tree_shapes = [
        (x.shape[0], x.shape[1] * (ranks if a in nested else 1)) for a, x in enumerate(tree)
    ]
    full = [((groups, *shape), BF16) for shape in tree_shapes]
    results = dict(
        normed_one=((count, model), BF16),
        low_one=((count, 3 * space), BF16),
        projected=((count, 3 * width), BF16),
        attended=((count, width), BF16),
        middle=((local, model), F32),
        two_short=((ranks, RANK, local), BF16),
        normed_rows=((count, model), BF16),
        low_three=((count, 2 * space), BF16),
        weights=((number, count), F32),
        mixed=((count, width), BF16),
        grad_recalled=((count, width), BF16),
        grad_gate=((count, width), BF16),
        scale=((count, 1), F32),
        low_four_back=((count, space), BF16),
        own_cotangent=((count, width), BF16),
        first=((count, picks), I32),
        second=((count, picks), I32),
        block_0=((local, model), BF16),
        block_1=((local, model), BF16),
        block_2=((local, model), BF16),
        block_3=((local, model), BF16),
    )
    vmem = dict(
        rows_in=((ranks, local, model), BF16),
        cotangent_in=((ranks, local, model), BF16),
        out_stage=(tree_shapes[3], BF16),
        attend_stage=(tree_shapes[4], BF16),
        attended_in=((local, model), BF16),
        normed_two=((local, model), BF16),
        asked=((count, 2 * half), F32),
        every=((NKEYS, count), F32),
        gate_pre=((count, width), F32),
        narrow=((ranks, number, count), BF16),
        grad_mixed=((count, width), F32),
        picks=(key_picks.shape, I32),
        by_token=((count, picks), F32),
        low=((NKEYS * stride + sub, 128), F32),
        high=((NKEYS * stride + sub, 128), F32),
        spread=((2, sub, NKEYS * NKEYS), BF16),
        dense_in=((2, count, piece), BF16),
        table_in=((2, piece, width), BF16),
        total=((count, width), F32),
        largest=((8, 1), F32),
    )
    outs = [
        *full,
        *results.values(),
        ((groups, rows, width), BF16),
        ((count, NKEYS * NKEYS), BF16),
    ]

    def body(*refs):
        inputs = refs[: len(names) + 2]
        out_refs = refs[len(inputs) : len(inputs) + len(outs)]
        rest = list(refs[len(inputs) + len(outs) :])

        def take(n):
            taken = rest[:n]
            del rest[:n]
            return taken

        held = take(len(names))
        gathered = take(len(tree))
        r = types.SimpleNamespace(**dict(zip(results, take(len(results)))))
        v = types.SimpleNamespace(**dict(zip(vmem, take(len(vmem)))))
        loaded, kept, stored, near_send, near_recv, tree_send, tree_recv, pass_send, pass_recv = rest[:9]
        moved = rest[9]
        table_ref, picks_ref = inputs[-2:]
        table_out, dense_out = out_refs[-2:]
        rank, group = lax.axis_index(TP), lax.axis_index(DP)
        barrier = pltpu.get_barrier_semaphore()
        for d in range(1, ranks):
            pl.semaphore_signal(
                barrier,
                inc=1,
                device_id={TP: lax.rem(rank + d, ranks)},
                device_id_type=MESH,
            )

        @pl.loop(1, groups)
        def _(d):
            pl.semaphore_signal(
                barrier,
                inc=1,
                device_id={DP: lax.rem(group + d, groups)},
                device_id_type=MESH,
            )

        loads = [
            pltpu.make_async_copy(inputs[i], held[i], loaded.at[i]) for i in range(len(names))
        ]
        loads.append(pltpu.make_async_copy(picks_ref, v.picks, loaded.at[len(names)]))
        for load in loads:
            load.start()
        need = Waited(names, held, loads)
        raw = types.SimpleNamespace(**dict(zip(names, inputs)))

        def near(i, d, src, dst):
            return pltpu.make_async_remote_copy(
                src_ref=src,
                dst_ref=dst,
                send_sem=near_send.at[i, d],
                recv_sem=near_recv.at[i, d],
                device_id={TP: lax.rem(rank + d, ranks)},
                device_id_type=MESH,
            )

        def columns(ref, p, wide):
            return ref.at[:, pl.ds(pl.multiple_of(p * wide, wide), wide)]

        def way(a):
            return 1 if a - len(tree) < cuts // 2 else 2

        def cut_of(a):
            return pl.ds((a - len(tree)) * (rows // cuts), rows // cuts)

        def source(a):
            if a in chunks:
                return table_ref.at[cut_of(a)]
            if a in nested:
                return (v.out_stage, v.attend_stage)[a - 3]
            return inputs[names.index(given_names[a])]

        given_names = [names[i] for i in tree_names]

        def place(a, p):
            if a in chunks:
                return table_out.at[p, cut_of(a)]
            return gathered[a].at[p]

        def partner(d):
            if not relayed:
                return lax.rem(group + 2 * d, groups)
            across = 2 - 4 * lax.rem(lax.div(group, 2), 2) if d & 1 else 0
            along = 4 - 8 * lax.div(group, 4) if d & 2 else 0
            return group + across + along

        def holder(d):
            if isinstance(d, int) and d == 0:
                return group
            return partner(d) if relayed else lax.rem(group - 2 * d + groups, groups)

        def to_chip(a, d):
            relay = relayed and a in chunks and d == 3
            shard = place(a, holder(way(a))) if relay else source(a)
            return pltpu.make_async_remote_copy(
                src_ref=shard,
                dst_ref=shard if relay else place(a, group),
                send_sem=tree_send.at[a, d],
                recv_sem=tree_recv.at[a, d],
                device_id={DP: partner(3 - way(a) if relay else d)},
                device_id_type=MESH,
            )

        def to_sibling(a, d):
            first = isinstance(d, int) and d == 0
            return pltpu.make_async_remote_copy(
                src_ref=source(a) if first else place(a, holder(d)),
                dst_ref=place(a, holder(d)),
                send_sem=pass_send.at[a, d],
                recv_sem=pass_recv.at[a, d],
                device_id={DP: group + 1 - 2 * lax.rem(group, 2)},
                device_id_type=MESH,
            )

        def own_copy(a):
            return pltpu.make_async_copy(source(a), place(a, group), kept.at[a])

        def begin(chosen):
            for a in chosen:
                own_copy(a).start()
                if relayed:
                    for d in range(1, 4):
                        to_chip(a, d).start()
                else:

                    @pl.loop(1, chips)
                    def _(d):
                        to_chip(a, d).start()

                to_sibling(a, 0).start()

        def begin_table(chosen):
            if not relayed:
                begin(chosen)
                return
            for a in chosen:
                to_chip(a, way(a)).start()
                own_copy(a).start()
                to_sibling(a, 0).start()

        def rest_of_table(chosen):
            if relayed:
                for a in chosen:
                    to_chip(a, 3 - way(a)).start()

        def onward(a, d):
            to_chip(a, d).wait_recv()
            to_sibling(a, d).start()

        def other(chosen):
            if relayed:
                for a in chosen:
                    onward(a, 3 - way(a))

        def last(chosen):
            for a in chosen:
                if relayed:
                    onward(a, 3)
                else:

                    @pl.loop(1, chips)
                    def _(d):
                        onward(a, d)

        def collect(chosen):
            if relayed:
                for d in range(1, 3):
                    for a in chosen:
                        onward(a, d)
            last(chosen)

        def settle(chosen):
            for a in chosen:
                own_copy(a).wait()
                to_sibling(a, 0).wait()
                if relayed:
                    for d in range(1, 4):
                        to_sibling(a, d).wait()
                        to_chip(a, d).wait_send()
                else:

                    @pl.loop(1, chips)
                    def _(d):
                        to_sibling(a, d).wait()
                        to_chip(a, d).wait_send()

        stores = []

        def store(src, dst):
            stores.append(pltpu.make_async_copy(src, dst, stored.at[len(stores)]))
            stores[-1].start()

        def store_trees(chosen):
            for a in chosen:
                store(gathered[a], out_refs[a])

        result_refs = dict(zip(results, out_refs[len(tree) :]))

        def flat(ref):
            return ref[...].reshape(-1, ref.shape[2])

        def done(ref):
            for name in results:
                if getattr(r, name) is ref:
                    store(ref, result_refs[name])

        pl.semaphore_wait(barrier, ranks + groups - 2)
        homes = []
        for i, (src, dst) in enumerate(((raw.inputs, v.rows_in), (raw.cotangent, v.cotangent_in))):
            homes.append(pltpu.make_async_copy(src, dst.at[rank], moved.at[i]))
        for i, (src, dst) in enumerate(((raw.out_t, v.out_stage), (raw.attend_t, v.attend_stage))):
            homes.append(
                pltpu.make_async_copy(src, columns(dst, rank, src.shape[1]), moved.at[2 + i])
            )
        for c in homes:
            c.start()
        nest_sent = [
            near(i, d, src, columns(dst, rank, src.shape[1]))
            for i, src, dst in ((0, raw.out_t, v.out_stage), (1, raw.attend_t, v.attend_stage))
            for d in range(1, ranks)
        ]
        rows_sent = [near(2, d, raw.inputs, v.rows_in.at[rank]) for d in range(1, ranks)]
        back_sent = [near(3, d, raw.cotangent, v.cotangent_in.at[rank]) for d in range(1, ranks)]
        for c in nest_sent + rows_sent:
            c.start()
        begin(early)
        begin(late)
        for c in nest_sent:
            c.wait()
        homes[2].wait()
        homes[3].wait()
        begin(nested)
        begin_table(chunks)
        gain_one, owner_ref = need.gain_one, need.owner
        homes[0].wait()
        for c in rows_sent:
            c.wait()
        for c in range(ranks):
            r.normed_one[c * local : (c + 1) * local, :] = rms_forward(
                v.rows_in[c].astype(F32), gain_one[...].astype(F32)[None, :]
            ).astype(BF16)
        done(r.normed_one)
        for c in back_sent:
            c.start()
        collect(early)
        settle(early)
        store_trees(early)
        weight_ref, down_ref, ups_ref = gathered[:3]

        def up(spot):
            return ups_ref[:, :, spot].reshape(space, -1)

        @pl.loop(0, ranks)
        def _(c):
            at = pl.ds(pl.multiple_of(c * local, local), local)
            normed = r.normed_one[at, :]
            low = masked(mm(normed, flat(down_ref)), owner_ref[at, :])
            r.low_one[at, :] = low
            for p in range(3):
                lanes = slice(p * width, (p + 1) * width)
                r.projected[at, lanes] = (
                    mm(normed, weight_ref[:, :, lanes].reshape(model, width))
                    + mm(low[:, p * space : (p + 1) * space], up(lanes))
                ).astype(BF16)

        across_ref, below_ref = need.across, need.below

        @pl.loop(0, width // (2 * HD))
        def _(pair):
            queries, keys, values = [r.projected[:, wide_lanes(pair, p * width)] for p in range(3)]
            for q in range(count // block):
                top = (q + 1) * block
                parts = []
                for lanes in (slice(0, HD), slice(HD, 2 * HD)):
                    probs = block_probs(
                        queries[:, lanes], keys[:, lanes], across_ref, below_ref, q, block
                    )
                    parts.append(mm(probs.astype(BF16), values[:top, lanes]))
                r.attended[q * block : top, wide_lanes(pair)] = jnp.concatenate(
                    parts, axis=1
                ).astype(BF16)

        def lines_of(p):
            return r.attended.at[pl.ds(pl.multiple_of(p * local, local), local)]

        attended_sent = [
            near(4, d, lines_of(lax.rem(rank + d, ranks)), columns(v.attended_in, rank, width))
            for d in range(1, ranks)
        ]
        for c in attended_sent:
            c.start()
        rest_of_table(chunks)
        own_rows = pl.ds(pl.multiple_of(rank * local, local), local)
        v.attended_in[:, pl.ds(pl.multiple_of(rank * width, width), width)] = r.attended[own_rows, :]
        done(r.low_one)
        done(r.projected)
        done(r.attended)
        collect(nested)
        settle(nested)
        store_trees(nested)
        out_ref, attend_ref = gathered[3:5]
        residual_ref, gain_two, owner_own = need.inputs, need.gain_two, need.owner_own[...]
        for c in attended_sent:
            c.wait()
        low = masked(mt(v.attended_in[...], flat(attend_ref)), owner_own)
        middle = (
            residual_ref[...].astype(F32)
            + mt(v.attended_in[...], flat(out_ref))
            + mm(low, up(attend_spot))
        )
        r.middle[...] = middle
        normed = rms_forward(middle, gain_two[...].astype(F32)[None, :]).astype(BF16)
        v.normed_two[...] = normed
        r.normed_rows[own_rows, :] = normed
        r.two_short[rank] = shorten(low)
        normed_sent = [
            near(5, d, v.normed_two, r.normed_rows.at[own_rows]) for d in range(1, ranks)
        ] + [near(6, d, r.two_short.at[rank], r.two_short.at[rank]) for d in range(1, ranks)]
        for c in normed_sent:
            c.start()
        done(r.middle)
        loads[-1].wait()
        r.first[...] = jnp.concatenate(
            [v.picks[m, 0] for m in range(key_picks.shape[0])], axis=0
        ).T
        r.second[...] = jnp.concatenate(
            [v.picks[m, 1] for m in range(key_picks.shape[0])], axis=0
        ).T
        done(r.first)
        done(r.second)
        collect(late)
        settle(late)
        store_trees(late)
        query_ref, gate_ref, memory_ref, mixed_ref = gathered[5:]
        homes[1].wait()
        for c in back_sent:
            c.wait()
        own_lanes = pl.ds(pl.multiple_of(rank * width, width), width)
        for c in range(ranks):
            at = slice(c * local, (c + 1) * local)
            r.own_cotangent[at, :] = v.cotangent_in[c, :, own_lanes]
            low = masked(mt(v.cotangent_in[c], up(mixed_spot)), owner_ref[at, :])
            r.low_four_back[at, :] = low
            v.grad_mixed[at, :] = mm(v.cotangent_in[c], flat(mixed_ref)) + mm(low, up(low_spot))
        done(r.own_cotangent)
        done(r.low_four_back)
        keys_ref = need.keys
        for c in normed_sent:
            c.wait()
        if relayed:
            for a in chunks:
                onward(a, way(a))
                to_chip(a, 3).start()
        done(r.normed_rows)
        done(r.two_short)

        @pl.loop(0, ranks)
        def _(c):
            at = pl.ds(pl.multiple_of(c * local, local), local)
            normed = r.normed_rows[at, :]
            low = masked(mm(normed, flat(memory_ref)), owner_ref[at, :])
            r.low_three[at, :] = low
            v.asked[at, :] = mm(normed, flat(query_ref)) + mm(low[:, :space], up(query_spot))
            v.gate_pre[at, :] = mm(normed, flat(gate_ref)) + mm(low[:, space:], up(gate_spot))

        done(r.low_three)
        slot = lax.broadcasted_iota(I32, (NKEYS, block), 0)
        for part in range(2):
            top, low = two_parts(v.asked[:, part * half : (part + 1) * half])
            v.every[...] = mt(keys_ref[part], top) + mt(keys_ref[part], low)

            @pl.loop(0, count // block)
            def _(c):
                lanes = pl.ds(pl.multiple_of(c * block, block), block)
                scores = v.every[:, lanes]
                found = []
                for k in range(number):
                    hit = slot == v.picks[rank, part, k : k + 1, lanes]
                    found.append(jnp.sum(jnp.where(hit, scores, 0.0), axis=0, keepdims=True))
                found = jnp.concatenate(found, axis=0)
                if part == 0:
                    r.weights[:, lanes] = found
                else:
                    added = (r.weights[:, lanes] + found) * (2 * half) ** -0.5
                    raised = jnp.exp(added - jnp.max(added, axis=0, keepdims=True))
                    weights = raised / jnp.sum(raised, axis=0, keepdims=True)
                    r.weights[:, lanes] = weights
                    v.narrow[rank, :, lanes] = weights.astype(BF16)

        narrow_sent = [
            near(7, d, v.narrow.at[rank], v.narrow.at[rank]) for d in range(1, ranks)
        ]
        for c in narrow_sent:
            c.start()
        done(r.weights)
        for c in narrow_sent:
            c.wait()
        v.by_token[...] = (
            jnp.concatenate([v.narrow[p] for p in range(ranks)], axis=0).astype(F32).T
        )

        wide_slot = lax.broadcasted_iota(I32, (NKEYS, picks), 0)
        steps = count // sub

        def spread_out(t, s):
            return pltpu.make_async_copy(
                v.spread.at[s],
                dense_out.at[pl.ds(pl.multiple_of(t * sub, sub), sub)],
                moved.at[4 + s],
            )

        @pl.loop(0, steps)
        def _(t):
            s = lax.rem(t, 2)
            at = pl.ds(pl.multiple_of(t * sub, sub), sub)
            firsts, seconds, weights = r.first[at, :], r.second[at, :], v.by_token[at, :]
            for n in range(sub):
                b = jnp.where(wide_slot == seconds[n : n + 1], 1.0, 0.0).astype(BF16)
                a = jnp.where(wide_slot == firsts[n : n + 1], weights[n : n + 1], 0.0).astype(BF16)
                both = mt(a, b)
                v.low[pl.ds(n, NKEYS, stride=stride), :] = both[:, :128]
                v.high[pl.ds(n, NKEYS, stride=stride), :] = both[:, 128:]

            @pl.when(t >= 2)
            def _():
                spread_out(t - 2, s).wait()

            @pl.loop(0, NKEYS // conv)
            def _(c):
                for q in range(conv):
                    i = c * conv + q
                    lanes = pl.multiple_of(i * NKEYS, NKEYS)
                    lines = pl.ds(i * stride, sub)
                    v.spread[s, :, pl.ds(lanes, 128)] = v.low[lines, :].astype(BF16)
                    v.spread[s, :, pl.ds(lanes + 128, 128)] = v.high[lines, :].astype(BF16)

            spread_out(t, s).start()

            @pl.when(t == steps - 5)
            def _():
                other(chunks)

        spread_out(steps - 2, steps % 2).wait()
        spread_out(steps - 1, (steps - 1) % 2).wait()

        def block_at(b):
            if not relayed:
                return lax.div(b, 2), lax.rem(b, 2)
            d = lax.div(b, 4)
            across = (2 - 4 * lax.rem(lax.div(group, 2), 2)) * lax.rem(d, 2)
            along = (4 - 8 * lax.div(group, 4)) * lax.div(d, 2)
            near_by = (1 - 2 * lax.rem(group, 2)) * lax.rem(lax.div(b, 2), 2)
            return group + across + along + near_by, lax.rem(b, 2)

        def fetch(b, s):
            p, h = block_at(b)
            return (
                pltpu.make_async_copy(
                    dense_out.at[:, pl.ds(pl.multiple_of((p * 2 + h) * piece, piece), piece)],
                    v.dense_in.at[s],
                    moved.at[6 + s],
                ),
                pltpu.make_async_copy(
                    table_out.at[p, pl.ds(pl.multiple_of(h * piece, piece), piece)],
                    v.table_in.at[s],
                    moved.at[8 + s],
                ),
            )

        def arrived(d):
            for a in chunks:
                if isinstance(d, int) and d == 0:
                    own_copy(a).wait()
                to_sibling(a, d).wait_recv()

        arrived(0)
        if relayed:
            arrived(1)
            arrived(2)
        else:
            last(chunks)

            @pl.loop(1, chips)
            def _(d):
                arrived(d)

        v.total[...] = jnp.zeros_like(v.total)
        v.largest[...] = jnp.zeros_like(v.largest)
        for c in fetch(0, 0):
            c.start()

        @pl.loop(0, blocks)
        def _(b):
            s = lax.rem(b, 2)
            if relayed:

                @pl.when(b == 11)
                def _():
                    last(chunks)

                @pl.when(b == 13)
                def _():
                    arrived(3)

            @pl.when(b + 1 < blocks)
            def _():
                for c in fetch(b + 1, 1 - s):
                    c.start()

            for c in fetch(b, s):
                c.wait()
            v.total[...] += mm(v.dense_in[s], v.table_in[s])
            peak = v.largest[...]
            for c in range(piece // 512):
                values = v.table_in[s, c * 512 : (c + 1) * 512, :].astype(F32)
                squares = values * values
                norms = jnp.sum(squares[:, :128] + squares[:, 128:], axis=1, keepdims=True)
                peak = jnp.maximum(peak, jnp.max(norms.reshape(-1, 8, 1), axis=0))
            v.largest[...] = peak

        gate, recalled, upstream = v.gate_pre[...], v.total[...], v.grad_mixed[...]
        sigmoid = 1.0 / (1.0 + jnp.exp(-gate))
        act = gate * sigmoid
        r.mixed[...] = (act * recalled).astype(BF16)
        grad = (upstream * act).astype(BF16)
        r.grad_recalled[...] = grad
        r.grad_gate[...] = (
            upstream * recalled * sigmoid * (1.0 + gate * (1.0 - sigmoid))
        ).astype(BF16)
        wide = grad.astype(F32)
        bound = jnp.max(v.largest[...]) * jnp.sum(wide * wide, axis=1, keepdims=True)
        r.scale[...] = 32000.0 * lax.rsqrt(jnp.maximum(bound, 1e-30))
        for ref in (r.mixed, r.grad_recalled, r.grad_gate, r.scale):
            done(ref)
        for d, ref in enumerate((r.block_0, r.block_1, r.block_2, r.block_3)):
            at = pl.ds(pl.multiple_of(lax.rem(rank + d, ranks) * local, local), local)
            ref[...] = mt(r.mixed[at, :], flat(mixed_ref)).astype(BF16)
            done(ref)
        for a in chunks:
            for d in range(4 if relayed else 1):
                to_sibling(a, d).wait_send()
            if relayed:
                for d in range(1, 4):
                    to_chip(a, d).wait_send()
            else:

                @pl.loop(1, chips)
                def _(d):
                    to_sibling(a, d).wait_send()
                    to_chip(a, d).wait_send()

        for name in names:
            getattr(need, name)
        for c in stores:
            c.wait()

    tree_names = [
        next(i for i, y in enumerate(local_arrays) if y is x) for x in tree
    ]
    arrays = [*local_arrays, table, key_picks]
    near_sems = pltpu.SemaphoreType.DMA((8, ranks))
    tree_sems = pltpu.SemaphoreType.DMA((len(tree) + cuts, hops))
    got = pl.pallas_call(
        body,
        out_shape=[jax.ShapeDtypeStruct(shape, dtype) for shape, dtype in outs],
        in_specs=[ANY] * len(arrays),
        out_specs=[ANY] * len(outs),
        scratch_shapes=[pltpu.VMEM(x.shape, x.dtype) for x in local_arrays]
        + [pltpu.VMEM(shape, dtype) for shape, dtype in full]
        + [pltpu.VMEM(shape, dtype) for shape, dtype in results.values()]
        + [pltpu.VMEM(shape, dtype) for shape, dtype in vmem.values()]
        + [
            pltpu.SemaphoreType.DMA((len(names) + 1,)),
            pltpu.SemaphoreType.DMA((len(tree) + cuts,)),
            pltpu.SemaphoreType.DMA((len(outs),)),
            near_sems,
            near_sems,
            tree_sems,
            tree_sems,
            tree_sems,
            tree_sems,
            pltpu.SemaphoreType.DMA((10,)),
        ],
        compiler_params=pltpu.CompilerParams(
            collective_id=cid, has_side_effects=True, vmem_limit_bytes=61 << 20
        ),
    )(*arrays)
    whole_arrays = [x.reshape(-1, x.shape[2]) for x in got[: len(tree)]]
    return whole_arrays, types.SimpleNamespace(**dict(zip(results, got[len(tree) :]))), got[-2]


def pick_grads(first, second, grads, scale, table):
    tokens, picks = first.shape
    width = grads.shape[1]
    per_block = 16
    rows = per_block * NKEYS
    blocks = table.shape[0] // rows

    def body(first_ref, second_ref, grads_ref, scale_ref, table_ref, out_ref, kept):
        step = pl.program_id(0)

        @pl.when(step == 0)
        def _():
            kept[...] = jnp.zeros_like(kept)

        own = first_ref[...]
        low = second_ref[...] & 127
        factor = jnp.broadcast_to(scale_ref[...], (tokens, 128))
        total = kept[...]
        for b in range(per_block):
            every = mt(grads_ref[...], table_ref[b * NKEYS : (b + 1) * NKEYS, :])
            packed = (every[:, 128:] * factor).astype(I32) * 65536 + (
                every[:, :128] * factor
            ).astype(I32)
            found = jnp.take_along_axis(packed, low, axis=1, mode="promise_in_bounds")
            total = jnp.where(own == step * per_block + b, found, total)
        kept[...] = total

        @pl.when(step == blocks - 1)
        def _():
            p = kept[...]
            right = lax.shift_right_arithmetic(lax.shift_left(p, 16), 16)
            left = lax.shift_right_arithmetic(p - right, 16)
            both = jnp.where(second_ref[...] >= 128, left, right).astype(F32) / factor
            out_ref[...] = both.T.astype(BF16)

    return pl.pallas_call(
        body,
        grid=(blocks,),
        out_shape=jax.ShapeDtypeStruct((picks, tokens), BF16),
        in_specs=[whole(x.shape) for x in (first, second, grads, scale)]
        + [pl.BlockSpec((rows, width), lambda s: (s, 0))],
        out_specs=whole((picks, tokens)),
        scratch_shapes=[pltpu.VMEM((tokens, picks), I32)],
        compiler_params=pltpu.CompilerParams(vmem_limit_bytes=61 << 20),
    )(first, second, grads, scale, table)


def by_part(down, parts):
    shaped = down.reshape(down.shape[0], NAD, parts, RANK).transpose(0, 2, 1, 3)
    return shaped.reshape(down.shape)


def add_up(inputs, plans, through):
    shapes = []
    for x, (axis, sizes) in zip(inputs, plans):
        for size in sizes:
            if isinstance(size, tuple):
                shapes.append((size[0], x.shape[1], size[1]))
            else:
                shapes.append((x.shape[1], size) if axis else (size, x.shape[2]))

    def body(*refs):
        outs = iter(refs[len(inputs) + len(through) :])
        for ref in refs[len(inputs) : len(inputs) + len(through)]:
            next(outs)[...] = ref[...]
        for ref, (axis, sizes) in zip(refs, plans):

            def total(start, size):
                cut = slice(start, start + size)
                return sum(
                    (ref[p, :, cut] if axis else ref[p, cut, :]).astype(F32)
                    for p in range(ref.shape[0])
                )

            at = 0
            for size in sizes:
                out = next(outs)
                if isinstance(size, tuple):
                    for q in range(size[0]):
                        out[q] = total(at, size[1])
                        at += size[1]
                else:
                    out[...] = total(at, size)
                    at += size

    kept = [(x.shape, x.dtype) for x in through]
    return stage(body, kept + [(shape, F32) for shape in shapes], (*inputs, *through))


def make_ready(segments, adapters, project_in, down_input, down_memory, turned, joined, local):
    count = segments.shape[1]
    parts, lines, width = project_in.shape

    def body(segments_ref, adapters_ref, project_ref, input_ref, memory_ref, *refs):
        ins, outs = refs[: len(turned) + len(joined)], refs[len(turned) + len(joined) :]

        def ordered(ref, parts):
            size = NAD * parts * RANK
            row = lax.broadcasted_iota(I32, (size, size), 0)
            column = lax.broadcasted_iota(I32, (size, size), 1)
            part, rest = lax.div(column, NAD * RANK), lax.rem(column, NAD * RANK)
            adapter, rank = lax.div(rest, RANK), lax.rem(rest, RANK)
            came = adapter * (parts * RANK) + part * RANK + rank
            return mm(ref[...], jnp.where(row == came, 1.0, 0.0).astype(BF16)).astype(BF16)

        for p in range(parts):
            outs[0][:, p * width : (p + 1) * width] = project_ref[p]
        outs[1][...] = ordered(input_ref, 3)
        outs[2][...] = ordered(memory_ref, 2)
        for p in range(parts):
            outs[3][:, p * width : (p + 1) * width] = ins[len(turned)][p]
        at = parts * width
        for ref in ins[len(turned) + 1 :]:
            outs[3][:, at : at + ref.shape[1]] = ref[...]
            at += ref.shape[1]
        for ref, out in zip(ins[: len(turned)], outs[4:]):
            out[...] = ref[...].astype(F32).T.astype(BF16)
        owner_ref, below_ref, owner_own_ref = outs[-3:]
        across = jnp.broadcast_to(segments_ref[...], (8, count))
        owner = jnp.zeros_like(across)
        for s in range(adapters.shape[1]):
            owner = jnp.where(across == s, adapters_ref[0:1, s : s + 1], owner)
        owner_ref[...] = owner.T[:, 0:1]
        below_ref[...] = across.T[:, 0:1]
        own = pl.ds(pl.multiple_of(lax.axis_index(TP) * local, local), local)
        owner_own_ref[...] = owner_ref[own, :]

    small = parts * width + sum(x.shape[1] for x in joined[1:])
    return stage(
        body,
        [
            ((lines, parts * width), BF16),
            (down_input.shape, BF16),
            (down_memory.shape, BF16),
            ((joined[1].shape[0], small), BF16),
        ]
        + [(x.shape[::-1], BF16) for x in turned]
        + [((count, 1), I32), ((count, 1), I32), ((local, 1), I32)],
        (segments, adapters, project_in, down_input, down_memory, *turned, *joined),
    )


def on_device(
    inputs,
    cotangent,
    norm_attend,
    norm_memory,
    project_in,
    project_out,
    query_weight,
    gate_weight,
    memory_out,
    half_keys,
    value_table,
    key_picks,
    segment_ids,
    adapter_ids,
    down_input,
    up_input,
    down_attend,
    up_attend,
    down_memory,
    up_query,
    up_gate,
    down_mixed,
    up_mixed,
):
    groups = lax.axis_size(DP)
    ranks = lax.axis_size(TP)
    rank = lax.axis_index(TP)
    local = inputs.shape[0]
    count = segment_ids.shape[0]
    width = project_in.shape[2]
    model = inputs.shape[1]

    across = segment_ids[None, :]
    attend_turned = down_attend.T
    joined = (up_input.transpose(1, 0, 2), up_query, up_gate, up_attend, up_mixed, down_mixed.T)
    turned = (project_out, memory_out)
    if project_out.shape[1] % 128 == 0:
        ready = make_ready(
            across,
            adapter_ids,
            project_in.transpose(1, 0, 2),
            down_input,
            down_memory,
            turned,
            joined,
            local,
        )
        flat_in, parted_input, parted_memory, small, out_turned, mixed_turned = ready[:6]
        owner, below, owner_own = ready[6:]
    else:
        flat_in = project_in.reshape(project_in.shape[0], 3 * width)
        parted_input, parted_memory = by_part(down_input, 3), by_part(down_memory, 2)
        out_turned, mixed_turned = [x.T for x in turned]
        small = jnp.concatenate((up_input.reshape(-1, 3 * width),) + joined[1:], axis=1)
        below = segment_ids[:, None]
        owner = jnp.zeros_like(below)
        for s in range(adapter_ids.shape[1]):
            owner = jnp.where(below == s, adapter_ids[0, s], owner)
        owner_own = lax.dynamic_slice_in_dim(owner, rank * local, local, 0)
    spots, at = [], 0
    for size in (3 * width, up_query.shape[1], width, model, model, width):
        spots.append(slice(at, at + size))
        at += size
    gain_one, gain_two, keys = norm_attend, norm_memory, half_keys[0]
    (
        (
            full_in,
            full_down_input,
            ups,
            out_t,
            attend_t,
            full_query,
            full_gate,
            full_down_memory,
            _,
        ),
        kept,
        table,
    ) = forward(
        dict(
            flat_in=flat_in,
            down_input=parted_input,
            ups=small,
            out_t=out_turned,
            attend_t=attend_turned,
            query=query_weight,
            gate=gate_weight,
            down_memory=parted_memory,
            mixed_t=mixed_turned,
            inputs=inputs,
            cotangent=cotangent,
            gain_one=gain_one,
            gain_two=gain_two,
            owner=owner,
            owner_own=owner_own,
            across=across,
            below=below,
            keys=keys,
        ),
        value_table,
        key_picks,
        spots,
        1,
    )

    def turn(d):
        return [(p, (p + d) % ranks) for p in range(ranks)]

    mixed_parts = [kept.block_0] + [
        lax.ppermute(block, TP, turn(d))
        for d, block in ((1, kept.block_1), (2, kept.block_2), (3, kept.block_3))
    ]
    picked = pick_grads(
        kept.first, kept.second, kept.grad_recalled, kept.scale, table.reshape(-1, width)
    )
    picked, mixed_parts = lax.optimization_barrier((picked, mixed_parts))
    given = dict(
        picked=picked.reshape(ranks, -1, count),
        weights=kept.weights,
        keys=keys,
        picks=key_picks,
        query=full_query,
        gate=full_gate,
        ups=ups,
        grad_gate=kept.grad_gate,
        mixed=kept.mixed,
        owner=owner,
        owner_own=owner_own,
        middle=kept.middle,
        cotangent=cotangent,
        gain_two=gain_two,
        down_memory=full_down_memory,
        out_t=out_t,
        attend_t=attend_t,
        low_three=kept.low_three,
        own_cotangent=kept.own_cotangent,
        low_four_back=kept.low_four_back,
        normed_rows=kept.normed_rows,
        projected=kept.projected,
        across=across,
        below=below,
        full_in=full_in,
        low_one=kept.low_one,
        attended=kept.attended,
        two_short=kept.two_short,
        down_input=full_down_input,
        inputs=inputs,
        gain_one=gain_one,
        normed_one=kept.normed_one,
    )
    wides, (outputs, input_grad, up_parts, memory_parts, down_parts) = backward(
        given, mixed_parts, spots, 5
    )
    (
        outputs,
        input_grad,
        grad_up_input,
        grad_up_query,
        grad_up_gate,
        grad_up_mixed,
        grad_down_attend,
        grad_down_mixed,
        grad_up_attend,
        grad_down_memory,
        grad_down_input,
    ) = add_up(
        (up_parts, memory_parts, down_parts),
        (
            (1, ((3, width), *wides[3:])),
            (0, (memory_parts.shape[1],)),
            (0, (down_parts.shape[1],)),
        ),
        (outputs, input_grad),
    )
    return (
        outputs,
        input_grad,
        grad_down_input.T,
        grad_up_input.transpose(1, 0, 2),
        grad_down_attend.T,
        grad_up_attend,
        grad_down_memory.T,
        grad_up_query,
        grad_up_gate,
        grad_down_mixed.T,
        grad_up_mixed,
    )


def solution(mesh):
    rows = P((DP, TP), None)
    both = P(DP, TP)
    wide = P(DP, None)
    turned = P(TP, DP)
    split = P(DP, None, TP)
    return jax.shard_map(
        on_device,
        mesh=mesh,
        in_specs=(
            rows,
            rows,
            P(),
            P(),
            split,
            turned,
            both,
            both,
            turned,
            P(TP, None, None, None),
            both,
            P(None, None, None, DP),
            P(DP),
            wide,
            wide,
            split,
            turned,
            wide,
            wide,
            both,
            both,
            turned,
            wide,
        ),
        out_specs=(rows, rows, both, split, turned, both, both, both, both, turned, both),
        check_vma=False,
    )
```
